128 devices in a mesh: gx: 8 (over y, core), gy: 8 (over x, z_hi), ga: 2 (over z_lo).
Axes of the slice: x: 4, y: 4, z: 4 (z_hi: 2, z_lo: 2; z = z_hi * 2 + z_lo), core: 2. Of those that a mesh axis runs over, the one named last changes fastest.
Arguments:
- offsets: float32 [3, 16, 16, 32, 128], P(None, 'gx', 'gy', 'ga'), may hold values from 0 to 1
- charge: float32 [16, 16, 32, 128], P('gx', 'gy', 'ga'), may hold values from -3 to 3
- counts: int32 [16, 16, 32], P('gx', 'gy', 'ga'), may hold values from 8 to 128, as said below
- partners: int32 [16, 16, 32, 128], P('gx', 'gy', 'ga'), may hold values from 0 to 127
Outputs:
- short_force: float32 [3, 16, 16, 32, 128], P(None, 'gx', 'gy', 'ga')
- long_force: float32 [3, 16, 16, 32, 128], P(None, 'gx', 'gy', 'ga')
The draws below stay inside these ranges and needn't reach their ends.
Inputs may be any that keep to these rules, and one draw needn't show every extreme that they name: `counts`: each cell holds at least 8 beads and at most 128; some cell holds exactly 128.
All inputs are finite; a program needn't handle non-finite values.
Results may differ from the reference program's by a relative error of at most 0.0003.
Values sent between devices are 32-bit elements; how exact they have to be, the bound alone decides.
No kernel may reach another device: no remote copies, remote signals or barrier semaphores. Data moves between devices by JAX's collectives and lax.ppermute only.
A program may use at most 192 MiB of HBM per device.

```python
import jax
import jax.numpy as jnp
from jax import lax

TILE = 128
CELLS_X = 16
CELLS_Y = 16
CELLS_Z = 32


def draw_counts(key, part):
    drawn = jax.random.randint(key, (CELLS_X, CELLS_Y, CELLS_Z), 8, TILE + 1)
    return drawn.at[0, 0, 0].set(TILE).astype(jnp.int32)


def set_ends(result, rng, least, top_value):
    longest = result.shape.index(max(result.shape))
    spots = []
    for shift in (0, 1):
        where = [jax.random.randint(jax.random.fold_in(rng, axis), (), 0, length) for axis, length in enumerate(result.shape)]
        where[longest] = (where[longest] + shift) % result.shape[longest]
        spots.append(tuple(where))
    return result.at[spots[0]].set(least).at[spots[1]].set(top_value)


def block_scale(rng, shape, split, least, top_value):
    factor_of, own = 1.0, jax.random.fold_in(rng, 6)
    for axis_at, blocks in split:
        heights = jnp.exp(jax.random.uniform(jax.random.fold_in(own, axis_at), (blocks,), jnp.float32, least / len(split), top_value / len(split)))
        factor_of = factor_of * jnp.repeat(heights, shape[axis_at] // blocks).reshape([-1 if axis == axis_at else 1 for axis in range(len(shape))])
    return factor_of


def bell_draw(key, shape, scale, reach, pieces=(), held_as=jnp.bfloat16):
    factor_of = block_scale(key, shape, pieces, -0.22, 0.18) if pieces else 1.0
    values = jax.random.normal(key, shape, jnp.float32) * scale * factor_of
    return jnp.minimum(jnp.maximum(values, -reach), reach).astype(held_as)


def setup_inputs(seed: int = 0) -> dict:
    keys = jax.random.split(jax.random.key(seed), 5)
    return {
        "offsets": jnp.clip(1.0 * jax.random.uniform(keys[0], (3, CELLS_X, CELLS_Y, CELLS_Z, TILE), jnp.float32) ** block_scale(keys[0], (3, CELLS_X, CELLS_Y, CELLS_Z, TILE), ((1, 8), (2, 8), (3, 2)), -0.2, 0.2), 0.0, 1.0),
        "charge": bell_draw(keys[1], (CELLS_X, CELLS_Y, CELLS_Z, TILE), 0.5, 3.0, ((0, 8), (1, 8), (2, 2)), jnp.float32),
        "counts": draw_counts(jax.random.fold_in(keys[4], 71), 0),
        "partners": set_ends(jax.random.randint(keys[3], (CELLS_X, CELLS_Y, CELLS_Z, TILE), 0, TILE), jax.random.fold_in(keys[3], 1), 0, TILE - 1).astype(jnp.int32),
    }


highest = lax.Precision.HIGHEST
cutoff_sq = 64.0
soften_sq = 1.0
bond_spring = 0.1
fine_scale = 4.0
coarse_scale = 2.0
fine_spread = 2.5
coarse_spread = 6.0


def spline(shifted):
    magnitude = jnp.abs(shifted)
    margin = jnp.maximum(1.5 - magnitude, 0.0)
    return jnp.where(magnitude < 0.5, 0.75 - shifted * shifted, 0.5 * margin * margin)


def spline_slope(shifted):
    magnitude = jnp.abs(shifted)
    margin = jnp.maximum(1.5 - magnitude, 0.0)
    return jnp.where(magnitude < 0.5, -2.0 * shifted, jnp.where(shifted > 0.0, -margin, margin))


def patch_weights(offset):
    points = jnp.arange(11).astype(jnp.float32)
    shifted = 8.0 * offset[..., None] + 1.0 - points
    return spline(shifted), spline_slope(shifted)


def charge_patches(weighted, offsets):
    weight_x, _ = patch_weights(offsets[0])
    weight_y, _ = patch_weights(offsets[1])
    weight_z, _ = patch_weights(offsets[2])
    plane_part = weighted[..., None, None] * weight_x[..., :, None] * weight_y[..., None, :]
    flattened = plane_part.reshape(plane_part.shape[:-2] + (121,))
    joined = jnp.einsum("...sp,...sc->...pc", flattened, weight_z, precision=highest)
    return joined.reshape(joined.shape[:-2] + (11, 11, 11))


def assemble(values, where_axis):
    cell_count = values.shape[where_axis]
    inner_part = lax.slice_in_dim(values, 0, 8, axis=where_axis + 1)
    overflow = lax.slice_in_dim(values, 8, 11, axis=where_axis + 1)
    inner_pad = [(0, 0)] * values.ndim
    inner_pad[where_axis] = (0, 1)
    over_pad = [(0, 0)] * values.ndim
    over_pad[where_axis] = (1, 0)
    over_pad[where_axis + 1] = (0, 5)
    merged = jnp.pad(inner_part, inner_pad) + jnp.pad(overflow, over_pad)
    new_shape = values.shape[:where_axis] + (8 * (cell_count + 1),) + values.shape[where_axis + 2:]
    return merged.reshape(new_shape)


def cut_patches(values, where_axis):
    cell_count = (values.shape[where_axis] - 4) // 8
    split_shape = values.shape[:where_axis] + (cell_count, 8) + values.shape[where_axis + 1:]
    head_part = lax.slice_in_dim(values, 1, 8 * cell_count + 1, axis=where_axis).reshape(split_shape)
    widths = [(0, 0)] * values.ndim
    widths[where_axis] = (0, 5)
    padded = jnp.pad(values, widths)
    tail_part = lax.slice_in_dim(padded, 9, 8 * cell_count + 9, axis=where_axis).reshape(split_shape)
    tail_part = lax.slice_in_dim(tail_part, 0, 3, axis=where_axis + 1)
    return jnp.concatenate([head_part, tail_part], axis=where_axis + 1)


def kernel_band(in_length, spread):
    row_index = jnp.arange(in_length)[:, None]
    column_index = jnp.arange(in_length - 16)[None, :]
    distance = row_index - column_index - 8
    gap = distance.astype(jnp.float32)
    return jnp.where(jnp.abs(distance) <= 8, jnp.exp(-gap * gap / (2.0 * spread * spread)), 0.0).astype(jnp.float32)


def along_axis(values, matrix, where_axis):
    contracted = jnp.tensordot(values, matrix, axes=([where_axis], [0]), precision=highest)
    return jnp.moveaxis(contracted, -1, where_axis)


def convolve(values, spread, strength):
    for where_axis in range(3):
        values = along_axis(values, kernel_band(values.shape[where_axis], spread), where_axis)
    return strength * values


def grid_map(fine_length, coarse_length, fine_start, coarse_start):
    fine_index = jnp.arange(fine_length)[:, None] + fine_start
    coarse_index = jnp.arange(coarse_length)[None, :] + coarse_start
    gap = fine_index - 2 * coarse_index
    return jnp.where(gap == 0, 1.0, jnp.where(jnp.abs(gap) == 1, 0.5, 0.0)).astype(jnp.float32)


def cell_positions(offsets, first_cell):
    coordinates = []
    for dimension in range(3):
        cell_count = offsets.shape[dimension + 1]
        cell_index = jnp.arange(cell_count).astype(jnp.float32) + first_cell
        broadcast_shape = [1, 1, 1, 1]
        broadcast_shape[dimension] = cell_count
        coordinates.append((cell_index.reshape(broadcast_shape) + offsets[dimension]) * 8.0)
    return jnp.stack(coordinates)


def pair_sum(own_pos, own_charge, near_pos, near_charge):
    separation = own_pos[..., :, None] - near_pos[..., None, :]
    distance_sq = jnp.sum(separation * separation, axis=0)
    reach_left = jnp.maximum(1.0 - distance_sq / cutoff_sq, 0.0)
    strength = reach_left * reach_left * reach_left / (distance_sq + soften_sq) * near_charge[..., None, :]
    return own_charge * jnp.sum(separation * strength, axis=-1)


def bond_force(positions, in_use, partners):
    slot_ids = jnp.arange(positions.shape[-1]).astype(jnp.int32)
    picker = (partners[..., :, None] == slot_ids).astype(jnp.float32)
    partner_pos = jnp.einsum("...sp,d...p->d...s", picker, positions, precision=highest)
    partner_use = jnp.einsum("...sp,...p->...s", picker, in_use, precision=highest)
    return -bond_spring * (positions - partner_pos) * (in_use * partner_use)


def grid_force(patches, weighted, offsets):
    weight_x, slope_x = patch_weights(offsets[0])
    weight_y, slope_y = patch_weights(offsets[1])
    weight_z, slope_z = patch_weights(offsets[2])
    flattened = patches.reshape(patches.shape[:-3] + (121, 11))
    level_part = jnp.einsum("...pc,...sc->...sp", flattened, weight_z, precision=highest)
    rising = jnp.einsum("...pc,...sc->...sp", flattened, slope_z, precision=highest)
    level_part = level_part.reshape(level_part.shape[:-1] + (11, 11))
    rising = rising.reshape(rising.shape[:-1] + (11, 11))
    force_x = jnp.sum(slope_x[..., :, None] * weight_y[..., None, :] * level_part, axis=(-2, -1))
    force_y = jnp.sum(weight_x[..., :, None] * slope_y[..., None, :] * level_part, axis=(-2, -1))
    force_z = jnp.sum(weight_x[..., :, None] * weight_y[..., None, :] * rising, axis=(-2, -1))
    return -weighted * jnp.stack([force_x, force_y, force_z])


def reference(offsets, charge, counts, partners):
    slot_count = charge.shape[-1]
    cells_x, cells_y, cells_z = charge.shape[:3]
    in_use = (jnp.arange(slot_count).astype(jnp.int32) < counts[..., None]).astype(jnp.float32)
    weighted = charge * in_use
    positions = cell_positions(offsets, 0.0)
    padded_pos = cell_positions(jnp.pad(offsets, ((0, 0), (1, 1), (1, 1), (1, 1), (0, 0))), -1.0)
    padded_charge = jnp.pad(weighted, ((1, 1), (1, 1), (1, 1), (0, 0)))

    def pair_slab(slab_index):
        own_pos = lax.dynamic_index_in_dim(positions, slab_index, axis=1, keepdims=False)
        own_charge = lax.dynamic_index_in_dim(weighted, slab_index, axis=0, keepdims=False)
        own_use = lax.dynamic_index_in_dim(in_use, slab_index, axis=0, keepdims=False)
        own_partners = lax.dynamic_index_in_dim(partners, slab_index, axis=0, keepdims=False)
        running = bond_force(own_pos, own_use, own_partners)
        for step_x in range(3):
            slab_pos = lax.dynamic_index_in_dim(padded_pos, slab_index + step_x, axis=1, keepdims=False)
            slab_charge = lax.dynamic_index_in_dim(padded_charge, slab_index + step_x, axis=0, keepdims=False)
            for step_y in range(3):
                for step_z in range(3):
                    near_pos = slab_pos[:, step_y:step_y + cells_y, step_z:step_z + cells_z]
                    near_charge = slab_charge[step_y:step_y + cells_y, step_z:step_z + cells_z]
                    running = running + pair_sum(own_pos, own_charge, near_pos, near_charge)
        return running

    slab_ids = jnp.arange(cells_x).astype(jnp.int32)
    short_force = jnp.moveaxis(lax.map(pair_slab, slab_ids), 0, 1)

    offsets_slabs = jnp.moveaxis(offsets, 1, 0)

    def patch_slab(pieces_in):
        return charge_patches(pieces_in[0], pieces_in[1])

    patches = lax.map(patch_slab, (weighted, offsets_slabs))
    spread_grid = jnp.transpose(patches, (0, 3, 1, 4, 2, 5))
    for where_axis in range(3):
        spread_grid = assemble(spread_grid, where_axis)
    grid_x, grid_y, grid_z = 8 * cells_x, 8 * cells_y, 8 * cells_z
    fine_charge = spread_grid[1:grid_x + 1, 1:grid_y + 1, 1:grid_z + 1]
    fine_potential = convolve(jnp.pad(fine_charge, 8), fine_spread, fine_scale)
    coarse_maps = [grid_map(length, length // 2, 0, 0) for length in (grid_x, grid_y, grid_z)]
    coarse_charge = fine_charge
    for where_axis in range(3):
        coarse_charge = along_axis(coarse_charge, coarse_maps[where_axis], where_axis)
    coarse_potential = convolve(jnp.pad(coarse_charge, 8), coarse_spread, coarse_scale)
    potential = coarse_potential
    for where_axis in range(3):
        potential = along_axis(potential, jnp.transpose(coarse_maps[where_axis]), where_axis)
    potential = jnp.pad(fine_potential + potential, 2)
    for where_axis in range(3):
        potential = cut_patches(potential, 2 * where_axis)
    near_grid = jnp.transpose(potential, (0, 2, 4, 1, 3, 5))

    def force_slab(pieces_in):
        return grid_force(pieces_in[0], pieces_in[1], pieces_in[2])

    long_force = jnp.moveaxis(lax.map(force_slab, (near_grid, weighted, offsets_slabs)), 0, 1)
    return short_force, long_force
```

```python
import jax
import jax.numpy as jnp
import numpy as np
from jax import lax
from jax.experimental import pallas as pl
from jax.experimental.pallas import tpu as pltpu
from jax.sharding import PartitionSpec as P

f32, bf16, i32 = jnp.float32, jnp.bfloat16, jnp.int32
LAST = (((1,), (1,)), ((), ()))
CAP = 65.0 / 64.0
ROWS, TILES, SLOTS = 64, 4, 4
VMEM = pl.BlockSpec(memory_space=pltpu.VMEM)
SMEM = pl.BlockSpec(memory_space=pltpu.SMEM)
ANY = pl.BlockSpec(memory_space=pl.ANY)


def fine_kernel(gap):
    return np.where(np.abs(gap) <= 8, np.exp(-gap * gap / 12.5), 0.0)


def coarse_kernel(gap):
    return np.where(np.abs(gap) <= 8, np.exp(-gap * gap / 72.0), 0.0)


def hat(gap):
    return np.where(gap == 0, 1.0, np.where(np.abs(gap) == 1, 0.5, 0.0))


def halves(matrix):
    high = matrix.astype(np.float32).astype(jnp.bfloat16)
    low = (matrix - high.astype(np.float64)).astype(np.float32).astype(jnp.bfloat16)
    return high, low


def z_operator(part):
    source = np.full(256, 10**6, np.int64)
    source[:131] = 128 * part - 1 + np.arange(131)
    source[160:181] = np.arange(21) + (127 if part == 0 else 109)
    inside = (source >= 0) & (source < 256)
    result = np.zeros((256, 256))
    target = 128 * part - 1 + np.arange(131)
    fine = fine_kernel((target[None, :] - source[:, None]).astype(np.float64))
    result[:, :131] = fine * ((target >= 0) & (target < 256))[None, :]
    middle = np.arange(128)
    down = hat((source[:, None] - 2 * middle[None, :]).astype(np.float64))
    point = 64 * part - 1 + np.arange(67)
    spread = coarse_kernel((middle[:, None] - point[None, :]).astype(np.float64))
    spread = spread * ((point >= 0) & (point < 128))[None, :]
    result[:, 136:203] = down @ spread
    return result * inside[:, None]


def y_operators():
    own = np.where(np.arange(24) < 19, np.arange(24), 10**6)
    below = np.where(np.arange(16) < 11, np.arange(16) - 8, 10**6)
    above = np.where(np.arange(16) < 11, np.arange(16) + 16, 10**6)
    source = np.concatenate([own, below, above]).astype(np.float64)
    fine = fine_kernel(np.arange(24)[:, None] - source[None, :])
    fine[19:] = 0
    own = np.where(np.arange(16) < 11, np.arange(16), 10**6)
    below = np.where(np.arange(16) < 11, np.arange(16) - 8, 10**6)
    above = np.where(np.arange(16) < 11, np.arange(16) + 8, 10**6)
    far_below = np.where(np.arange(8) < 3, np.arange(8) - 8, 10**6)
    far_above = np.where(np.arange(8) < 3, np.arange(8) + 16, 10**6)
    source = np.concatenate([own, below, above, far_below, far_above]).astype(np.float64)
    coarse = coarse_kernel(np.arange(16)[:, None] - source[None, :])
    coarse[11:] = 0
    down = hat(np.arange(24)[None, :] - (2.0 * np.arange(16)[:, None] - 1))
    down[11:] = 0
    up = hat(np.arange(24)[:, None] - (2.0 * np.arange(16)[None, :] - 1))
    up[19:] = 0
    up[:, 11:] = 0
    stack = lambda m: np.concatenate([halves(m)[0], halves(m)[1], halves(m)[0]], 1)
    thrice = lambda m: np.concatenate([halves(m)[0]] * 3, 1)
    return stack(fine), stack(coarse), thrice(down), thrice(up)


def z_prolong():
    result = np.zeros((128, 256))
    point = 2.0 * np.arange(67) - 1
    result[8:75, :131] = hat(np.arange(131)[None, :] - point[:, None])
    return halves(result)[0]


def split2(value):
    high = value.astype(bf16)
    return high, (value - high.astype(f32)).astype(bf16)


def split3(value):
    high = value.astype(bf16).astype(f32)
    rest = value - high
    middle = rest.astype(bf16).astype(f32)
    return high, middle, rest - middle


def dot(left, right):
    return jnp.dot(left, right, preferred_element_type=f32)


def spline(shifted):
    magnitude = jnp.abs(shifted)
    margin = jnp.maximum(1.5 - magnitude, 0.0)
    return jnp.where(magnitude < 0.5, 0.75 - shifted * shifted, 0.5 * margin * margin)


def spline_slope(shifted):
    magnitude = jnp.abs(shifted)
    margin = jnp.maximum(1.5 - magnitude, 0.0)
    return jnp.where(magnitude < 0.5, -2.0 * shifted, jnp.where(shifted > 0.0, -margin, margin))


def weights_at(offset, rows, first):
    points = lax.broadcasted_iota(i32, (rows, 128), 0).astype(f32)
    return 8.0 * offset + (1.0 + first) - points


def inside_mask(shape, dim, start, count):
    point = lax.broadcasted_iota(i32, shape, dim) + start
    return ((point >= 0) & (point < count)).astype(f32)


def spread_kernel(off_ref, charge_ref, counts_ref, block_ref, near_ref, rho_ref, msg_ref):
    dx, dy, dz = lax.axis_index("gx"), lax.axis_index("gy"), lax.axis_index("ga")
    lane = lax.broadcasted_iota(i32, (1, 128), 1)
    row8 = lax.broadcasted_iota(i32, (8, 128), 0)
    rho_ref[...] = jnp.zeros((19, 24, 256), f32)
    zero8 = jnp.zeros((8, 128), f32)
    for i in range(2):
        for j in range(2):
            near_ref[i, j, 0] = zero8
            near_ref[i, j, 17] = zero8

    def column(ij, _):
        i, j = ij >> 1, ij & 1
        shift_x = 8.0 * (i + 1).astype(f32)
        shift_y = 8.0 * (j + 1).astype(f32)
        total = jnp.zeros((176, 128), f32)
        tail = None
        for m in range(8):
            highs, lows, z_highs, z_lows = [], [], [], []
            for half in range(2):
                k = 2 * m + half
                ox = off_ref[0, i, j, k : k + 1]
                oy = off_ref[1, i, j, k : k + 1]
                oz = off_ref[2, i, j, k : k + 1]
                count = counts_ref[ij * 16 + k]
                weighted = jnp.where(lane < count, charge_ref[i, j, k : k + 1], 0.0)
                near_ref[i, j, k + 1] = jnp.concatenate(
                    [8.0 * ox + shift_x, 8.0 * oy + shift_y, 8.0 * oz + 8.0 * (k + 1), weighted, zero8[:4]], 0
                )
                wx = spline(weights_at(ox, 16, 0)) * weighted
                wy = spline(weights_at(oy, 16, 0))
                wz = spline(weights_at(oz, 32, 8 * half))
                plane = jnp.concatenate([wx[a : a + 1] * wy for a in range(11)], 0)
                high, low = split2(plane)
                highs.append(high)
                lows.append(low)
                z_high, z_low = split2(wz)
                z_highs.append(z_high)
                z_lows.append(z_low)
            left = jnp.concatenate(highs + lows + highs, 1)
            right = jnp.concatenate(z_highs + z_highs + z_lows, 1)
            if m < 7:
                pieces = [right]
                if m > 0:
                    pieces = [jnp.zeros((16 * m, 768), bf16)] + pieces
                if m < 6:
                    pieces = pieces + [jnp.zeros((96 - 16 * m, 768), bf16)]
                total = total + lax.dot_general(left, jnp.concatenate(pieces, 0), LAST, preferred_element_type=f32)
            else:
                wide = jnp.concatenate([jnp.zeros((112, 768), bf16), right, jnp.zeros((112, 768), bf16)], 0)
                both = lax.dot_general(left, wide, LAST, preferred_element_type=f32)
                total = total + both[:, :128]
                tail = both[:, 128:]
        first = pl.multiple_of(8 * j, 8)
        for a in range(11):
            rho_ref[8 * i + a, pl.ds(first, 16), 0:128] += total[16 * a : 16 * a + 16]
            rho_ref[8 * i + a, pl.ds(first, 16), 128:256] += tail[16 * a : 16 * a + 16]
        return 0

    lax.fori_loop(0, 4, column, 0)
    mask_y = inside_mask((24, 256), 0, 16 * dy - 1, 128)
    mask_z = inside_mask((24, 256), 1, 128 * dz - 1, 256)
    mask = mask_y * mask_z
    wide_lane = lax.broadcasted_iota(i32, (24, 128), 1)
    msg_ref[0:8] = block_ref[...]
    for i in range(2):
        picked = [jnp.where(dz == 0, near_ref[i, j, 16], near_ref[i, j, 1]) for j in range(2)]
        msg_ref[8 + 8 * i : 16 + 8 * i] = jnp.where(row8 < 4, picked[0], pltpu.roll(picked[1], 4, 0))
    faces = []
    for a in range(19):
        point = 16 * dx - 1 + a
        keep = ((point >= 0) & (point < 128)).astype(f32)
        plane = rho_ref[a] * (mask * keep)
        rho_ref[a] = plane
        low, high = plane[:, :128], plane[:, 128:]
        top = jnp.where(wide_lane < 18, pltpu.roll(low, 18, 1), pltpu.roll(high, 18, 1))
        face = jnp.where(dz == 0, top, low)
        faces.append(jnp.where(wide_lane < 21, face, 0.0))
    faces.append(jnp.zeros((24, 128), f32))
    for p in range(5):
        packed = faces[p]
        for g in range(1, 4):
            packed = packed + pltpu.roll(faces[5 * g + p], 32 * g, 1)
        msg_ref[24 + 24 * p : 48 + 24 * p] = packed


def along_z_kernel(near_ref, rho_ref, own_msg_ref, got_ref, op_ref, down_ref,
                   near1_ref, full_ref, restr_ref, up_ref, dn_ref, up2_ref, dn2_ref):
    dy, dz = lax.axis_index("gy"), lax.axis_index("ga")
    row8 = lax.broadcasted_iota(i32, (8, 128), 0)
    shift = jnp.where(row8 == 2, jnp.where(dz == 0, 128.0, -128.0), 0.0)
    for i in range(2):
        got = got_ref[8 + 8 * i : 16 + 8 * i]
        parts = [jnp.where(row8 < 4, got, 0.0), jnp.where(row8 < 4, pltpu.roll(got, 4, 0), 0.0)]
        for j in range(2):
            near1_ref[i, j, 1:17] = near_ref[i, j, 1:17]
            moved = parts[j] + shift
            near1_ref[i, j, 0] = jnp.where(dz == 1, moved, 0.0)
            near1_ref[i, j, 17] = jnp.where(dz == 0, moved, 0.0)
    lane = lax.broadcasted_iota(i32, (24, 128), 1)
    high_op, low_op = op_ref[dz, 0], op_ref[dz, 1]
    down = down_ref[...]
    lane16 = lax.broadcasted_iota(i32, (16, 128), 1)
    keep = inside_mask((16, 128), 0, 8 * dy - 1, 64)
    for g in range(4):
        planes = range(5 * g, min(5 * g + 5, 19))
        stacked = []
        for p, a in enumerate(planes):
            face = pltpu.roll(got_ref[24 + 24 * p : 48 + 24 * p], (32 - 32 * g) % 128, 1)
            second = jnp.where((lane >= 32) & (lane < 64), face, rho_ref[a, :, 128:256])
            stacked.append(jnp.concatenate([rho_ref[a, :, 0:128], second], 1))
        high, low = split2(jnp.concatenate(stacked, 0))
        result = dot(high, high_op) + dot(low, high_op) + dot(high, low_op)
        for p, a in enumerate(planes):
            plane = result[24 * p : 24 * p + 24]
            full_ref[a] = plane
            h, m, l = split3(plane[:, 128:256])
            restricted = dot(down, jnp.concatenate([h, m, l], 0).astype(bf16)) * keep
            restr_ref[a] = restricted
            for out, first in ((up_ref, 8), (dn_ref, 0)):
                out[152 + 16 * a : 168 + 16 * a] = plane[first : first + 16, 0:128]
                out[456 + 16 * a : 472 + 16 * a] = jnp.where(
                    lane16 < 8, plane[first : first + 16, 128:256], restricted
                )
            up2_ref[8 * a : 8 * a + 8] = restricted[8:16]
            dn2_ref[8 * a : 8 * a + 8] = restricted[0:8]
    counts = jnp.where(row8 == 0, own_msg_ref[0:8], jnp.where(row8 == 1, pltpu.roll(got_ref[0:8], 1, 0), 0.0))
    for out, j in ((up_ref, 1), (dn_ref, 0)):
        out[0:8] = counts
        for level in range(18):
            out[8 + 8 * level : 16 + 8 * level] = jnp.where(
                row8 < 4, near1_ref[0, j, level], pltpu.roll(near1_ref[1, j, level], 4, 0)
            )


def along_y_kernel(near1_ref, full_ref, restr_ref, up_own_ref, below_ref, above_ref, below2_ref, above2_ref,
                   fine_ref, coarse_ref, after_ref, near2_ref, fine2_ref, coarse2_ref,
                   up_ref, dn_ref, up2_ref, dn2_ref):
    dx, dy = lax.axis_index("gx"), lax.axis_index("gy")
    row8 = lax.broadcasted_iota(i32, (8, 128), 0)
    keep = inside_mask((16, 128), 0, 8 * dy - 1, 64)
    lane16 = lax.broadcasted_iota(i32, (16, 128), 1)
    lane24 = lax.broadcasted_iota(i32, (24, 128), 1)
    fine_op, coarse_op = fine_ref[...], coarse_ref[...]

    def plane(a, _):
        at = pl.multiple_of(16 * a, 16)
        at8 = pl.multiple_of(8 * a, 8)
        below_low = below_ref[pl.ds(152 + at, 16)]
        below_high = below_ref[pl.ds(456 + at, 16)]
        above_low = above_ref[pl.ds(152 + at, 16)]
        above_high = above_ref[pl.ds(456 + at, 16)]
        stack = jnp.concatenate(
            [
                full_ref[a],
                jnp.concatenate([below_low, below_high], 1),
                jnp.concatenate([above_low, above_high], 1),
            ],
            0,
        )
        high, low = split3(stack)[:2]
        fine2_ref[a] = dot(fine_op, jnp.concatenate([high, high, low], 0).astype(bf16))
        stack = jnp.concatenate(
            [restr_ref[a], below_high, above_high, below2_ref[pl.ds(at8, 8)], above2_ref[pl.ds(at8, 8)]], 0
        )
        high, low = split3(stack)[:2]
        coarse2_ref[a] = dot(coarse_op, jnp.concatenate([high, high, low], 0).astype(bf16)) * keep
        return 0

    lax.fori_loop(0, 19, plane, 0)
    restricted = []
    for e in range(11):
        value = None
        for a, weight in ((2 * e - 2, 0.5), (2 * e - 1, 1.0), (2 * e, 0.5)):
            if 0 <= a < 19:
                term = coarse2_ref[a] * weight
                value = term if value is None else value + term
        point = 8 * dx - 1 + e
        restricted.append(value * ((point >= 0) & (point < 64)).astype(f32))
    blank = jnp.zeros((8, 128), f32)
    for out, first in ((up_ref, 8), (dn_ref, 0)):
        for n in range(11):
            plane_value = fine2_ref[first + n]
            out[296 + 24 * n : 320 + 24 * n] = plane_value[:, 0:128]
            out[560 + 24 * n : 584 + 24 * n] = jnp.where(
                lane24 < 8, plane_value[:, 128:256], jnp.concatenate([restricted[n], blank], 0)
            )
    for n in range(3):
        up2_ref[16 * n : 16 * n + 16] = restricted[8 + n]
        dn2_ref[16 * n : 16 * n + 16] = restricted[n]
    shift_down = jnp.where(row8 == 1, -16.0, 0.0)
    shift_up = jnp.where(row8 == 1, 16.0, 0.0)
    for level in range(18):
        for y, source, shift in ((0, below_ref, shift_down), (3, above_ref, shift_up)):
            got = source[8 + 8 * level : 16 + 8 * level]
            near2_ref[0, y, level] = jnp.where(row8 < 4, got, 0.0) + shift
            near2_ref[1, y, level] = jnp.where(row8 < 4, pltpu.roll(got, 4, 0), 0.0) + shift
        for x in range(2):
            for y in range(2):
                near2_ref[x, y + 1, level] = near1_ref[x, y, level]
    counts = jnp.where(row8 < 2, up_own_ref[0:8], 0.0)
    counts = jnp.where((row8 >= 2) & (row8 < 4), pltpu.roll(below_ref[0:8], 2, 0), counts)
    counts = jnp.where((row8 >= 4) & (row8 < 6), pltpu.roll(above_ref[0:8], 4, 0), counts)
    for out, x in ((up_ref, 1), (dn_ref, 0)):
        out[0:8] = counts
        for level in range(18):
            for pair in range(2):
                at = 8 + 8 * (2 * level + pair)
                out[at : at + 8] = jnp.where(
                    row8 < 4, near2_ref[x, 2 * pair, level], pltpu.roll(near2_ref[x, 2 * pair + 1, level], 4, 0)
                )


def along_x_kernel(fine2_ref, up_own_ref, dn_own_ref, below_ref, above_ref, below2_ref, above2_ref,
                   up_y_ref, up_z_ref, after_ref, phi_ref, source, third, coarse):
    dx, dy, dz = lax.axis_index("gx"), lax.axis_index("gy"), lax.axis_index("ga")
    for p in range(35):
        rel = p - 8
        low = high = None
        pieces = []
        if 0 <= rel < 19:
            pieces.append((fine2_ref[rel, :, 0:128], fine2_ref[rel, :, 128:256]))
        if rel <= 2:
            n = rel + 8
            pieces.append((below_ref[296 + 24 * n : 320 + 24 * n], below_ref[560 + 24 * n : 584 + 24 * n]))
        if rel >= 16:
            n = rel - 16
            pieces.append((above_ref[296 + 24 * n : 320 + 24 * n], above_ref[560 + 24 * n : 584 + 24 * n]))
        for low_piece, high_piece in pieces:
            low = low_piece if low is None else low + low_piece
            high = high_piece if high is None else high + high_piece
        source[p, :, 0:128] = low
        source[p, :, 128:256] = high
    fine_weights = [float(w) for w in fine_kernel(np.arange(9.0))]
    coarse_weights = [float(w) for w in coarse_kernel(np.arange(9.0))]

    def fine_plane(a, _):
        value = source[a + 8] * (4.0 * fine_weights[0])
        for d in range(1, 9):
            value = value + (source[a + 8 - d] + source[a + 8 + d]) * (4.0 * fine_weights[d])
        third[a] = value
        return 0

    lax.fori_loop(0, 19, fine_plane, 0)

    def own_coarse(e):
        ref, n = (up_own_ref, e)
        return ref[560 + 24 * n : 576 + 24 * n]

    for p in range(27):
        rel = p - 8
        value = None
        pieces = []
        if 0 <= rel < 11:
            pieces.append(own_coarse(rel))
        if rel <= 2:
            n = rel + 8
            pieces.append(below_ref[560 + 24 * n : 576 + 24 * n])
        if rel >= 8:
            n = rel - 8
            pieces.append(above_ref[560 + 24 * n : 576 + 24 * n])
        if rel <= -6:
            n = rel + 8
            pieces.append(below2_ref[16 * n : 16 * n + 16])
        if rel >= 16:
            n = rel - 16
            pieces.append(above2_ref[16 * n : 16 * n + 16])
        for piece in pieces:
            value = piece if value is None else value + piece
        coarse[p] = value
    lifted = []
    up_y, up_z = up_y_ref[...], up_z_ref[...]
    for e in range(11):
        value = coarse[e + 8] * (2.0 * coarse_weights[0])
        for d in range(1, 9):
            value = value + (coarse[e + 8 - d] + coarse[e + 8 + d]) * (2.0 * coarse_weights[d])
        point = 8 * dx - 1 + e
        value = value * ((point >= 0) & (point < 64)).astype(f32)
        h, m, l = split3(value)
        tall = dot(up_y, jnp.concatenate([h, m, l], 0).astype(bf16))
        h, m, l = split3(tall)
        stacked = jnp.concatenate([h, m, l], 0).astype(bf16)
        wide = dot(stacked, up_z)
        lifted.append(wide[0:24] + wide[24:48] + wide[48:72])
    mask = inside_mask((24, 256), 0, 16 * dy - 1, 128) * inside_mask((24, 256), 1, 128 * dz - 1, 256)
    lane = lax.broadcasted_iota(i32, (24, 256), 1)
    mask = jnp.where(lane < 131, mask, 0.0)
    for a in range(19):
        if a % 2:
            value = lifted[(a + 1) // 2]
        else:
            value = 0.5 * (lifted[a // 2] + lifted[a // 2 + 1])
        point = 16 * dx - 1 + a
        keep = mask * ((point >= 0) & (point < 128)).astype(f32)
        phi_ref[a] = jnp.where(keep > 0.0, third[a] + value, 0.0)


def gather_kernel(off_ref, charge_ref, counts_ref, phi_ref, out_ref):
    lane = lax.broadcasted_iota(i32, (1, 128), 1)
    lane176 = lax.broadcasted_iota(i32, (176, 128), 1)

    def column(ij, _):
        i, j = ij >> 1, ij & 1
        first = pl.multiple_of(8 * j, 8)
        low = jnp.concatenate([phi_ref[8 * i + a, pl.ds(first, 16), 0:128] for a in range(11)], 0)
        high = jnp.concatenate([phi_ref[8 * i + a, pl.ds(first, 16), 128:256] for a in range(11)], 0)
        for m in range(8):
            window = pltpu.roll(low, (128 - 16 * m) % 128, 1) if m else low
            if m == 7:
                window = jnp.where(lane176 < 16, window, pltpu.roll(high, 16, 1))
            window = jnp.where(lane176 < 32, window, 0.0)
            part_h = window.astype(bf16).astype(f32)
            part_m = window - part_h
            left = (part_h + pltpu.roll(part_m, 32, 1) + pltpu.roll(part_h, 64, 1)).astype(bf16)
            stacks, slopes, sides = [], [], []
            for half in range(2):
                k = 2 * m + half
                ox = off_ref[0, i, j, k : k + 1]
                oy = off_ref[1, i, j, k : k + 1]
                oz = off_ref[2, i, j, k : k + 1]
                count = counts_ref[ij * 16 + k]
                weighted = jnp.where(lane < count, charge_ref[i, j, k : k + 1], 0.0)
                shifted = weights_at(oz, 32, 8 * half)
                for bag, value in ((stacks, spline(shifted)), (slopes, spline_slope(shifted))):
                    high_part, low_part = split2(value)
                    bag.append(jnp.concatenate([high_part, high_part, low_part, jnp.zeros((32, 128), bf16)], 0))
                sides.append((ox, oy, weighted))
            right = jnp.concatenate(stacks + slopes, 1)
            product = dot(left, right)
            for half in range(2):
                k = 2 * m + half
                ox, oy, weighted = sides[half]
                level = product[:, 128 * half : 128 * half + 128]
                rising = product[:, 256 + 128 * half : 384 + 128 * half]
                sx = weights_at(ox, 16, 0)
                sy = weights_at(oy, 16, 0)
                wx, gx = spline(sx), spline_slope(sx)
                wy, gy = spline(sy), spline_slope(sy)
                along = across = up = None
                for a in range(11):
                    piece = level[16 * a : 16 * a + 16]
                    rise = rising[16 * a : 16 * a + 16]
                    terms = (gx[a : a + 1] * piece, wx[a : a + 1] * piece, wx[a : a + 1] * rise)
                    if a == 0:
                        along, across, up = terms
                    else:
                        along, across, up = along + terms[0], across + terms[1], up + terms[2]
                force_x = jnp.sum(along * wy, axis=0, keepdims=True)
                force_y = jnp.sum(across * gy, axis=0, keepdims=True)
                force_z = jnp.sum(up * wy, axis=0, keepdims=True)
                out_ref[0, i, j, k : k + 1] = -weighted * force_x
                out_ref[1, i, j, k : k + 1] = -weighted * force_y
                out_ref[2, i, j, k : k + 1] = -weighted * force_z
        return 0

    lax.fori_loop(0, 4, column, 0)


def pair_scratch(cells, tiles):
    return (
        [
            pltpu.VMEM((tiles, 8, 128), f32),
            pltpu.VMEM((tiles, 48, 128), bf16),
            pltpu.VMEM((tiles, 16, 128), bf16),
            pltpu.VMEM((cells + 1, 128, 128), bf16),
            pltpu.VMEM(((cells + 1) * (128 // ROWS), 16, 128), f32),
        ]
        + [
            pltpu.VMEM((ROWS, TILES * 128), f32),
            pltpu.VMEM((ROWS, TILES * 128), bf16),
            pltpu.VMEM((ROWS, TILES * 128), bf16),
        ]
        * SLOTS
        + [pltpu.SMEM((16,), i32)]
        + [pltpu.SMEM((cells + 1,), i32)] * 3
    )


def pair_task(scratch, cells, levels, center, own_pos, own_count, own_level, emit):
    packed, features, sources, own_features, sums = scratch[:5]
    start, first_tile, groups_of, blocks_of = scratch[-4:]
    slots = [scratch[5 + 3 * e : 8 + 3 * e] for e in range(SLOTS)]
    blocks = 128 // ROWS
    lane = lax.broadcasted_iota(i32, (8, 128), 1)
    row = lax.broadcasted_iota(i32, (8, 128), 0)

    def add_level(level, carry, beads):
        end, current = carry
        start[level] = end
        for value, count in beads(level):
            within, tile = end & 127, end >> 7
            turned = pltpu.roll(value, within, 1)
            keep = lane < within
            current = jnp.where(keep, current, turned)
            packed[tile] = current
            end = end + count
            current = jnp.where((end >> 7) > tile, jnp.where(keep, turned, 0.0), current)
        packed[end >> 7] = current
        return end, current

    carry = (i32(0), jnp.zeros((8, 128), f32))
    for low, high, beads in levels:
        if high - low > 1:
            carry = lax.fori_loop(low, high, lambda n, c, beads=beads: add_level(n, c, beads), carry)
        else:
            carry = add_level(low, carry, beads)
    end, current = carry
    start[10] = end
    packed[end >> 7] = jnp.where(lane < (end & 127), current, 0.0)
    for e in range(1, TILES + 4):
        packed[(end >> 7) + e] = jnp.zeros((8, 128), f32)
    used = (end >> 7) + 1 + TILES
    middle = jnp.where(row < 2, 16.0, jnp.where(row == 2, center, 0.0))

    def near_step(step, _):
        for e in range(4):
            tile = 4 * step + e
            value = packed[tile] - middle
            norm = value[0:1] * value[0:1] + value[1:2] * value[1:2] + value[2:3] * value[2:3]
            vector = jnp.where(row < 3, value, jnp.where(row == 3, norm, jnp.where(row == 4, 1.0, 0.0)))
            h, m, l = split3(vector)
            features[tile] = jnp.concatenate([h, h, m, m, h, l], 0).astype(bf16)
            charge = value[3:4]
            vector = jnp.where(row < 3, value * charge, jnp.where(row == 3, charge, 0.0))
            h, m, l = split3(vector)
            sources[tile] = jnp.concatenate(
                [jnp.where(row < 4, h, pltpu.roll(m, 4, 0)), jnp.where(row < 4, l, 0.0)], 0
            ).astype(bf16)
        return 0

    lax.fori_loop(0, (used + 3) // 4, near_step, 0)

    def own_step(n, total):
        value = own_pos(n) - middle
        norm = value[0:1] * value[0:1] + value[1:2] * value[1:2] + value[2:3] * value[2:3]
        vector = jnp.where(
            row < 3,
            value * (2.0 / 64),
            jnp.where(row == 3, -1.0 / 64, jnp.where(row == 4, 1.0 - norm * (1.0 / 64), 0.0)),
        )
        h, m, l = split3(vector)
        stacked = jnp.concatenate([h, m, h, m, l, h, jnp.zeros((80, 128), f32)], 0)
        own_features[n] = jnp.transpose(stacked).astype(bf16)
        for e in range(blocks):
            sums[n * blocks + e] = jnp.zeros((16, 128), f32)
        level = own_level(n)
        begin, stop = start[level], start[level + 3]
        tile = begin >> 7
        groups = jnp.maximum((((stop + 127) >> 7) - tile + TILES - 1) // TILES, 1)
        rows = (own_count(n) + ROWS - 1) // ROWS
        first_tile[n], groups_of[n], blocks_of[n] = tile, groups, rows
        return total + groups * rows

    total = lax.fori_loop(0, cells, own_step, i32(0))
    own_features[cells] = jnp.zeros((128, 128), bf16)
    for e in range(blocks):
        sums[cells * blocks + e] = jnp.zeros((16, 128), f32)
    first_tile[cells], groups_of[cells], blocks_of[cells] = i32(0), i32(1), i32(1)
    for distance, high, low in slots:
        distance[...] = jnp.zeros((ROWS, TILES * 128), f32)
        high[...] = jnp.zeros((ROWS, TILES * 128), bf16)
        low[...] = jnp.zeros((ROWS, TILES * 128), bf16)

    def item(_, state):
        cell, block, group = state[:3]
        older, oldest = state[3 : 3 + 2 * SLOTS], state[3 + 2 * SLOTS :]
        added, shares, fresh, tags = [], [], [], []
        for e in range(SLOTS):
            distance, high, low = slots[e]
            tile = oldest[2 * e + 1]
            source = jnp.concatenate([sources[tile + s] for s in range(TILES)], 1)
            added.append(
                lax.dot_general(
                    jnp.concatenate([source, source], 1),
                    jnp.concatenate([high[...], low[...]], 1),
                    LAST,
                    preferred_element_type=f32,
                )
            )
            reach = distance[...]
            kept = jnp.maximum(reach, 0.0)
            strength = (kept * kept * kept) / (CAP - reach)
            shares.append(split2(strength))
            groups, rows = groups_of[cell], blocks_of[cell]
            tile = first_tile[cell] + group * TILES
            at = pl.multiple_of(block * ROWS, ROWS)
            left = own_features[cell, pl.ds(at, ROWS), 0:48]
            right = jnp.concatenate([features[tile + s] for s in range(TILES)], 1)
            fresh.append(dot(left, right))
            tags += [cell * blocks + block, tile]
            group = group + 1
            wrap = (group >= groups).astype(i32)
            group = group * (1 - wrap)
            block = block + wrap
            wrap = (block >= rows).astype(i32)
            block = block * (1 - wrap)
            cell = jnp.minimum(cell + wrap, cells)
        for e in range(SLOTS):
            distance, high, low = slots[e]
            where = oldest[2 * e]
            sums[where, :, 0:ROWS] = sums[where, :, 0:ROWS] + added[e]
            high[...], low[...] = shares[e]
            distance[...] = fresh[e]
        return (cell, block, group) + tuple(tags) + tuple(older)

    spare = (i32(cells * blocks), i32(0))
    lax.fori_loop(0, (total + SLOTS - 1) // SLOTS + 2, item, (i32(0),) * 3 + spare * (2 * SLOTS))

    def finish(n, _):
        parts = [sums[n * blocks + e, :, 0:ROWS] for e in range(blocks)]
        whole = jnp.concatenate(parts, 1) if blocks > 1 else parts[0]
        whole = whole[0:4] + whole[4:8] + whole[8:12]
        raw = own_pos(n)
        value = raw - middle
        emit(n, (value[0:3] * whole[3:4] - whole[0:3]) * (raw[3:4] * (1.0 / 64)), raw)
        return 0

    lax.fori_loop(0, cells, finish, 0)


def inner_pairs_kernel(part, near_ref, counts_ref, partners_ref, after_ref, out_ref, *scratch):
    lane = lax.broadcasted_iota(i32, (1, 128), 1)

    def count_at(x, y, k):
        return counts_ref[(x * 2 + y) * 16 + k]

    def place(n):
        return n >> 4, (n >> 3) & 1, 8 * part + (n & 7)

    def beads(level):
        at = 8 * part + level
        valid = ((at >= 1) & (at <= 16)).astype(i32)
        return [
            (near_ref[x, y, at], count_at(x, y, jnp.clip(at - 1, 0, 15)) * valid) for x in range(2) for y in range(2)
        ]

    def own_pos(n):
        x, y, k = place(n)
        return near_ref[x, y, k + 1]

    def emit(n, value, raw):
        x, y, k = place(n)
        count = count_at(x, y, k)
        partner = partners_ref[x, y, pl.ds(k, 1), :]
        other = jnp.take_along_axis(raw, jnp.broadcast_to(partner, (8, 128)), axis=1)
        both = (lane < count) & (partner < count)
        out_ref[x, y, n & 7, 0:3] = value + jnp.where(both, -0.1 * (raw[0:3] - other[0:3]), 0.0)

    pair_task(
        scratch, 32, [(0, 10, beads)], 64.0 * part + 40.0, own_pos, lambda n: count_at(*place(n)), lambda n: n & 7, emit
    )


def outer_pairs_kernel(near2_ref, own_msg_ref, below_ref, above_ref, first_ref, second_ref, out_ref,
                       near, counts, table, *scratch):
    dz = lax.axis_index("ga")
    row8 = lax.broadcasted_iota(i32, (8, 128), 0)
    for n, source in enumerate((below_ref, own_msg_ref, above_ref)):
        pltpu.sync_copy(source.at[0:8], counts.at[n])
    below_shift = jnp.where(row8 == 0, -16.0, 0.0)
    above_shift = jnp.where(row8 == 0, 16.0, 0.0)

    def level_step(level, _):
        for x in range(2):
            for y in range(4):
                near[x + 1, y, level] = near2_ref[x, y, level]
        for x, source, shift in ((0, below_ref, below_shift), (3, above_ref, above_shift)):
            for pair in range(2):
                at = pl.multiple_of(8 + 8 * (2 * level + pair), 8)
                got = source[pl.ds(at, 8)]
                near[x, 2 * pair, level] = jnp.where(row8 < 4, got, 0.0) + shift
                near[x, 2 * pair + 1, level] = jnp.where(row8 < 4, pltpu.roll(got, 4, 0), 0.0) + shift
        return 0

    lax.fori_loop(0, 18, level_step, 0)
    for x in range(4):
        which, along = ((0, 1), (1, 0), (1, 1), (2, 0))[x]
        for y in range(4):
            pair_row, across = ((2, 1), (0, 0), (0, 1), (4, 0))[y]
            base = 32 * along + 16 * across
            at = (x * 4 + y) * 18
            table[at] = jnp.where(dz == 1, counts[which, pair_row + 1, base + 15], 0.0).astype(i32)
            table[at + 17] = jnp.where(dz == 0, counts[which, pair_row + 1, base], 0.0).astype(i32)

            def copy_count(k, _, which=which, pair_row=pair_row, base=base, at=at):
                table[at + 1 + k] = counts[which, pair_row, base + k].astype(i32)
                return 0

            lax.fori_loop(0, 16, copy_count, 0)

    def count_at(x, y, level):
        return table[(x * 4 + y) * 18 + level]

    def task(number, _):
        part, j, i = number & 1, (number >> 1) & 1, number >> 2
        outside = [(3 * i, j), (3 * i, j + 1), (3 * i, j + 2), (1, 3 * j), (2, 3 * j)]
        within = [(1, 1), (1, 2), (2, 1), (2, 2)]

        def beads(level):
            return [(near[x, y, 8 * part + level], count_at(x, y, 8 * part + level)) for x, y in outside]

        def with_inner(level, use):
            return beads(level) + [
                (near[x, y, 8 * part + level], count_at(x, y, 8 * part + level) * use) for x, y in within
            ]

        def emit(n, value, raw):
            first, second = first_ref[i, j, n, 0:3], second_ref[i, j, n, 0:3]
            value = value + jnp.where(part == 0, first, second)
            for d in range(3):
                out_ref[d, i, j, pl.ds(8 * part + n, 1), :] = value[d : d + 1]

        pair_task(
            scratch,
            8,
            [(0, 1, lambda n: with_inner(n, 1 - part)), (1, 9, beads), (9, 10, lambda n: with_inner(n, part))],
            64.0 * part.astype(f32) + 40.0,
            lambda n: near[i + 1, j + 1, 8 * part + n + 1],
            lambda n: count_at(i + 1, j + 1, 8 * part + n + 1),
            lambda n: n,
            emit,
        )
        return 0

    lax.fori_loop(0, 8, task, 0)


def call(kernel, shapes, inputs, specs=None, scratch=(), flops=10**6, out_specs=None):
    single = not isinstance(shapes, (list, tuple)) or isinstance(shapes[0], int)
    shapes = [shapes] if single else shapes
    result = pl.pallas_call(
        kernel,
        out_shape=[jax.ShapeDtypeStruct(s, f32) for s in shapes],
        in_specs=specs or [VMEM] * len(inputs),
        out_specs=[VMEM] * len(shapes),
        scratch_shapes=list(scratch),
        cost_estimate=pl.CostEstimate(flops=flops, transcendentals=0, bytes_accessed=10**6),
        compiler_params=pltpu.CompilerParams(vmem_limit_bytes=40 << 20),
    )(*inputs)
    return result[0] if single else result


def move(value, axis, step):
    size = lax.axis_size(axis)
    return lax.ppermute(value, axis, [(n, n + step) for n in range(size) if 0 <= n + step < size])


def exchange(up, down, up2, down2, axis):
    return move(up, axis, 1), move(down, axis, -1), move(up2, axis, 2), move(down2, axis, -2)


def per_device(offsets, charge, counts, partners):
    z_op = jnp.asarray(np.stack([np.stack(halves(z_operator(part))) for part in range(2)]))
    fine_op, coarse_op, y_down, y_up = [jnp.asarray(m) for m in y_operators()]
    z_up = jnp.asarray(z_prolong())
    counts = counts.reshape(64)
    block = jnp.pad(counts.astype(f32)[None, :], ((0, 7), (0, 64)))
    near, rho, z_msg = call(
        spread_kernel,
        [(2, 2, 18, 8, 128), (19, 24, 256), (144, 128)],
        (offsets, charge, counts, block),
        [VMEM, VMEM, SMEM, VMEM],
    )
    z_got = lax.ppermute(z_msg, "ga", [(0, 1), (1, 0)])
    near1, full, restr, *y_msgs = call(
        along_z_kernel,
        [(2, 2, 18, 8, 128), (19, 24, 256), (19, 16, 128), (760, 128), (760, 128), (152, 128), (152, 128)],
        (near, rho, z_msg, z_got, z_op, y_down),
    )
    y_got = exchange(*y_msgs, "gy")
    inner = lambda part, near_in, after: call(
        lambda *refs: inner_pairs_kernel(part, *refs),
        (2, 2, 8, 8, 128),
        (near_in, counts, partners, after),
        [VMEM, SMEM, VMEM, ANY],
        pair_scratch(32, 40 + TILES + 10),
        flops=10**9,
    )
    first = inner(0, near, full)
    near2, fine2, _, *x_msgs = call(
        along_y_kernel,
        [(2, 4, 18, 8, 128), (19, 24, 256), (19, 16, 128), (824, 128), (824, 128), (48, 128), (48, 128)],
        (near1, full, restr, y_msgs[0], *y_got, fine_op, coarse_op, first),
        [VMEM] * 10 + [ANY],
    )
    x_got = exchange(*x_msgs, "gx")
    second = inner(1, near, fine2)
    phi = call(
        along_x_kernel,
        (19, 24, 256),
        (fine2, x_msgs[0], x_msgs[1], *x_got, y_up, z_up, second),
        [VMEM] * 9 + [ANY],
        [pltpu.VMEM((35, 24, 256), f32), pltpu.VMEM((19, 24, 256), f32), pltpu.VMEM((27, 16, 128), f32)],
    )
    short_force = call(
        outer_pairs_kernel,
        (3, 2, 2, 16, 128),
        (near2, x_msgs[0], x_got[0], x_got[1], first, second),
        None,
        [
            pltpu.VMEM((4, 4, 18, 8, 128), f32),
            pltpu.SMEM((3, 8, 128), f32),
            pltpu.SMEM((288,), i32),
        ]
        + pair_scratch(8, 56 + TILES + 10),
        flops=10**9,
    )
    long_force = call(
        gather_kernel, (3, 2, 2, 16, 128), (offsets, charge, counts, phi), [VMEM, VMEM, SMEM, VMEM]
    )
    return short_force, long_force


def solution(mesh):
    return jax.shard_map(
        per_device,
        mesh=mesh,
        in_specs=(
            P(None, "gx", "gy", "ga", None),
            P("gx", "gy", "ga", None),
            P("gx", "gy", "ga"),
            P("gx", "gy", "ga", None),
        ),
        out_specs=(P(None, "gx", "gy", "ga", None), P(None, "gx", "gy", "ga", None)),
        check_vma=False,
    )
```

```python
import jax
import jax.numpy as jnp
import numpy as np
from jax import lax
from jax.experimental import pallas as pl
from jax.experimental.pallas import tpu as pltpu
from jax.sharding import PartitionSpec as P

f32, bf16, i32 = jnp.float32, jnp.bfloat16, jnp.int32
LAST = (((1,), (1,)), ((), ()))
CAP = 65.0 / 64.0
ROWS, TILES, SLOTS = 64, 2, 8
VMEM = pl.BlockSpec(memory_space=pltpu.VMEM)
SMEM = pl.BlockSpec(memory_space=pltpu.SMEM)
ANY = pl.BlockSpec(memory_space=pl.ANY)


def fine_kernel(gap):
    return np.where(np.abs(gap) <= 8, np.exp(-gap * gap / 12.5), 0.0)


def coarse_kernel(gap):
    return np.where(np.abs(gap) <= 8, np.exp(-gap * gap / 72.0), 0.0)


def hat(gap):
    return np.where(gap == 0, 1.0, np.where(np.abs(gap) == 1, 0.5, 0.0))


def halves(matrix):
    high = matrix.astype(np.float32).astype(jnp.bfloat16)
    low = (matrix - high.astype(np.float64)).astype(np.float32).astype(jnp.bfloat16)
    return high, low


def z_operator(part):
    source = np.full(256, 10**6, np.int64)
    source[:131] = 128 * part - 1 + np.arange(131)
    source[160:181] = np.arange(21) + (127 if part == 0 else 109)
    inside = (source >= 0) & (source < 256)
    result = np.zeros((256, 256))
    target = 128 * part - 1 + np.arange(131)
    fine = fine_kernel((target[None, :] - source[:, None]).astype(np.float64))
    result[:, :131] = fine * ((target >= 0) & (target < 256))[None, :]
    middle = np.arange(128)
    down = hat((source[:, None] - 2 * middle[None, :]).astype(np.float64))
    point = 64 * part - 1 + np.arange(67)
    spread = coarse_kernel((middle[:, None] - point[None, :]).astype(np.float64))
    spread = spread * ((point >= 0) & (point < 128))[None, :]
    result[:, 136:203] = down @ spread
    return result * inside[:, None]


def y_operators():
    own = np.where(np.arange(24) < 19, np.arange(24), 10**6)
    below = np.where(np.arange(16) < 11, np.arange(16) - 8, 10**6)
    above = np.where(np.arange(16) < 11, np.arange(16) + 16, 10**6)
    source = np.concatenate([own, below, above]).astype(np.float64)
    fine = fine_kernel(np.arange(24)[:, None] - source[None, :])
    fine[19:] = 0
    own = np.where(np.arange(16) < 11, np.arange(16), 10**6)
    below = np.where(np.arange(16) < 11, np.arange(16) - 8, 10**6)
    above = np.where(np.arange(16) < 11, np.arange(16) + 8, 10**6)
    far_below = np.where(np.arange(8) < 3, np.arange(8) - 8, 10**6)
    far_above = np.where(np.arange(8) < 3, np.arange(8) + 16, 10**6)
    source = np.concatenate([own, below, above, far_below, far_above]).astype(np.float64)
    coarse = coarse_kernel(np.arange(16)[:, None] - source[None, :])
    coarse[11:] = 0
    down = hat(np.arange(24)[None, :] - (2.0 * np.arange(16)[:, None] - 1))
    down[11:] = 0
    up = hat(np.arange(24)[:, None] - (2.0 * np.arange(16)[None, :] - 1))
    up[19:] = 0
    up[:, 11:] = 0
    stack = lambda m: np.concatenate([halves(m)[0], halves(m)[1], halves(m)[0]], 1)
    thrice = lambda m: np.concatenate([halves(m)[0]] * 3, 1)
    return stack(fine), stack(coarse), thrice(down), thrice(up)


def z_prolong():
    result = np.zeros((128, 256))
    point = 2.0 * np.arange(67) - 1
    result[8:75, :131] = hat(np.arange(131)[None, :] - point[:, None])
    return halves(result)[0]


def split2(value):
    high = value.astype(bf16)
    return high, (value - high.astype(f32)).astype(bf16)


def split3(value):
    high = value.astype(bf16).astype(f32)
    rest = value - high
    middle = rest.astype(bf16).astype(f32)
    return high, middle, rest - middle


def dot(left, right):
    return jnp.dot(left, right, preferred_element_type=f32)


def spline(shifted):
    magnitude = jnp.abs(shifted)
    margin = jnp.maximum(1.5 - magnitude, 0.0)
    return jnp.where(magnitude < 0.5, 0.75 - shifted * shifted, 0.5 * margin * margin)


def spline_slope(shifted):
    magnitude = jnp.abs(shifted)
    margin = jnp.maximum(1.5 - magnitude, 0.0)
    return jnp.where(magnitude < 0.5, -2.0 * shifted, jnp.where(shifted > 0.0, -margin, margin))


def weights_at(offset, rows, first):
    points = lax.broadcasted_iota(i32, (rows, 128), 0).astype(f32)
    return 8.0 * offset + (1.0 + first) - points


def inside_mask(shape, dim, start, count):
    point = lax.broadcasted_iota(i32, shape, dim) + start
    return ((point >= 0) & (point < count)).astype(f32)


def spread_kernel(off_ref, charge_ref, counts_ref, block_ref, near_ref, rho_ref, msg_ref):
    dx, dy, dz = lax.axis_index("gx"), lax.axis_index("gy"), lax.axis_index("ga")
    lane = lax.broadcasted_iota(i32, (1, 128), 1)
    row8 = lax.broadcasted_iota(i32, (8, 128), 0)
    rho_ref[...] = jnp.zeros((19, 24, 256), f32)
    zero8 = jnp.zeros((8, 128), f32)
    for i in range(2):
        for j in range(2):
            near_ref[i, j, 0] = zero8
            near_ref[i, j, 17] = zero8

    def column(ij, _):
        i, j = ij >> 1, ij & 1
        shift_x = 8.0 * (i + 1).astype(f32)
        shift_y = 8.0 * (j + 1).astype(f32)
        total = jnp.zeros((176, 128), f32)
        tail = None
        for m in range(8):
            highs, lows, z_highs, z_lows = [], [], [], []
            for half in range(2):
                k = 2 * m + half
                ox = off_ref[0, i, j, k : k + 1]
                oy = off_ref[1, i, j, k : k + 1]
                oz = off_ref[2, i, j, k : k + 1]
                count = counts_ref[ij * 16 + k]
                weighted = jnp.where(lane < count, charge_ref[i, j, k : k + 1], 0.0)
                near_ref[i, j, k + 1] = jnp.concatenate(
                    [8.0 * ox + shift_x, 8.0 * oy + shift_y, 8.0 * oz + 8.0 * (k + 1), weighted, zero8[:4]], 0
                )
                wx = spline(weights_at(ox, 16, 0)) * weighted
                wy = spline(weights_at(oy, 16, 0))
                wz = spline(weights_at(oz, 32, 8 * half))
                plane = jnp.concatenate([wx[a : a + 1] * wy for a in range(11)], 0)
                high, low = split2(plane)
                highs.append(high)
                lows.append(low)
                z_high, z_low = split2(wz)
                z_highs.append(z_high)
                z_lows.append(z_low)
            left = jnp.concatenate(highs + lows + highs, 1)
            right = jnp.concatenate(z_highs + z_highs + z_lows, 1)
            if m < 7:
                pieces = [right]
                if m > 0:
                    pieces = [jnp.zeros((16 * m, 768), bf16)] + pieces
                if m < 6:
                    pieces = pieces + [jnp.zeros((96 - 16 * m, 768), bf16)]
                total = total + lax.dot_general(left, jnp.concatenate(pieces, 0), LAST, preferred_element_type=f32)
            else:
                wide = jnp.concatenate([jnp.zeros((112, 768), bf16), right, jnp.zeros((112, 768), bf16)], 0)
                both = lax.dot_general(left, wide, LAST, preferred_element_type=f32)
                total = total + both[:, :128]
                tail = both[:, 128:]
        first = pl.multiple_of(8 * j, 8)
        for a in range(11):
            rho_ref[8 * i + a, pl.ds(first, 16), 0:128] += total[16 * a : 16 * a + 16]
            rho_ref[8 * i + a, pl.ds(first, 16), 128:256] += tail[16 * a : 16 * a + 16]
        return 0

    lax.fori_loop(0, 4, column, 0)
    mask_y = inside_mask((24, 256), 0, 16 * dy - 1, 128)
    mask_z = inside_mask((24, 256), 1, 128 * dz - 1, 256)
    mask = mask_y * mask_z
    wide_lane = lax.broadcasted_iota(i32, (24, 128), 1)
    msg_ref[0:8] = block_ref[...]
    for i in range(2):
        picked = [jnp.where(dz == 0, near_ref[i, j, 16], near_ref[i, j, 1]) for j in range(2)]
        msg_ref[8 + 8 * i : 16 + 8 * i] = jnp.where(row8 < 4, picked[0], pltpu.roll(picked[1], 4, 0))
    faces = []
    for a in range(19):
        point = 16 * dx - 1 + a
        keep = ((point >= 0) & (point < 128)).astype(f32)
        plane = rho_ref[a] * (mask * keep)
        rho_ref[a] = plane
        low, high = plane[:, :128], plane[:, 128:]
        top = jnp.where(wide_lane < 18, pltpu.roll(low, 18, 1), pltpu.roll(high, 18, 1))
        face = jnp.where(dz == 0, top, low)
        faces.append(jnp.where(wide_lane < 21, face, 0.0))
    faces.append(jnp.zeros((24, 128), f32))
    for p in range(5):
        packed = faces[p]
        for g in range(1, 4):
            packed = packed + pltpu.roll(faces[5 * g + p], 32 * g, 1)
        msg_ref[24 + 24 * p : 48 + 24 * p] = packed


def along_z_kernel(near_ref, rho_ref, own_msg_ref, got_ref, op_ref, down_ref,
                   near1_ref, full_ref, restr_ref, up_ref, dn_ref, up2_ref, dn2_ref):
    dy, dz = lax.axis_index("gy"), lax.axis_index("ga")
    row8 = lax.broadcasted_iota(i32, (8, 128), 0)
    shift = jnp.where(row8 == 2, jnp.where(dz == 0, 128.0, -128.0), 0.0)
    for i in range(2):
        got = got_ref[8 + 8 * i : 16 + 8 * i]
        parts = [jnp.where(row8 < 4, got, 0.0), jnp.where(row8 < 4, pltpu.roll(got, 4, 0), 0.0)]
        for j in range(2):
            near1_ref[i, j, 1:17] = near_ref[i, j, 1:17]
            moved = parts[j] + shift
            near1_ref[i, j, 0] = jnp.where(dz == 1, moved, 0.0)
            near1_ref[i, j, 17] = jnp.where(dz == 0, moved, 0.0)
    lane = lax.broadcasted_iota(i32, (24, 128), 1)
    high_op, low_op = op_ref[dz, 0], op_ref[dz, 1]
    down = down_ref[...]
    lane16 = lax.broadcasted_iota(i32, (16, 128), 1)
    keep = inside_mask((16, 128), 0, 8 * dy - 1, 64)
    for g in range(4):
        planes = range(5 * g, min(5 * g + 5, 19))
        stacked = []
        for p, a in enumerate(planes):
            face = pltpu.roll(got_ref[24 + 24 * p : 48 + 24 * p], (32 - 32 * g) % 128, 1)
            second = jnp.where((lane >= 32) & (lane < 64), face, rho_ref[a, :, 128:256])
            stacked.append(jnp.concatenate([rho_ref[a, :, 0:128], second], 1))
        high, low = split2(jnp.concatenate(stacked, 0))
        result = dot(high, high_op) + dot(low, high_op) + dot(high, low_op)
        for p, a in enumerate(planes):
            plane = result[24 * p : 24 * p + 24]
            full_ref[a] = plane
            h, m, l = split3(plane[:, 128:256])
            restricted = dot(down, jnp.concatenate([h, m, l], 0).astype(bf16)) * keep
            restr_ref[a] = restricted
            for out, first in ((up_ref, 8), (dn_ref, 0)):
                out[152 + 16 * a : 168 + 16 * a] = plane[first : first + 16, 0:128]
                out[456 + 16 * a : 472 + 16 * a] = jnp.where(
                    lane16 < 8, plane[first : first + 16, 128:256], restricted
                )
            up2_ref[8 * a : 8 * a + 8] = restricted[8:16]
            dn2_ref[8 * a : 8 * a + 8] = restricted[0:8]
    counts = jnp.where(row8 == 0, own_msg_ref[0:8], jnp.where(row8 == 1, pltpu.roll(got_ref[0:8], 1, 0), 0.0))
    for out, j in ((up_ref, 1), (dn_ref, 0)):
        out[0:8] = counts
        for level in range(18):
            out[8 + 8 * level : 16 + 8 * level] = jnp.where(
                row8 < 4, near1_ref[0, j, level], pltpu.roll(near1_ref[1, j, level], 4, 0)
            )


def along_y_kernel(near1_ref, full_ref, restr_ref, up_own_ref, below_ref, above_ref, below2_ref, above2_ref,
                   fine_ref, coarse_ref, after_ref, near2_ref, fine2_ref, coarse2_ref,
                   up_ref, dn_ref, up2_ref, dn2_ref):
    dx, dy = lax.axis_index("gx"), lax.axis_index("gy")
    row8 = lax.broadcasted_iota(i32, (8, 128), 0)
    keep = inside_mask((16, 128), 0, 8 * dy - 1, 64)
    lane16 = lax.broadcasted_iota(i32, (16, 128), 1)
    lane24 = lax.broadcasted_iota(i32, (24, 128), 1)
    fine_op, coarse_op = fine_ref[...], coarse_ref[...]

    def plane(a, _):
        at = pl.multiple_of(16 * a, 16)
        at8 = pl.multiple_of(8 * a, 8)
        below_low = below_ref[pl.ds(152 + at, 16)]
        below_high = below_ref[pl.ds(456 + at, 16)]
        above_low = above_ref[pl.ds(152 + at, 16)]
        above_high = above_ref[pl.ds(456 + at, 16)]
        stack = jnp.concatenate(
            [
                full_ref[a],
                jnp.concatenate([below_low, below_high], 1),
                jnp.concatenate([above_low, above_high], 1),
            ],
            0,
        )
        high, low = split3(stack)[:2]
        fine2_ref[a] = dot(fine_op, jnp.concatenate([high, high, low], 0).astype(bf16))
        stack = jnp.concatenate(
            [restr_ref[a], below_high, above_high, below2_ref[pl.ds(at8, 8)], above2_ref[pl.ds(at8, 8)]], 0
        )
        high, low = split3(stack)[:2]
        coarse2_ref[a] = dot(coarse_op, jnp.concatenate([high, high, low], 0).astype(bf16)) * keep
        return 0

    lax.fori_loop(0, 19, plane, 0)
    restricted = []
    for e in range(11):
        value = None
        for a, weight in ((2 * e - 2, 0.5), (2 * e - 1, 1.0), (2 * e, 0.5)):
            if 0 <= a < 19:
                term = coarse2_ref[a] * weight
                value = term if value is None else value + term
        point = 8 * dx - 1 + e
        restricted.append(value * ((point >= 0) & (point < 64)).astype(f32))
    blank = jnp.zeros((8, 128), f32)
    for out, first in ((up_ref, 8), (dn_ref, 0)):
        for n in range(11):
            plane_value = fine2_ref[first + n]
            out[296 + 24 * n : 320 + 24 * n] = plane_value[:, 0:128]
            out[560 + 24 * n : 584 + 24 * n] = jnp.where(
                lane24 < 8, plane_value[:, 128:256], jnp.concatenate([restricted[n], blank], 0)
            )
    for n in range(3):
        up2_ref[16 * n : 16 * n + 16] = restricted[8 + n]
        dn2_ref[16 * n : 16 * n + 16] = restricted[n]
    shift_down = jnp.where(row8 == 1, -16.0, 0.0)
    shift_up = jnp.where(row8 == 1, 16.0, 0.0)
    for level in range(18):
        for y, source, shift in ((0, below_ref, shift_down), (3, above_ref, shift_up)):
            got = source[8 + 8 * level : 16 + 8 * level]
            near2_ref[0, y, level] = jnp.where(row8 < 4, got, 0.0) + shift
            near2_ref[1, y, level] = jnp.where(row8 < 4, pltpu.roll(got, 4, 0), 0.0) + shift
        for x in range(2):
            for y in range(2):
                near2_ref[x, y + 1, level] = near1_ref[x, y, level]
    counts = jnp.where(row8 < 2, up_own_ref[0:8], 0.0)
    counts = jnp.where((row8 >= 2) & (row8 < 4), pltpu.roll(below_ref[0:8], 2, 0), counts)
    counts = jnp.where((row8 >= 4) & (row8 < 6), pltpu.roll(above_ref[0:8], 4, 0), counts)
    for out, x in ((up_ref, 1), (dn_ref, 0)):
        out[0:8] = counts
        for level in range(18):
            for pair in range(2):
                at = 8 + 8 * (2 * level + pair)
                out[at : at + 8] = jnp.where(
                    row8 < 4, near2_ref[x, 2 * pair, level], pltpu.roll(near2_ref[x, 2 * pair + 1, level], 4, 0)
                )


def along_x_kernel(fine2_ref, up_own_ref, dn_own_ref, below_ref, above_ref, below2_ref, above2_ref,
                   up_y_ref, up_z_ref, after_ref, phi_ref, source, third, coarse):
    dx, dy, dz = lax.axis_index("gx"), lax.axis_index("gy"), lax.axis_index("ga")
    for p in range(35):
        rel = p - 8
        low = high = None
        pieces = []
        if 0 <= rel < 19:
            pieces.append((fine2_ref[rel, :, 0:128], fine2_ref[rel, :, 128:256]))
        if rel <= 2:
            n = rel + 8
            pieces.append((below_ref[296 + 24 * n : 320 + 24 * n], below_ref[560 + 24 * n : 584 + 24 * n]))
        if rel >= 16:
            n = rel - 16
            pieces.append((above_ref[296 + 24 * n : 320 + 24 * n], above_ref[560 + 24 * n : 584 + 24 * n]))
        for low_piece, high_piece in pieces:
            low = low_piece if low is None else low + low_piece
            high = high_piece if high is None else high + high_piece
        source[p, :, 0:128] = low
        source[p, :, 128:256] = high
    fine_weights = [float(w) for w in fine_kernel(np.arange(9.0))]
    coarse_weights = [float(w) for w in coarse_kernel(np.arange(9.0))]

    def fine_plane(a, _):
        value = source[a + 8] * (4.0 * fine_weights[0])
        for d in range(1, 9):
            value = value + (source[a + 8 - d] + source[a + 8 + d]) * (4.0 * fine_weights[d])
        third[a] = value
        return 0

    lax.fori_loop(0, 19, fine_plane, 0)

    def own_coarse(e):
        ref, n = (up_own_ref, e)
        return ref[560 + 24 * n : 576 + 24 * n]

    for p in range(27):
        rel = p - 8
        value = None
        pieces = []
        if 0 <= rel < 11:
            pieces.append(own_coarse(rel))
        if rel <= 2:
            n = rel + 8
            pieces.append(below_ref[560 + 24 * n : 576 + 24 * n])
        if rel >= 8:
            n = rel - 8
            pieces.append(above_ref[560 + 24 * n : 576 + 24 * n])
        if rel <= -6:
            n = rel + 8
            pieces.append(below2_ref[16 * n : 16 * n + 16])
        if rel >= 16:
            n = rel - 16
            pieces.append(above2_ref[16 * n : 16 * n + 16])
        for piece in pieces:
            value = piece if value is None else value + piece
        coarse[p] = value
    lifted = []
    up_y, up_z = up_y_ref[...], up_z_ref[...]
    for e in range(11):
        value = coarse[e + 8] * (2.0 * coarse_weights[0])
        for d in range(1, 9):
            value = value + (coarse[e + 8 - d] + coarse[e + 8 + d]) * (2.0 * coarse_weights[d])
        point = 8 * dx - 1 + e
        value = value * ((point >= 0) & (point < 64)).astype(f32)
        h, m, l = split3(value)
        tall = dot(up_y, jnp.concatenate([h, m, l], 0).astype(bf16))
        h, m, l = split3(tall)
        stacked = jnp.concatenate([h, m, l], 0).astype(bf16)
        wide = dot(stacked, up_z)
        lifted.append(wide[0:24] + wide[24:48] + wide[48:72])
    mask = inside_mask((24, 256), 0, 16 * dy - 1, 128) * inside_mask((24, 256), 1, 128 * dz - 1, 256)
    lane = lax.broadcasted_iota(i32, (24, 256), 1)
    mask = jnp.where(lane < 131, mask, 0.0)
    for a in range(19):
        if a % 2:
            value = lifted[(a + 1) // 2]
        else:
            value = 0.5 * (lifted[a // 2] + lifted[a // 2 + 1])
        point = 16 * dx - 1 + a
        keep = mask * ((point >= 0) & (point < 128)).astype(f32)
        phi_ref[a] = jnp.where(keep > 0.0, third[a] + value, 0.0)


def gather_kernel(off_ref, charge_ref, counts_ref, phi_ref, out_ref):
    lane = lax.broadcasted_iota(i32, (1, 128), 1)
    lane176 = lax.broadcasted_iota(i32, (176, 128), 1)

    def column(ij, _):
        i, j = ij >> 1, ij & 1
        first = pl.multiple_of(8 * j, 8)
        low = jnp.concatenate([phi_ref[8 * i + a, pl.ds(first, 16), 0:128] for a in range(11)], 0)
        high = jnp.concatenate([phi_ref[8 * i + a, pl.ds(first, 16), 128:256] for a in range(11)], 0)
        for m in range(8):
            window = pltpu.roll(low, (128 - 16 * m) % 128, 1) if m else low
            if m == 7:
                window = jnp.where(lane176 < 16, window, pltpu.roll(high, 16, 1))
            window = jnp.where(lane176 < 32, window, 0.0)
            part_h = window.astype(bf16).astype(f32)
            part_m = window - part_h
            left = (part_h + pltpu.roll(part_m, 32, 1) + pltpu.roll(part_h, 64, 1)).astype(bf16)
            stacks, slopes, sides = [], [], []
            for half in range(2):
                k = 2 * m + half
                ox = off_ref[0, i, j, k : k + 1]
                oy = off_ref[1, i, j, k : k + 1]
                oz = off_ref[2, i, j, k : k + 1]
                count = counts_ref[ij * 16 + k]
                weighted = jnp.where(lane < count, charge_ref[i, j, k : k + 1], 0.0)
                shifted = weights_at(oz, 32, 8 * half)
                for bag, value in ((stacks, spline(shifted)), (slopes, spline_slope(shifted))):
                    high_part, low_part = split2(value)
                    bag.append(jnp.concatenate([high_part, high_part, low_part, jnp.zeros((32, 128), bf16)], 0))
                sides.append((ox, oy, weighted))
            right = jnp.concatenate(stacks + slopes, 1)
            product = dot(left, right)
            for half in range(2):
                k = 2 * m + half
                ox, oy, weighted = sides[half]
                level = product[:, 128 * half : 128 * half + 128]
                rising = product[:, 256 + 128 * half : 384 + 128 * half]
                sx = weights_at(ox, 16, 0)
                sy = weights_at(oy, 16, 0)
                wx, gx = spline(sx), spline_slope(sx)
                wy, gy = spline(sy), spline_slope(sy)
                along = across = up = None
                for a in range(11):
                    piece = level[16 * a : 16 * a + 16]
                    rise = rising[16 * a : 16 * a + 16]
                    terms = (gx[a : a + 1] * piece, wx[a : a + 1] * piece, wx[a : a + 1] * rise)
                    if a == 0:
                        along, across, up = terms
                    else:
                        along, across, up = along + terms[0], across + terms[1], up + terms[2]
                force_x = jnp.sum(along * wy, axis=0, keepdims=True)
                force_y = jnp.sum(across * gy, axis=0, keepdims=True)
                force_z = jnp.sum(up * wy, axis=0, keepdims=True)
                out_ref[0, i, j, k : k + 1] = -weighted * force_x
                out_ref[1, i, j, k : k + 1] = -weighted * force_y
                out_ref[2, i, j, k : k + 1] = -weighted * force_z
        return 0

    lax.fori_loop(0, 4, column, 0)


def pair_scratch(cells, tiles):
    return (
        [
            pltpu.VMEM((tiles, 8, 128), f32),
            pltpu.VMEM((tiles, 48, 128), bf16),
            pltpu.VMEM((tiles, 16, 128), bf16),
            pltpu.VMEM((cells + 1, 128, 128), f32),
            pltpu.VMEM(((cells + 1) * (128 // ROWS), 16, 128), f32),
        ]
        + [
            pltpu.VMEM((ROWS, TILES * 128), f32),
            pltpu.VMEM((ROWS, TILES * 128), bf16),
            pltpu.VMEM((ROWS, TILES * 128), bf16),
        ]
        * SLOTS
        + [pltpu.SMEM((16,), i32)]
        + [pltpu.SMEM((cells + 1,), i32)] * 3
    )


def pair_task(scratch, cells, levels, center, own_pos, own_count, own_level, emit):
    packed, features, sources, own_features, sums = scratch[:5]
    start, first_tile, groups_of, blocks_of = scratch[-4:]
    slots = [scratch[5 + 3 * e : 8 + 3 * e] for e in range(SLOTS)]
    blocks = 128 // ROWS
    lane = lax.broadcasted_iota(i32, (8, 128), 1)
    row = lax.broadcasted_iota(i32, (8, 128), 0)

    def add_level(level, carry, beads):
        end, current = carry
        start[level] = end
        for value, count in beads(level):
            within, tile = end & 127, end >> 7
            turned = pltpu.roll(value, within, 1)
            keep = lane < within
            current = jnp.where(keep, current, turned)
            packed[tile] = current
            end = end + count
            current = jnp.where((end >> 7) > tile, jnp.where(keep, turned, 0.0), current)
        packed[end >> 7] = current
        return end, current

    carry = (i32(0), jnp.zeros((8, 128), f32))
    for low, high, beads in levels:
        for level in range(low, high):
            carry = add_level(level, carry, beads)
    end, current = carry
    start[10] = end
    packed[end >> 7] = jnp.where(lane < (end & 127), current, 0.0)
    for e in range(1, TILES + 9):
        packed[(end >> 7) + e] = jnp.zeros((8, 128), f32)
    used = (end >> 7) + 1 + TILES
    middle = jnp.where(row < 2, 16.0, jnp.where(row == 2, center, 0.0))

    def near_step(step, _):
        for e in range(8):
            tile = 8 * step + e
            value = packed[tile] - middle
            norm = value[0:1] * value[0:1] + value[1:2] * value[1:2] + value[2:3] * value[2:3]
            vector = jnp.where(row < 3, value, jnp.where(row == 3, norm, jnp.where(row == 4, 1.0, 0.0)))
            h, m, l = split3(vector)
            features[tile] = jnp.concatenate([h, h, m, m, h, l], 0).astype(bf16)
            charge = value[3:4]
            vector = jnp.where(row < 3, value * charge, jnp.where(row == 3, charge, 0.0))
            h, m, l = split3(vector)
            sources[tile] = jnp.concatenate(
                [jnp.where(row < 4, h, pltpu.roll(m, 4, 0)), jnp.where(row < 4, l, 0.0)], 0
            ).astype(bf16)
        return 0

    lax.fori_loop(0, (used + 7) // 8, near_step, 0)

    def own_one(n, total):
        value = own_pos(n) - middle
        norm = value[0:1] * value[0:1] + value[1:2] * value[1:2] + value[2:3] * value[2:3]
        vector = jnp.where(
            row < 3,
            value * (2.0 / 64),
            jnp.where(row == 3, -1.0 / 64, jnp.where(row == 4, 1.0 - norm * (1.0 / 64), 0.0)),
        )
        h, m, l = split3(vector)
        stacked = jnp.concatenate([h, m, h, m, l, h, jnp.zeros((80, 128), f32)], 0)
        own_features[n] = jnp.transpose(stacked)
        for e in range(blocks):
            sums[n * blocks + e] = jnp.zeros((16, 128), f32)
        level = own_level(n)
        begin, stop = start[level], start[level + 3]
        tile = begin >> 7
        groups = jnp.maximum((((stop + 127) >> 7) - tile + TILES - 1) // TILES, 1)
        rows = (own_count(n) + ROWS - 1) // ROWS
        first_tile[n], groups_of[n], blocks_of[n] = tile, groups, rows
        return total + groups * rows

    def own_step(step, total):
        for e in range(8):
            total = own_one(8 * step + e, total)
        return total

    total = lax.fori_loop(0, cells // 8, own_step, i32(0))
    own_features[cells] = jnp.zeros((128, 128), f32)
    for e in range(blocks):
        sums[cells * blocks + e] = jnp.zeros((16, 128), f32)
    first_tile[cells], groups_of[cells], blocks_of[cells] = i32(0), i32(1), i32(1)
    for distance, high, low in slots:
        distance[...] = jnp.zeros((ROWS, TILES * 128), f32)
        high[...] = jnp.zeros((ROWS, TILES * 128), bf16)
        low[...] = jnp.zeros((ROWS, TILES * 128), bf16)

    def item(_, state):
        cell, block, group = state[:3]
        older, oldest = state[3 : 3 + 2 * SLOTS], state[3 + 2 * SLOTS :]
        added, shares, fresh, tags = [], [], [], []
        for e in range(SLOTS):
            distance, high, low = slots[e]
            tile = oldest[2 * e + 1]
            source = jnp.concatenate([sources[tile + s] for s in range(TILES)], 1)
            added.append(
                lax.dot_general(
                    jnp.concatenate([source, source], 1),
                    jnp.concatenate([high[...], low[...]], 1),
                    LAST,
                    preferred_element_type=f32,
                )
            )
            reach = distance[...]
            kept = jnp.maximum(reach, 0.0)
            strength = (kept * kept * kept) / (CAP - reach)
            shares.append(split2(strength))
            groups, rows = groups_of[cell], blocks_of[cell]
            tile = first_tile[cell] + group * TILES
            at = pl.multiple_of(block * ROWS, ROWS)
            left = own_features[cell, pl.ds(at, ROWS), 0:48].astype(bf16)
            right = jnp.concatenate([features[tile + s] for s in range(TILES)], 1)
            fresh.append(dot(left, right))
            tags += [cell * blocks + block, tile]
            group = group + 1
            wrap = (group >= groups).astype(i32)
            group = group * (1 - wrap)
            block = block + wrap
            wrap = (block >= rows).astype(i32)
            block = block * (1 - wrap)
            cell = jnp.minimum(cell + wrap, cells)
        for e in range(SLOTS):
            distance, high, low = slots[e]
            where = oldest[2 * e]
            sums[where, :, 0:ROWS] = sums[where, :, 0:ROWS] + added[e]
            high[...], low[...] = shares[e]
            distance[...] = fresh[e]
        return (cell, block, group) + tuple(tags) + tuple(older)

    spare = (i32(cells * blocks), i32(0))
    lax.fori_loop(0, (total + SLOTS - 1) // SLOTS + 2, item, (i32(0),) * 3 + spare * (2 * SLOTS))

    def finish_one(n):
        parts = [sums[n * blocks + e, :, 0:ROWS] for e in range(blocks)]
        whole = jnp.concatenate(parts, 1) if blocks > 1 else parts[0]
        whole = whole[0:4] + whole[4:8] + whole[8:12]
        raw = own_pos(n)
        value = raw - middle
        emit(n, (value[0:3] * whole[3:4] - whole[0:3]) * (raw[3:4] * (1.0 / 64)), raw)

    def finish(step, _):
        for e in range(4):
            finish_one(4 * step + e)
        return 0

    lax.fori_loop(0, cells // 4, finish, 0)


def inner_pairs_kernel(part, near_ref, counts_ref, partners_ref, after_ref, out_ref, table, *scratch):
    lane = lax.broadcasted_iota(i32, (1, 128), 1)
    for column in range(4):
        table[18 * column] = i32(0)
        table[18 * column + 17] = i32(0)

    def copy_count(k, _):
        for column in range(4):
            table[18 * column + 1 + k] = counts_ref[16 * column + k]
        return 0

    lax.fori_loop(0, 16, copy_count, 0)

    def beads(level):
        return [(near_ref[18 * c + 8 * part + level], table[18 * c + 8 * part + level]) for c in range(4)]

    def cell_at(n):
        return (n >> 3) * 18 + (n & 7) + (8 * part + 1)

    def emit(n, value, raw):
        x, y, k = n >> 4, (n >> 3) & 1, 8 * part + (n & 7)
        count = table[cell_at(n)]
        partner = partners_ref[x, y, pl.ds(k, 1), :]
        other = jnp.take_along_axis(raw, jnp.broadcast_to(partner, (8, 128)), axis=1)
        both = (lane < count) & (partner < count)
        out_ref[x, y, n & 7, 0:3] = value + jnp.where(both, -0.1 * (raw[0:3] - other[0:3]), 0.0)

    pair_task(
        scratch,
        32,
        [(0, 10, beads)],
        64.0 * part + 40.0,
        lambda n: near_ref[cell_at(n)],
        lambda n: table[cell_at(n)],
        lambda n: n & 7,
        emit,
    )


def outer_pairs_kernel(near2_ref, own_msg_ref, below_ref, above_ref, first_ref, second_ref, out_ref,
                       near, counts, table, *scratch):
    dz = lax.axis_index("ga")
    row8 = lax.broadcasted_iota(i32, (8, 128), 0)
    for n, source in enumerate((below_ref, own_msg_ref, above_ref)):
        pltpu.sync_copy(source.at[0:8], counts.at[n])
    below_shift = jnp.where(row8 == 0, -16.0, 0.0)
    above_shift = jnp.where(row8 == 0, 16.0, 0.0)

    def level_step(level, _):
        for x in range(2):
            for y in range(4):
                near[(4 * x + 4 + y) * 18 + level] = near2_ref[x, y, level]
        for x, source, shift in ((0, below_ref, below_shift), (3, above_ref, above_shift)):
            for pair in range(2):
                at = pl.multiple_of(8 + 8 * (2 * level + pair), 8)
                got = source[pl.ds(at, 8)]
                near[(4 * x + 2 * pair) * 18 + level] = jnp.where(row8 < 4, got, 0.0) + shift
                near[(4 * x + 2 * pair + 1) * 18 + level] = jnp.where(row8 < 4, pltpu.roll(got, 4, 0), 0.0) + shift
        return 0

    lax.fori_loop(0, 18, level_step, 0)
    for x in range(4):
        which, along = ((0, 1), (1, 0), (1, 1), (2, 0))[x]
        for y in range(4):
            pair_row, across = ((2, 1), (0, 0), (0, 1), (4, 0))[y]
            base = 32 * along + 16 * across
            at = (x * 4 + y) * 18
            table[at] = jnp.where(dz == 1, counts[which, pair_row + 1, base + 15], 0.0).astype(i32)
            table[at + 17] = jnp.where(dz == 0, counts[which, pair_row + 1, base], 0.0).astype(i32)

            def copy_count(k, _, which=which, pair_row=pair_row, base=base, at=at):
                table[at + 1 + k] = counts[which, pair_row, base + k].astype(i32)
                return 0

            lax.fori_loop(0, 16, copy_count, 0)

    def task(number, _):
        part, j, i = number & 1, (number >> 1) & 1, number >> 2
        outside = [(12 * i + j + c) * 18 + 8 * part for c in range(3)]
        outside += [(4 * x + 3 * j) * 18 + 8 * part for x in (1, 2)]
        within = [(4 * x + y) * 18 + 8 * part for x in (1, 2) for y in (1, 2)]
        own = (4 * (i + 1) + j + 1) * 18 + 8 * part + 1

        def beads(level):
            return [(near[base + level], table[base + level]) for base in outside]

        def with_inner(level, use):
            return beads(level) + [(near[base + level], table[base + level] * use) for base in within]

        def emit(n, value, raw):
            first, second = first_ref[i, j, n, 0:3], second_ref[i, j, n, 0:3]
            value = value + jnp.where(part == 0, first, second)
            for d in range(3):
                out_ref[d, i, j, pl.ds(8 * part + n, 1), :] = value[d : d + 1]

        pair_task(
            scratch,
            8,
            [(0, 1, lambda n: with_inner(n, 1 - part)), (1, 9, beads), (9, 10, lambda n: with_inner(n, part))],
            64.0 * part.astype(f32) + 40.0,
            lambda n: near[own + n],
            lambda n: table[own + n],
            lambda n: n,
            emit,
        )
        return 0

    lax.fori_loop(0, 8, task, 0)


def call(kernel, shapes, inputs, specs=None, scratch=(), flops=10**6, out_specs=None):
    single = not isinstance(shapes, (list, tuple)) or isinstance(shapes[0], int)
    shapes = [shapes] if single else shapes
    result = pl.pallas_call(
        kernel,
        out_shape=[jax.ShapeDtypeStruct(s, f32) for s in shapes],
        in_specs=specs or [VMEM] * len(inputs),
        out_specs=[VMEM] * len(shapes),
        scratch_shapes=list(scratch),
        cost_estimate=pl.CostEstimate(flops=flops, transcendentals=0, bytes_accessed=10**6),
        compiler_params=pltpu.CompilerParams(vmem_limit_bytes=40 << 20),
    )(*inputs)
    return result[0] if single else result


def move(value, axis, step):
    size = lax.axis_size(axis)
    return lax.ppermute(value, axis, [(n, n + step) for n in range(size) if 0 <= n + step < size])


def exchange(up, down, up2, down2, axis):
    return move(up, axis, 1), move(down, axis, -1), move(up2, axis, 2), move(down2, axis, -2)


def per_device(offsets, charge, counts, partners):
    z_op = jnp.asarray(np.stack([np.stack(halves(z_operator(part))) for part in range(2)]))
    fine_op, coarse_op, y_down, y_up = [jnp.asarray(m) for m in y_operators()]
    z_up = jnp.asarray(z_prolong())
    counts = counts.reshape(64)
    block = jnp.pad(counts.astype(f32)[None, :], ((0, 7), (0, 64)))
    near, rho, z_msg = call(
        spread_kernel,
        [(2, 2, 18, 8, 128), (19, 24, 256), (144, 128)],
        (offsets, charge, counts, block),
        [VMEM, VMEM, SMEM, VMEM],
    )
    z_got = lax.ppermute(z_msg, "ga", [(0, 1), (1, 0)])
    near1, full, restr, *y_msgs = call(
        along_z_kernel,
        [(2, 2, 18, 8, 128), (19, 24, 256), (19, 16, 128), (760, 128), (760, 128), (152, 128), (152, 128)],
        (near, rho, z_msg, z_got, z_op, y_down),
    )
    y_got = exchange(*y_msgs, "gy")
    inner = lambda part, near_in, after: call(
        lambda *refs: inner_pairs_kernel(part, *refs),
        (2, 2, 8, 8, 128),
        (near_in.reshape(72, 8, 128), counts, partners, after),
        [VMEM, SMEM, VMEM, ANY],
        [pltpu.SMEM((72,), i32)] + pair_scratch(32, 40 + TILES + 16),
        flops=10**9,
    )
    first = inner(0, near, full)
    near2, fine2, _, *x_msgs = call(
        along_y_kernel,
        [(2, 4, 18, 8, 128), (19, 24, 256), (19, 16, 128), (824, 128), (824, 128), (48, 128), (48, 128)],
        (near1, full, restr, y_msgs[0], *y_got, fine_op, coarse_op, first),
        [VMEM] * 10 + [ANY],
    )
    x_got = exchange(*x_msgs, "gx")
    second = inner(1, near, fine2)
    phi = call(
        along_x_kernel,
        (19, 24, 256),
        (fine2, x_msgs[0], x_msgs[1], *x_got, y_up, z_up, second),
        [VMEM] * 9 + [ANY],
        [pltpu.VMEM((35, 24, 256), f32), pltpu.VMEM((19, 24, 256), f32), pltpu.VMEM((27, 16, 128), f32)],
    )
    short_force = call(
        outer_pairs_kernel,
        (3, 2, 2, 16, 128),
        (near2, x_msgs[0], x_got[0], x_got[1], first, second),
        None,
        [
            pltpu.VMEM((288, 8, 128), f32),
            pltpu.SMEM((3, 8, 128), f32),
            pltpu.SMEM((288,), i32),
        ]
        + pair_scratch(8, 56 + TILES + 16),
        flops=10**9,
    )
    long_force = call(
        gather_kernel, (3, 2, 2, 16, 128), (offsets, charge, counts, phi), [VMEM, VMEM, SMEM, VMEM]
    )
    return short_force, long_force


def solution(mesh):
    return jax.shard_map(
        per_device,
        mesh=mesh,
        in_specs=(
            P(None, "gx", "gy", "ga", None),
            P("gx", "gy", "ga", None),
            P("gx", "gy", "ga"),
            P("gx", "gy", "ga", None),
        ),
        out_specs=(P(None, "gx", "gy", "ga", None), P(None, "gx", "gy", "ga", None)),
        check_vma=False,
    )
```

```python
import jax
import jax.numpy as jnp
import numpy as np
from jax import lax
from jax.experimental import pallas as pl
from jax.experimental.pallas import tpu as pltpu
from jax.sharding import PartitionSpec as P

f32, bf16, i32 = jnp.float32, jnp.bfloat16, jnp.int32
LAST = (((1,), (1,)), ((), ()))
CAP = 65.0 / 64.0
TILES = 2
INNER, OUTER = (128, 4, 4), (64, 8, 1)
VMEM = pl.BlockSpec(memory_space=pltpu.VMEM)
SMEM = pl.BlockSpec(memory_space=pltpu.SMEM)
ANY = pl.BlockSpec(memory_space=pl.ANY)


def fine_kernel(gap):
    return np.where(np.abs(gap) <= 8, np.exp(-gap * gap / 12.5), 0.0)


def coarse_kernel(gap):
    return np.where(np.abs(gap) <= 8, np.exp(-gap * gap / 72.0), 0.0)


def hat(gap):
    return np.where(gap == 0, 1.0, np.where(np.abs(gap) == 1, 0.5, 0.0))


def halves(matrix):
    high = matrix.astype(np.float32).astype(jnp.bfloat16)
    low = (matrix - high.astype(np.float64)).astype(np.float32).astype(jnp.bfloat16)
    return high, low


def z_operator(part):
    source = np.full(256, 10**6, np.int64)
    source[:131] = 128 * part - 1 + np.arange(131)
    source[160:181] = np.arange(21) + (127 if part == 0 else 109)
    inside = (source >= 0) & (source < 256)
    result = np.zeros((256, 256))
    target = 128 * part - 1 + np.arange(131)
    fine = fine_kernel((target[None, :] - source[:, None]).astype(np.float64))
    result[:, :131] = fine * ((target >= 0) & (target < 256))[None, :]
    middle = np.arange(128)
    down = hat((source[:, None] - 2 * middle[None, :]).astype(np.float64))
    point = 64 * part - 1 + np.arange(67)
    spread = coarse_kernel((middle[:, None] - point[None, :]).astype(np.float64))
    spread = spread * ((point >= 0) & (point < 128))[None, :]
    result[:, 136:203] = down @ spread
    return result * inside[:, None]


def y_operators():
    own = np.where(np.arange(24) < 19, np.arange(24), 10**6)
    below = np.where(np.arange(16) < 11, np.arange(16) - 8, 10**6)
    above = np.where(np.arange(16) < 11, np.arange(16) + 16, 10**6)
    source = np.concatenate([own, below, above]).astype(np.float64)
    fine = fine_kernel(np.arange(24)[:, None] - source[None, :])
    fine[19:] = 0
    own = np.where(np.arange(16) < 11, np.arange(16), 10**6)
    below = np.where(np.arange(16) < 11, np.arange(16) - 8, 10**6)
    above = np.where(np.arange(16) < 11, np.arange(16) + 8, 10**6)
    far_below = np.where(np.arange(8) < 3, np.arange(8) - 8, 10**6)
    far_above = np.where(np.arange(8) < 3, np.arange(8) + 16, 10**6)
    source = np.concatenate([own, below, above, far_below, far_above]).astype(np.float64)
    coarse = coarse_kernel(np.arange(16)[:, None] - source[None, :])
    coarse[11:] = 0
    down = hat(np.arange(24)[None, :] - (2.0 * np.arange(16)[:, None] - 1))
    down[11:] = 0
    up = hat(np.arange(24)[:, None] - (2.0 * np.arange(16)[None, :] - 1))
    up[19:] = 0
    up[:, 11:] = 0
    stack = lambda m: np.concatenate([halves(m)[0], halves(m)[1], halves(m)[0]], 1)
    thrice = lambda m: np.concatenate([halves(m)[0]] * 3, 1)
    return stack(fine), stack(coarse), thrice(down), thrice(up)


def z_prolong():
    result = np.zeros((128, 256))
    point = 2.0 * np.arange(67) - 1
    result[8:75, :131] = hat(np.arange(131)[None, :] - point[:, None])
    return halves(result)[0]


def split2(value):
    high = value.astype(bf16)
    return high, (value - high.astype(f32)).astype(bf16)


def split3(value):
    high = value.astype(bf16).astype(f32)
    rest = value - high
    middle = rest.astype(bf16).astype(f32)
    return high, middle, rest - middle


def dot(left, right):
    return jnp.dot(left, right, preferred_element_type=f32)


def spline(shifted):
    magnitude = jnp.abs(shifted)
    margin = jnp.maximum(1.5 - magnitude, 0.0)
    return jnp.where(magnitude < 0.5, 0.75 - shifted * shifted, 0.5 * margin * margin)


def spline_slope(shifted):
    magnitude = jnp.abs(shifted)
    margin = jnp.maximum(1.5 - magnitude, 0.0)
    return jnp.where(magnitude < 0.5, -2.0 * shifted, jnp.where(shifted > 0.0, -margin, margin))


def weights_at(offset, rows, first):
    points = lax.broadcasted_iota(i32, (rows, 128), 0).astype(f32)
    return 8.0 * offset + (1.0 + first) - points


def inside_mask(shape, dim, start, count):
    point = lax.broadcasted_iota(i32, shape, dim) + start
    return ((point >= 0) & (point < count)).astype(f32)


def spread_kernel(off_ref, charge_ref, counts_ref, block_ref, near_ref, rho_ref, msg_ref):
    dx, dy, dz = lax.axis_index("gx"), lax.axis_index("gy"), lax.axis_index("ga")
    lane = lax.broadcasted_iota(i32, (1, 128), 1)
    row8 = lax.broadcasted_iota(i32, (8, 128), 0)
    rho_ref[...] = jnp.zeros((19, 24, 256), f32)
    zero8 = jnp.zeros((8, 128), f32)
    for i in range(2):
        for j in range(2):
            near_ref[i, j, 0] = zero8
            near_ref[i, j, 17] = zero8

    def column(ij, _):
        i, j = ij >> 1, ij & 1
        shift_x = 8.0 * (i + 1).astype(f32)
        shift_y = 8.0 * (j + 1).astype(f32)
        total = jnp.zeros((176, 128), f32)
        tail = None
        for m in range(8):
            highs, lows, z_highs, z_lows = [], [], [], []
            for half in range(2):
                k = 2 * m + half
                ox = off_ref[0, i, j, k : k + 1]
                oy = off_ref[1, i, j, k : k + 1]
                oz = off_ref[2, i, j, k : k + 1]
                count = counts_ref[ij * 16 + k]
                weighted = jnp.where(lane < count, charge_ref[i, j, k : k + 1], 0.0)
                near_ref[i, j, k + 1] = jnp.concatenate(
                    [8.0 * ox + shift_x, 8.0 * oy + shift_y, 8.0 * oz + 8.0 * (k + 1), weighted, zero8[:4]], 0
                )
                wx = spline(weights_at(ox, 16, 0)) * weighted
                wy = spline(weights_at(oy, 16, 0))
                wz = spline(weights_at(oz, 32, 8 * half))
                plane = jnp.concatenate([wx[a : a + 1] * wy for a in range(11)], 0)
                high, low = split2(plane)
                highs.append(high)
                lows.append(low)
                z_high, z_low = split2(wz)
                z_highs.append(z_high)
                z_lows.append(z_low)
            left = jnp.concatenate(highs + lows + highs, 1)
            right = jnp.concatenate(z_highs + z_highs + z_lows, 1)
            if m < 7:
                pieces = [right]
                if m > 0:
                    pieces = [jnp.zeros((16 * m, 768), bf16)] + pieces
                if m < 6:
                    pieces = pieces + [jnp.zeros((96 - 16 * m, 768), bf16)]
                total = total + lax.dot_general(left, jnp.concatenate(pieces, 0), LAST, preferred_element_type=f32)
            else:
                wide = jnp.concatenate([jnp.zeros((112, 768), bf16), right, jnp.zeros((112, 768), bf16)], 0)
                both = lax.dot_general(left, wide, LAST, preferred_element_type=f32)
                total = total + both[:, :128]
                tail = both[:, 128:]
        first = pl.multiple_of(8 * j, 8)
        for a in range(11):
            rho_ref[8 * i + a, pl.ds(first, 16), 0:128] += total[16 * a : 16 * a + 16]
            rho_ref[8 * i + a, pl.ds(first, 16), 128:256] += tail[16 * a : 16 * a + 16]
        return 0

    lax.fori_loop(0, 4, column, 0)
    mask_y = inside_mask((24, 256), 0, 16 * dy - 1, 128)
    mask_z = inside_mask((24, 256), 1, 128 * dz - 1, 256)
    mask = mask_y * mask_z
    wide_lane = lax.broadcasted_iota(i32, (24, 128), 1)
    msg_ref[0:8] = block_ref[...]
    for i in range(2):
        picked = [jnp.where(dz == 0, near_ref[i, j, 16], near_ref[i, j, 1]) for j in range(2)]
        msg_ref[8 + 8 * i : 16 + 8 * i] = jnp.where(row8 < 4, picked[0], pltpu.roll(picked[1], 4, 0))
    faces = []
    for a in range(19):
        point = 16 * dx - 1 + a
        keep = ((point >= 0) & (point < 128)).astype(f32)
        plane = rho_ref[a] * (mask * keep)
        rho_ref[a] = plane
        low, high = plane[:, :128], plane[:, 128:]
        top = jnp.where(wide_lane < 18, pltpu.roll(low, 18, 1), pltpu.roll(high, 18, 1))
        face = jnp.where(dz == 0, top, low)
        faces.append(jnp.where(wide_lane < 21, face, 0.0))
    faces.append(jnp.zeros((24, 128), f32))
    for p in range(5):
        packed = faces[p]
        for g in range(1, 4):
            packed = packed + pltpu.roll(faces[5 * g + p], 32 * g, 1)
        msg_ref[24 + 24 * p : 48 + 24 * p] = packed


def along_z_kernel(near_ref, rho_ref, own_msg_ref, got_ref, op_ref, down_ref,
                   near1_ref, full_ref, restr_ref, up_ref, dn_ref, up2_ref, dn2_ref):
    dy, dz = lax.axis_index("gy"), lax.axis_index("ga")
    row8 = lax.broadcasted_iota(i32, (8, 128), 0)
    shift = jnp.where(row8 == 2, jnp.where(dz == 0, 128.0, -128.0), 0.0)
    for i in range(2):
        got = got_ref[8 + 8 * i : 16 + 8 * i]
        parts = [jnp.where(row8 < 4, got, 0.0), jnp.where(row8 < 4, pltpu.roll(got, 4, 0), 0.0)]
        for j in range(2):
            near1_ref[i, j, 1:17] = near_ref[i, j, 1:17]
            moved = parts[j] + shift
            near1_ref[i, j, 0] = jnp.where(dz == 1, moved, 0.0)
            near1_ref[i, j, 17] = jnp.where(dz == 0, moved, 0.0)
    lane = lax.broadcasted_iota(i32, (24, 128), 1)
    high_op, low_op = op_ref[dz, 0], op_ref[dz, 1]
    down = down_ref[...]
    lane16 = lax.broadcasted_iota(i32, (16, 128), 1)
    keep = inside_mask((16, 128), 0, 8 * dy - 1, 64)
    for g in range(4):
        planes = range(5 * g, min(5 * g + 5, 19))
        stacked = []
        for p, a in enumerate(planes):
            face = pltpu.roll(got_ref[24 + 24 * p : 48 + 24 * p], (32 - 32 * g) % 128, 1)
            second = jnp.where((lane >= 32) & (lane < 64), face, rho_ref[a, :, 128:256])
            stacked.append(jnp.concatenate([rho_ref[a, :, 0:128], second], 1))
        high, low = split2(jnp.concatenate(stacked, 0))
        result = dot(high, high_op) + dot(low, high_op) + dot(high, low_op)
        for p, a in enumerate(planes):
            plane = result[24 * p : 24 * p + 24]
            full_ref[a] = plane
            h, m, l = split3(plane[:, 128:256])
            restricted = dot(down, jnp.concatenate([h, m, l], 0).astype(bf16)) * keep
            restr_ref[a] = restricted
            for out, first in ((up_ref, 8), (dn_ref, 0)):
                out[152 + 16 * a : 168 + 16 * a] = plane[first : first + 16, 0:128]
                out[456 + 16 * a : 472 + 16 * a] = jnp.where(
                    lane16 < 8, plane[first : first + 16, 128:256], restricted
                )
            up2_ref[8 * a : 8 * a + 8] = restricted[8:16]
            dn2_ref[8 * a : 8 * a + 8] = restricted[0:8]
    counts = jnp.where(row8 == 0, own_msg_ref[0:8], jnp.where(row8 == 1, pltpu.roll(got_ref[0:8], 1, 0), 0.0))
    for out, j in ((up_ref, 1), (dn_ref, 0)):
        out[0:8] = counts
        for level in range(18):
            out[8 + 8 * level : 16 + 8 * level] = jnp.where(
                row8 < 4, near1_ref[0, j, level], pltpu.roll(near1_ref[1, j, level], 4, 0)
            )


def along_y_kernel(near1_ref, full_ref, restr_ref, up_own_ref, below_ref, above_ref, below2_ref, above2_ref,
                   fine_ref, coarse_ref, after_ref, near2_ref, fine2_ref, coarse2_ref,
                   up_ref, dn_ref, up2_ref, dn2_ref):
    dx, dy = lax.axis_index("gx"), lax.axis_index("gy")
    row8 = lax.broadcasted_iota(i32, (8, 128), 0)
    keep = inside_mask((16, 128), 0, 8 * dy - 1, 64)
    lane16 = lax.broadcasted_iota(i32, (16, 128), 1)
    lane24 = lax.broadcasted_iota(i32, (24, 128), 1)
    fine_op, coarse_op = fine_ref[...], coarse_ref[...]

    def plane(a, _):
        at = pl.multiple_of(16 * a, 16)
        at8 = pl.multiple_of(8 * a, 8)
        below_low = below_ref[pl.ds(152 + at, 16)]
        below_high = below_ref[pl.ds(456 + at, 16)]
        above_low = above_ref[pl.ds(152 + at, 16)]
        above_high = above_ref[pl.ds(456 + at, 16)]
        stack = jnp.concatenate(
            [
                full_ref[a],
                jnp.concatenate([below_low, below_high], 1),
                jnp.concatenate([above_low, above_high], 1),
            ],
            0,
        )
        high, low = split3(stack)[:2]
        fine2_ref[a] = dot(fine_op, jnp.concatenate([high, high, low], 0).astype(bf16))
        stack = jnp.concatenate(
            [restr_ref[a], below_high, above_high, below2_ref[pl.ds(at8, 8)], above2_ref[pl.ds(at8, 8)]], 0
        )
        high, low = split3(stack)[:2]
        coarse2_ref[a] = dot(coarse_op, jnp.concatenate([high, high, low], 0).astype(bf16)) * keep
        return 0

    lax.fori_loop(0, 19, plane, 0)
    restricted = []
    for e in range(11):
        value = None
        for a, weight in ((2 * e - 2, 0.5), (2 * e - 1, 1.0), (2 * e, 0.5)):
            if 0 <= a < 19:
                term = coarse2_ref[a] * weight
                value = term if value is None else value + term
        point = 8 * dx - 1 + e
        restricted.append(value * ((point >= 0) & (point < 64)).astype(f32))
    blank = jnp.zeros((8, 128), f32)
    for out, first in ((up_ref, 8), (dn_ref, 0)):
        for n in range(11):
            plane_value = fine2_ref[first + n]
            out[296 + 24 * n : 320 + 24 * n] = plane_value[:, 0:128]
            out[560 + 24 * n : 584 + 24 * n] = jnp.where(
                lane24 < 8, plane_value[:, 128:256], jnp.concatenate([restricted[n], blank], 0)
            )
    for n in range(3):
        up2_ref[16 * n : 16 * n + 16] = restricted[8 + n]
        dn2_ref[16 * n : 16 * n + 16] = restricted[n]
    shift_down = jnp.where(row8 == 1, -16.0, 0.0)
    shift_up = jnp.where(row8 == 1, 16.0, 0.0)
    for level in range(18):
        for y, source, shift in ((0, below_ref, shift_down), (3, above_ref, shift_up)):
            got = source[8 + 8 * level : 16 + 8 * level]
            near2_ref[0, y, level] = jnp.where(row8 < 4, got, 0.0) + shift
            near2_ref[1, y, level] = jnp.where(row8 < 4, pltpu.roll(got, 4, 0), 0.0) + shift
        for x in range(2):
            for y in range(2):
                near2_ref[x, y + 1, level] = near1_ref[x, y, level]
    counts = jnp.where(row8 < 2, up_own_ref[0:8], 0.0)
    counts = jnp.where((row8 >= 2) & (row8 < 4), pltpu.roll(below_ref[0:8], 2, 0), counts)
    counts = jnp.where((row8 >= 4) & (row8 < 6), pltpu.roll(above_ref[0:8], 4, 0), counts)
    for out, x in ((up_ref, 1), (dn_ref, 0)):
        out[0:8] = counts
        for level in range(18):
            for pair in range(2):
                at = 8 + 8 * (2 * level + pair)
                out[at : at + 8] = jnp.where(
                    row8 < 4, near2_ref[x, 2 * pair, level], pltpu.roll(near2_ref[x, 2 * pair + 1, level], 4, 0)
                )


def along_x_kernel(fine2_ref, up_own_ref, dn_own_ref, below_ref, above_ref, below2_ref, above2_ref,
                   up_y_ref, up_z_ref, after_ref, phi_ref, source, third, coarse):
    dx, dy, dz = lax.axis_index("gx"), lax.axis_index("gy"), lax.axis_index("ga")
    for p in range(35):
        rel = p - 8
        low = high = None
        pieces = []
        if 0 <= rel < 19:
            pieces.append((fine2_ref[rel, :, 0:128], fine2_ref[rel, :, 128:256]))
        if rel <= 2:
            n = rel + 8
            pieces.append((below_ref[296 + 24 * n : 320 + 24 * n], below_ref[560 + 24 * n : 584 + 24 * n]))
        if rel >= 16:
            n = rel - 16
            pieces.append((above_ref[296 + 24 * n : 320 + 24 * n], above_ref[560 + 24 * n : 584 + 24 * n]))
        for low_piece, high_piece in pieces:
            low = low_piece if low is None else low + low_piece
            high = high_piece if high is None else high + high_piece
        source[p, :, 0:128] = low
        source[p, :, 128:256] = high
    fine_weights = [float(w) for w in fine_kernel(np.arange(9.0))]
    coarse_weights = [float(w) for w in coarse_kernel(np.arange(9.0))]

    def fine_plane(a, _):
        value = source[a + 8] * (4.0 * fine_weights[0])
        for d in range(1, 9):
            value = value + (source[a + 8 - d] + source[a + 8 + d]) * (4.0 * fine_weights[d])
        third[a] = value
        return 0

    lax.fori_loop(0, 19, fine_plane, 0)

    def own_coarse(e):
        ref, n = (up_own_ref, e)
        return ref[560 + 24 * n : 576 + 24 * n]

    for p in range(27):
        rel = p - 8
        value = None
        pieces = []
        if 0 <= rel < 11:
            pieces.append(own_coarse(rel))
        if rel <= 2:
            n = rel + 8
            pieces.append(below_ref[560 + 24 * n : 576 + 24 * n])
        if rel >= 8:
            n = rel - 8
            pieces.append(above_ref[560 + 24 * n : 576 + 24 * n])
        if rel <= -6:
            n = rel + 8
            pieces.append(below2_ref[16 * n : 16 * n + 16])
        if rel >= 16:
            n = rel - 16
            pieces.append(above2_ref[16 * n : 16 * n + 16])
        for piece in pieces:
            value = piece if value is None else value + piece
        coarse[p] = value
    lifted = []
    up_y, up_z = up_y_ref[...], up_z_ref[...]
    for e in range(11):
        value = coarse[e + 8] * (2.0 * coarse_weights[0])
        for d in range(1, 9):
            value = value + (coarse[e + 8 - d] + coarse[e + 8 + d]) * (2.0 * coarse_weights[d])
        point = 8 * dx - 1 + e
        value = value * ((point >= 0) & (point < 64)).astype(f32)
        h, m, l = split3(value)
        tall = dot(up_y, jnp.concatenate([h, m, l], 0).astype(bf16))
        h, m, l = split3(tall)
        stacked = jnp.concatenate([h, m, l], 0).astype(bf16)
        wide = dot(stacked, up_z)
        lifted.append(wide[0:24] + wide[24:48] + wide[48:72])
    mask = inside_mask((24, 256), 0, 16 * dy - 1, 128) * inside_mask((24, 256), 1, 128 * dz - 1, 256)
    lane = lax.broadcasted_iota(i32, (24, 256), 1)
    mask = jnp.where(lane < 131, mask, 0.0)
    for a in range(19):
        if a % 2:
            value = lifted[(a + 1) // 2]
        else:
            value = 0.5 * (lifted[a // 2] + lifted[a // 2 + 1])
        point = 16 * dx - 1 + a
        keep = mask * ((point >= 0) & (point < 128)).astype(f32)
        phi_ref[a] = jnp.where(keep > 0.0, third[a] + value, 0.0)


def gather_kernel(off_ref, charge_ref, counts_ref, phi_ref, out_ref):
    lane = lax.broadcasted_iota(i32, (1, 128), 1)
    lane176 = lax.broadcasted_iota(i32, (176, 128), 1)

    def column(ij, _):
        i, j = ij >> 1, ij & 1
        first = pl.multiple_of(8 * j, 8)
        low = jnp.concatenate([phi_ref[8 * i + a, pl.ds(first, 16), 0:128] for a in range(11)], 0)
        high = jnp.concatenate([phi_ref[8 * i + a, pl.ds(first, 16), 128:256] for a in range(11)], 0)
        for m in range(8):
            window = pltpu.roll(low, (128 - 16 * m) % 128, 1) if m else low
            if m == 7:
                window = jnp.where(lane176 < 16, window, pltpu.roll(high, 16, 1))
            window = jnp.where(lane176 < 32, window, 0.0)
            part_h = window.astype(bf16).astype(f32)
            part_m = window - part_h
            left = (part_h + pltpu.roll(part_m, 32, 1) + pltpu.roll(part_h, 64, 1)).astype(bf16)
            stacks, slopes, sides = [], [], []
            for half in range(2):
                k = 2 * m + half
                ox = off_ref[0, i, j, k : k + 1]
                oy = off_ref[1, i, j, k : k + 1]
                oz = off_ref[2, i, j, k : k + 1]
                count = counts_ref[ij * 16 + k]
                weighted = jnp.where(lane < count, charge_ref[i, j, k : k + 1], 0.0)
                shifted = weights_at(oz, 32, 8 * half)
                for bag, value in ((stacks, spline(shifted)), (slopes, spline_slope(shifted))):
                    high_part, low_part = split2(value)
                    bag.append(jnp.concatenate([high_part, high_part, low_part, jnp.zeros((32, 128), bf16)], 0))
                sides.append((ox, oy, weighted))
            right = jnp.concatenate(stacks + slopes, 1)
            product = dot(left, right)
            for half in range(2):
                k = 2 * m + half
                ox, oy, weighted = sides[half]
                level = product[:, 128 * half : 128 * half + 128]
                rising = product[:, 256 + 128 * half : 384 + 128 * half]
                sx = weights_at(ox, 16, 0)
                sy = weights_at(oy, 16, 0)
                wx, gx = spline(sx), spline_slope(sx)
                wy, gy = spline(sy), spline_slope(sy)
                along = across = up = None
                for a in range(11):
                    piece = level[16 * a : 16 * a + 16]
                    rise = rising[16 * a : 16 * a + 16]
                    terms = (gx[a : a + 1] * piece, wx[a : a + 1] * piece, wx[a : a + 1] * rise)
                    if a == 0:
                        along, across, up = terms
                    else:
                        along, across, up = along + terms[0], across + terms[1], up + terms[2]
                force_x = jnp.sum(along * wy, axis=0, keepdims=True)
                force_y = jnp.sum(across * gy, axis=0, keepdims=True)
                force_z = jnp.sum(up * wy, axis=0, keepdims=True)
                out_ref[0, i, j, k : k + 1] = -weighted * force_x
                out_ref[1, i, j, k : k + 1] = -weighted * force_y
                out_ref[2, i, j, k : k + 1] = -weighted * force_z
        return 0

    lax.fori_loop(0, 4, column, 0)


def pair_scratch(form, cells, tiles):
    rows, slots, share = form
    sets = cells // share
    return (
        [
            pltpu.VMEM((tiles, 8, 128), f32),
            pltpu.VMEM((tiles, 48, 128), bf16),
            pltpu.VMEM((tiles, 16, 128), bf16),
            pltpu.VMEM((sets + 1, share * 128, 128), f32),
            pltpu.VMEM(((sets + 1) * (share * 128 // rows), 16, 128), f32),
        ]
        + [
            pltpu.VMEM((rows, TILES * 128), f32),
            pltpu.VMEM((rows, TILES * 128), bf16),
            pltpu.VMEM((rows, TILES * 128), bf16),
        ]
        * slots
        + [pltpu.SMEM((128,), i32), pltpu.SMEM((cells,), i32)]
        + [pltpu.SMEM((sets + 1,), i32)] * 3
    )


def middle_of(center):
    row = lax.broadcasted_iota(i32, (8, 128), 0)
    return jnp.where(row < 2, 16.0, jnp.where(row == 2, center, 0.0))


def pack_list(packed, start, base, tile, levels, center):
    lane = lax.broadcasted_iota(i32, (8, 128), 1)
    middle = middle_of(center)
    end, current = tile * 128, jnp.zeros((8, 128), f32)
    for level, beads in enumerate(levels):
        start[base + level] = end
        for value, count in beads:
            within, tile = end & 127, end >> 7
            turned = pltpu.roll(value - middle, within, 1)
            keep = lane < within
            current = jnp.where(keep, current, turned)
            packed[tile] = current
            end = end + count
            current = jnp.where((end >> 7) > tile, jnp.where(keep, turned, 0.0), current)
    start[base + 10] = end
    packed[end >> 7] = jnp.where(lane < (end & 127), current, 0.0)
    for e in range(1, TILES):
        packed[(end >> 7) + e] = jnp.zeros((8, 128), f32)
    return (end >> 7) + TILES


def pair_sums(scratch, form, cells, used, own_pos, own_count, own_start, own_center, emit):
    packed, features, sources, own_features, sums = scratch[:5]
    start, row_at, first_tile, groups_of, blocks_of = scratch[-5:]
    height, flight, share = form
    sets = cells // share
    slots = [scratch[5 + 3 * e : 8 + 3 * e] for e in range(flight)]
    blocks = share * 128 // height
    lane = lax.broadcasted_iota(i32, (16, 128), 1)
    row = lax.broadcasted_iota(i32, (8, 128), 0)
    for e in range(8):
        packed[used + e] = jnp.zeros((8, 128), f32)

    def near_step(step, _):
        for e in range(8):
            tile = 8 * step + e
            value = packed[tile]
            norm = value[0:1] * value[0:1] + value[1:2] * value[1:2] + value[2:3] * value[2:3]
            vector = jnp.where(row < 3, value, jnp.where(row == 3, norm, jnp.where(row == 4, 1.0, 0.0)))
            h, m, l = split3(vector)
            features[tile] = jnp.concatenate([h, h, m, m, h, l], 0).astype(bf16)
            charge = value[3:4]
            vector = jnp.where(row < 3, value * charge, jnp.where(row == 3, charge, 0.0))
            h, m, l = split3(vector)
            sources[tile] = jnp.concatenate(
                [jnp.where(row < 4, h, pltpu.roll(m, 4, 0)), jnp.where(row < 4, l, 0.0)], 0
            ).astype(bf16)
        return 0

    lax.fori_loop(0, (used + 7) // 8, near_step, 0)

    def own_one(n, which, at):
        value = own_pos(n) - middle_of(own_center(n))
        norm = value[0:1] * value[0:1] + value[1:2] * value[1:2] + value[2:3] * value[2:3]
        vector = jnp.where(
            row < 3,
            value * (2.0 / 64),
            jnp.where(row == 3, -1.0 / 64, jnp.where(row == 4, 1.0 - norm * (1.0 / 64), 0.0)),
        )
        h, m, l = split3(vector)
        stacked = jnp.concatenate([h, m, h, m, l, h, jnp.zeros((80, 128), f32)], 0)
        own_features[which, pl.ds(pl.multiple_of(at, 8), 128), :] = jnp.transpose(stacked)
        row_at[n] = at
        return at + ((own_count(n) + 7) >> 3) * 8

    def own_step(step, total):
        for e in range(8 // share):
            which = step * (8 // share) + e
            at = i32(0)
            for c in range(share):
                at = own_one(c * sets + which, which, at)
            for b in range(blocks):
                sums[which * blocks + b] = jnp.zeros((16, 128), f32)
            level = own_start(which)
            begin, stop = start[level], start[level + 3]
            tile = begin >> 7
            groups = jnp.maximum((((stop + 127) >> 7) - tile + TILES - 1) // TILES, 1)
            rows = (at + height - 1) // height
            first_tile[which], groups_of[which], blocks_of[which] = tile, groups, rows
            total = total + groups * rows
        return total

    total = lax.fori_loop(0, cells // 8, own_step, i32(0))
    own_features[sets] = jnp.zeros((share * 128, 128), f32)
    for e in range(blocks):
        sums[sets * blocks + e] = jnp.zeros((16, 128), f32)
    first_tile[sets], groups_of[sets], blocks_of[sets] = i32(0), i32(1), i32(1)
    for distance, high, low in slots:
        distance[...] = jnp.zeros((height, TILES * 128), f32)
        high[...] = jnp.zeros((height, TILES * 128), bf16)
        low[...] = jnp.zeros((height, TILES * 128), bf16)

    def item(_, state):
        cell, block, group = state[:3]
        older, oldest = state[3 : 3 + 2 * flight], state[3 + 2 * flight :]
        added, shares, fresh, tags = [], [], [], []
        for e in range(flight):
            distance, high, low = slots[e]
            tile = oldest[2 * e + 1]
            source = jnp.concatenate([sources[tile + s] for s in range(TILES)], 1)
            added.append(
                lax.dot_general(
                    jnp.concatenate([source, source], 1),
                    jnp.concatenate([high[...], low[...]], 1),
                    LAST,
                    preferred_element_type=f32,
                )
            )
            reach = distance[...]
            kept = jnp.maximum(reach, 0.0)
            strength = (kept * kept * kept) / (CAP - reach)
            shares.append(split2(strength))
            groups, rows = groups_of[cell], blocks_of[cell]
            tile = first_tile[cell] + group * TILES
            at = pl.multiple_of(block * height, height)
            left = own_features[cell, pl.ds(at, height), 0:48].astype(bf16)
            right = jnp.concatenate([features[tile + s] for s in range(TILES)], 1)
            fresh.append(dot(left, right))
            tags += [cell * blocks + block, tile]
            group = group + 1
            wrap = (group >= groups).astype(i32)
            group = group * (1 - wrap)
            block = block + wrap
            wrap = (block >= rows).astype(i32)
            block = block * (1 - wrap)
            cell = jnp.minimum(cell + wrap, sets)
        for e in range(flight):
            distance, high, low = slots[e]
            where = oldest[2 * e]
            sums[where, :, 0:height] = sums[where, :, 0:height] + added[e]
            high[...], low[...] = shares[e]
            distance[...] = fresh[e]
        return (cell, block, group) + tuple(tags) + tuple(older)

    spare = (i32(sets * blocks), i32(0))
    lax.fori_loop(0, (total + flight - 1) // flight + 2, item, (i32(0),) * 3 + spare * (2 * flight))

    def finish_one(n):
        if share == 1:
            parts = [sums[n * blocks + e, :, 0:height] for e in range(blocks)]
            whole = jnp.concatenate(parts, 1) if blocks > 1 else parts[0]
        else:
            at = row_at[n]
            block, within = (n % sets) * blocks + (at >> 7), at & 127
            back = (128 - within) & 127
            whole = jnp.where(
                lane < 128 - within, pltpu.roll(sums[block], back, 1), pltpu.roll(sums[block + 1], back, 1)
            )
        whole = whole[0:4] + whole[4:8] + whole[8:12]
        raw = own_pos(n)
        value = raw - middle_of(own_center(n))
        emit(n, (value[0:3] * whole[3:4] - whole[0:3]) * (raw[3:4] * (1.0 / 64)), raw)

    def finish(step, _):
        for e in range(4):
            finish_one(4 * step + e)
        return 0

    lax.fori_loop(0, cells // 4, finish, 0)


def inner_pairs_kernel(part, near_ref, counts_ref, partners_ref, after_ref, out_ref, table, *scratch):
    lane = lax.broadcasted_iota(i32, (1, 128), 1)
    for column in range(4):
        table[18 * column] = i32(0)
        table[18 * column + 17] = i32(0)

    def copy_count(k, _):
        for column in range(4):
            table[18 * column + 1 + k] = counts_ref[16 * column + k]
        return 0

    lax.fori_loop(0, 16, copy_count, 0)

    levels = [[(near_ref[18 * c + 8 * part + n], table[18 * c + 8 * part + n]) for c in range(4)] for n in range(10)]
    used = pack_list(scratch[0], scratch[-5], 0, i32(0), levels, 64.0 * part + 40.0)

    def cell_at(n):
        return (n >> 3) * 18 + (n & 7) + (8 * part + 1)

    def emit(n, value, raw):
        x, y, k = n >> 4, (n >> 3) & 1, 8 * part + (n & 7)
        count = table[cell_at(n)]
        partner = partners_ref[x, y, pl.ds(k, 1), :]
        other = jnp.take_along_axis(raw, jnp.broadcast_to(partner, (8, 128)), axis=1)
        both = (lane < count) & (partner < count)
        out_ref[x, y, n & 7, 0:3] = value + jnp.where(both, -0.1 * (raw[0:3] - other[0:3]), 0.0)

    pair_sums(
        scratch,
        INNER,
        32,
        used,
        lambda n: near_ref[cell_at(n)],
        lambda n: table[cell_at(n)],
        lambda n: n & 7,
        lambda n: 64.0 * part + 40.0,
        emit,
    )


def outer_pairs_kernel(near2_ref, own_msg_ref, below_ref, above_ref, first_ref, second_ref, out_ref,
                       near, counts, table, *scratch):
    dz = lax.axis_index("ga")
    row8 = lax.broadcasted_iota(i32, (8, 128), 0)
    for n, source in enumerate((below_ref, own_msg_ref, above_ref)):
        pltpu.sync_copy(source.at[0:8], counts.at[n])
    below_shift = jnp.where(row8 == 0, -16.0, 0.0)
    above_shift = jnp.where(row8 == 0, 16.0, 0.0)

    def level_step(level, _):
        for x in range(2):
            for y in range(4):
                near[(4 * x + 4 + y) * 18 + level] = near2_ref[x, y, level]
        for x, source, shift in ((0, below_ref, below_shift), (3, above_ref, above_shift)):
            for pair in range(2):
                at = pl.multiple_of(8 + 8 * (2 * level + pair), 8)
                got = source[pl.ds(at, 8)]
                near[(4 * x + 2 * pair) * 18 + level] = jnp.where(row8 < 4, got, 0.0) + shift
                near[(4 * x + 2 * pair + 1) * 18 + level] = jnp.where(row8 < 4, pltpu.roll(got, 4, 0), 0.0) + shift
        return 0

    lax.fori_loop(0, 18, level_step, 0)
    for x in range(4):
        which, along = ((0, 1), (1, 0), (1, 1), (2, 0))[x]
        for y in range(4):
            pair_row, across = ((2, 1), (0, 0), (0, 1), (4, 0))[y]
            base = 32 * along + 16 * across
            at = (x * 4 + y) * 18
            table[at] = jnp.where(dz == 1, counts[which, pair_row + 1, base + 15], 0.0).astype(i32)
            table[at + 17] = jnp.where(dz == 0, counts[which, pair_row + 1, base], 0.0).astype(i32)

            def copy_count(k, _, which=which, pair_row=pair_row, base=base, at=at):
                table[at + 1 + k] = counts[which, pair_row, base + k].astype(i32)
                return 0

            lax.fori_loop(0, 16, copy_count, 0)

    def split(number):
        return number >> 2, (number >> 1) & 1, number & 1

    def one_list(number, tile):
        i, j, part = split(number)
        outside = [(12 * i + j + c) * 18 + 8 * part for c in range(3)]
        outside += [(4 * x + 3 * j) * 18 + 8 * part for x in (1, 2)]
        within = [(4 * x + y) * 18 + 8 * part for x in (1, 2) for y in (1, 2)]
        levels = []
        for level in range(10):
            beads = [(near[base + level], table[base + level]) for base in outside]
            if level in (0, 9):
                use = part if level else 1 - part
                beads += [(near[base + level], table[base + level] * use) for base in within]
            levels.append(beads)
        return pack_list(scratch[0], scratch[-5], 16 * number, tile, levels, 64.0 * part.astype(f32) + 40.0)

    used = lax.fori_loop(0, 8, one_list, i32(0))

    def own_at(n):
        i, j, part = split(n >> 3)
        return (4 * (i + 1) + j + 1) * 18 + 8 * part + 1 + (n & 7)

    def emit(n, value, raw):
        i, j, part = split(n >> 3)
        value = value + jnp.where(part == 0, first_ref[i, j, n & 7, 0:3], second_ref[i, j, n & 7, 0:3])
        for d in range(3):
            out_ref[d, i, j, pl.ds(8 * part + (n & 7), 1), :] = value[d : d + 1]

    pair_sums(
        scratch,
        OUTER,
        64,
        used,
        lambda n: near[own_at(n)],
        lambda n: table[own_at(n)],
        lambda n: 16 * (n >> 3) + (n & 7),
        lambda n: 64.0 * ((n >> 3) & 1).astype(f32) + 40.0,
        emit,
    )


def call(kernel, shapes, inputs, specs=None, scratch=(), flops=10**6, out_specs=None):
    single = not isinstance(shapes, (list, tuple)) or isinstance(shapes[0], int)
    shapes = [shapes] if single else shapes
    result = pl.pallas_call(
        kernel,
        out_shape=[jax.ShapeDtypeStruct(s, f32) for s in shapes],
        in_specs=specs or [VMEM] * len(inputs),
        out_specs=[VMEM] * len(shapes),
        scratch_shapes=list(scratch),
        cost_estimate=pl.CostEstimate(flops=flops, transcendentals=0, bytes_accessed=10**6),
        compiler_params=pltpu.CompilerParams(vmem_limit_bytes=40 << 20),
    )(*inputs)
    return result[0] if single else result


def move(value, axis, step):
    size = lax.axis_size(axis)
    return lax.ppermute(value, axis, [(n, n + step) for n in range(size) if 0 <= n + step < size])


def exchange(up, down, up2, down2, axis):
    return move(up, axis, 1), move(down, axis, -1), move(up2, axis, 2), move(down2, axis, -2)


def per_device(offsets, charge, counts, partners):
    z_op = jnp.asarray(np.stack([np.stack(halves(z_operator(part))) for part in range(2)]))
    fine_op, coarse_op, y_down, y_up = [jnp.asarray(m) for m in y_operators()]
    z_up = jnp.asarray(z_prolong())
    counts = counts.reshape(64)
    block = jnp.pad(counts.astype(f32)[None, :], ((0, 7), (0, 64)))
    near, rho, z_msg = call(
        spread_kernel,
        [(2, 2, 18, 8, 128), (19, 24, 256), (144, 128)],
        (offsets, charge, counts, block),
        [VMEM, VMEM, SMEM, VMEM],
    )
    z_got = lax.ppermute(z_msg, "ga", [(0, 1), (1, 0)])
    near1, full, restr, *y_msgs = call(
        along_z_kernel,
        [(2, 2, 18, 8, 128), (19, 24, 256), (19, 16, 128), (760, 128), (760, 128), (152, 128), (152, 128)],
        (near, rho, z_msg, z_got, z_op, y_down),
    )
    y_got = exchange(*y_msgs, "gy")
    inner = lambda part, near_in, after: call(
        lambda *refs: inner_pairs_kernel(part, *refs),
        (2, 2, 8, 8, 128),
        (near_in.reshape(72, 8, 128), counts, partners, after),
        [VMEM, SMEM, VMEM, ANY],
        [pltpu.SMEM((72,), i32)] + pair_scratch(INNER, 32, 40 + TILES + 16),
        flops=10**9,
    )
    first = inner(0, near, full)
    near2, fine2, _, *x_msgs = call(
        along_y_kernel,
        [(2, 4, 18, 8, 128), (19, 24, 256), (19, 16, 128), (824, 128), (824, 128), (48, 128), (48, 128)],
        (near1, full, restr, y_msgs[0], *y_got, fine_op, coarse_op, first),
        [VMEM] * 10 + [ANY],
    )
    x_got = exchange(*x_msgs, "gx")
    second = inner(1, near, fine2)
    phi = call(
        along_x_kernel,
        (19, 24, 256),
        (fine2, x_msgs[0], x_msgs[1], *x_got, y_up, z_up, second),
        [VMEM] * 9 + [ANY],
        [pltpu.VMEM((35, 24, 256), f32), pltpu.VMEM((19, 24, 256), f32), pltpu.VMEM((27, 16, 128), f32)],
    )
    short_force = call(
        outer_pairs_kernel,
        (3, 2, 2, 16, 128),
        (near2, x_msgs[0], x_got[0], x_got[1], first, second),
        None,
        [
            pltpu.VMEM((288, 8, 128), f32),
            pltpu.SMEM((3, 8, 128), f32),
            pltpu.SMEM((288,), i32),
        ]
        + pair_scratch(OUTER, 64, 8 * (54 + TILES) + 24),
        flops=10**9,
    )
    long_force = call(
        gather_kernel, (3, 2, 2, 16, 128), (offsets, charge, counts, phi), [VMEM, VMEM, SMEM, VMEM]
    )
    return short_force, long_force


def solution(mesh):
    return jax.shard_map(
        per_device,
        mesh=mesh,
        in_specs=(
            P(None, "gx", "gy", "ga", None),
            P("gx", "gy", "ga", None),
            P("gx", "gy", "ga"),
            P("gx", "gy", "ga", None),
        ),
        out_specs=(P(None, "gx", "gy", "ga", None), P(None, "gx", "gy", "ga", None)),
        check_vma=False,
    )
```

```python
import jax
import jax.numpy as jnp
import numpy as np
from jax import lax
from jax.experimental import pallas as pl
from jax.experimental.pallas import tpu as pltpu
from jax.sharding import PartitionSpec as P

f32, bf16, i32 = jnp.float32, jnp.bfloat16, jnp.int32
LAST = (((1,), (1,)), ((), ()))
CAP = 65.0 / 64.0
TILES = 2
INNER, OUTER = (128, 8, 4), (64, 16, 1)
VMEM = pl.BlockSpec(memory_space=pltpu.VMEM)
SMEM = pl.BlockSpec(memory_space=pltpu.SMEM)
ANY = pl.BlockSpec(memory_space=pl.ANY)


def fine_kernel(gap):
    return np.where(np.abs(gap) <= 8, np.exp(-gap * gap / 12.5), 0.0)


def coarse_kernel(gap):
    return np.where(np.abs(gap) <= 8, np.exp(-gap * gap / 72.0), 0.0)


def hat(gap):
    return np.where(gap == 0, 1.0, np.where(np.abs(gap) == 1, 0.5, 0.0))


def halves(matrix):
    high = matrix.astype(np.float32).astype(jnp.bfloat16)
    low = (matrix - high.astype(np.float64)).astype(np.float32).astype(jnp.bfloat16)
    return high, low


def z_operator(part):
    source = np.full(256, 10**6, np.int64)
    source[:131] = 128 * part - 1 + np.arange(131)
    source[160:181] = np.arange(21) + (127 if part == 0 else 109)
    inside = (source >= 0) & (source < 256)
    result = np.zeros((256, 256))
    target = 128 * part - 1 + np.arange(131)
    fine = fine_kernel((target[None, :] - source[:, None]).astype(np.float64))
    result[:, :131] = fine * ((target >= 0) & (target < 256))[None, :]
    middle = np.arange(128)
    down = hat((source[:, None] - 2 * middle[None, :]).astype(np.float64))
    point = 64 * part - 1 + np.arange(67)
    spread = coarse_kernel((middle[:, None] - point[None, :]).astype(np.float64))
    spread = spread * ((point >= 0) & (point < 128))[None, :]
    result[:, 136:203] = down @ spread
    return result * inside[:, None]


def y_operators():
    fines, coarses = [], []
    for place in range(4):
        near, far = (1 - 2 * (place & 1)), (1 - (place & 2))
        parts = [np.where(np.arange(24) < 19, np.arange(24), 10**6)]
        for side in (near, -near):
            parts.append(np.where(np.arange(16) < 11, np.arange(16) + (16 if side > 0 else -8), 10**6))
        fine = fine_kernel(np.arange(24)[:, None] - np.concatenate(parts)[None, :].astype(np.float64))
        fine[19:] = 0
        parts = [np.where(np.arange(16) < 11, np.arange(16), 10**6)]
        for side in (near, -near):
            parts.append(np.where(np.arange(16) < 11, np.arange(16) + (8 if side > 0 else -8), 10**6))
        for side in (far, -far):
            parts.append(np.where(np.arange(8) < 3, np.arange(8) + (16 if side > 0 else -8), 10**6))
        coarse = coarse_kernel(np.arange(16)[:, None] - np.concatenate(parts)[None, :].astype(np.float64))
        coarse[11:] = 0
        fines.append(fine)
        coarses.append(coarse)
    down = hat(np.arange(24)[None, :] - (2.0 * np.arange(16)[:, None] - 1))
    down[11:] = 0
    up = hat(np.arange(24)[:, None] - (2.0 * np.arange(16)[None, :] - 1))
    up[19:] = 0
    up[:, 11:] = 0
    stack = lambda m: np.concatenate([halves(m)[0], halves(m)[1], halves(m)[0]], 1)
    thrice = lambda m: np.concatenate([halves(m)[0]] * 3, 1)
    return np.stack([stack(m) for m in fines]), np.stack([stack(m) for m in coarses]), thrice(down), thrice(up)


def z_prolong():
    result = np.zeros((128, 256))
    point = 2.0 * np.arange(67) - 1
    result[8:75, :131] = hat(np.arange(131)[None, :] - point[:, None])
    return halves(result)[0]


def split2(value):
    high = value.astype(bf16)
    return high, (value - high.astype(f32)).astype(bf16)


def split3(value):
    high = value.astype(bf16).astype(f32)
    rest = value - high
    middle = rest.astype(bf16).astype(f32)
    return high, middle, rest - middle


def dot(left, right):
    return jnp.dot(left, right, preferred_element_type=f32)


def spline(shifted):
    magnitude = jnp.abs(shifted)
    margin = jnp.maximum(1.5 - magnitude, 0.0)
    return jnp.where(magnitude < 0.5, 0.75 - shifted * shifted, 0.5 * margin * margin)


def spline_slope(shifted):
    magnitude = jnp.abs(shifted)
    margin = jnp.maximum(1.5 - magnitude, 0.0)
    return jnp.where(magnitude < 0.5, -2.0 * shifted, jnp.where(shifted > 0.0, -margin, margin))


def weights_at(offset, rows, first):
    points = lax.broadcasted_iota(i32, (rows, 128), 0).astype(f32)
    return 8.0 * offset + (1.0 + first) - points


def inside_mask(shape, dim, start, count):
    point = lax.broadcasted_iota(i32, shape, dim) + start
    return ((point >= 0) & (point < count)).astype(f32)


def spread_kernel(off_ref, charge_ref, counts_ref, near_ref, rho_ref, msg_ref):
    dx, dy, dz = lax.axis_index("gx"), lax.axis_index("gy"), lax.axis_index("ga")
    lane = lax.broadcasted_iota(i32, (1, 128), 1)
    row8 = lax.broadcasted_iota(i32, (8, 128), 0)
    rho_ref[...] = jnp.zeros((19, 24, 256), f32)
    zero8 = jnp.zeros((8, 128), f32)
    for i in range(2):
        for j in range(2):
            near_ref[i, j, 0] = zero8
            near_ref[i, j, 17] = zero8

    def column(ij, _):
        i, j = ij >> 1, ij & 1
        shift_x = 8.0 * (i + 1).astype(f32)
        shift_y = 8.0 * (j + 1).astype(f32)
        total = jnp.zeros((176, 128), f32)
        tail = None
        for m in range(8):
            highs, lows, z_highs, z_lows = [], [], [], []
            for half in range(2):
                k = 2 * m + half
                ox = off_ref[0, i, j, k : k + 1]
                oy = off_ref[1, i, j, k : k + 1]
                oz = off_ref[2, i, j, k : k + 1]
                count = counts_ref[i, j, k]
                weighted = jnp.where(lane < count, charge_ref[i, j, k : k + 1], 0.0)
                near_ref[i, j, k + 1] = jnp.concatenate(
                    [8.0 * ox + shift_x, 8.0 * oy + shift_y, 8.0 * oz + 8.0 * (k + 1), weighted, zero8[:4]], 0
                )
                wx = spline(weights_at(ox, 16, 0)) * weighted
                wy = spline(weights_at(oy, 16, 0))
                wz = spline(weights_at(oz, 32, 8 * half))
                plane = jnp.concatenate([wx[a : a + 1] * wy for a in range(11)], 0)
                high, low = split2(plane)
                highs.append(high)
                lows.append(low)
                z_high, z_low = split2(wz)
                z_highs.append(z_high)
                z_lows.append(z_low)
            left = jnp.concatenate(highs + lows + highs, 1)
            right = jnp.concatenate(z_highs + z_highs + z_lows, 1)
            if m < 7:
                pieces = [right]
                if m > 0:
                    pieces = [jnp.zeros((16 * m, 768), bf16)] + pieces
                if m < 6:
                    pieces = pieces + [jnp.zeros((96 - 16 * m, 768), bf16)]
                total = total + lax.dot_general(left, jnp.concatenate(pieces, 0), LAST, preferred_element_type=f32)
            else:
                wide = jnp.concatenate([jnp.zeros((112, 768), bf16), right, jnp.zeros((112, 768), bf16)], 0)
                both = lax.dot_general(left, wide, LAST, preferred_element_type=f32)
                total = total + both[:, :128]
                tail = both[:, 128:]
        first = pl.multiple_of(8 * j, 8)
        for a in range(11):
            rho_ref[8 * i + a, pl.ds(first, 16), 0:128] += total[16 * a : 16 * a + 16]
            rho_ref[8 * i + a, pl.ds(first, 16), 128:256] += tail[16 * a : 16 * a + 16]
        return 0

    lax.fori_loop(0, 4, column, 0)
    mask_y = inside_mask((24, 256), 0, 16 * dy - 1, 128)
    mask_z = inside_mask((24, 256), 1, 128 * dz - 1, 256)
    mask = mask_y * mask_z
    wide_lane = lax.broadcasted_iota(i32, (24, 128), 1)
    lane8 = lax.broadcasted_iota(i32, (8, 128), 1)
    block = jnp.zeros((8, 128), i32)
    for n in range(64):
        block = jnp.where(lane8 == n, counts_ref[n >> 5, (n >> 4) & 1, n & 15], block)
    msg_ref[0:8] = block.astype(f32)
    for i in range(2):
        picked = [jnp.where(dz == 0, near_ref[i, j, 16], near_ref[i, j, 1]) for j in range(2)]
        msg_ref[8 + 8 * i : 16 + 8 * i] = jnp.where(row8 < 4, picked[0], pltpu.roll(picked[1], 4, 0))
    faces = []
    for a in range(19):
        point = 16 * dx - 1 + a
        keep = ((point >= 0) & (point < 128)).astype(f32)
        plane = rho_ref[a] * (mask * keep)
        rho_ref[a] = plane
        low, high = plane[:, :128], plane[:, 128:]
        top = jnp.where(wide_lane < 18, pltpu.roll(low, 18, 1), pltpu.roll(high, 18, 1))
        face = jnp.where(dz == 0, top, low)
        faces.append(jnp.where(wide_lane < 21, face, 0.0))
    faces.append(jnp.zeros((24, 128), f32))
    for p in range(5):
        packed = faces[p]
        for g in range(1, 4):
            packed = packed + pltpu.roll(faces[5 * g + p], 32 * g, 1)
        msg_ref[24 + 24 * p : 48 + 24 * p] = packed


def along_z_kernel(near_ref, rho_ref, own_msg_ref, got_ref, op_ref, down_ref,
                   near1_ref, full_ref, restr_ref, a_ref, b_ref, m_ref, n_ref):
    dy, dz = lax.axis_index("gy"), lax.axis_index("ga")
    even, far = (dy & 1) == 0, (dy & 2) == 0
    row8 = lax.broadcasted_iota(i32, (8, 128), 0)
    shift = jnp.where(row8 == 2, jnp.where(dz == 0, 128.0, -128.0), 0.0)
    for i in range(2):
        got = got_ref[8 + 8 * i : 16 + 8 * i]
        parts = [jnp.where(row8 < 4, got, 0.0), jnp.where(row8 < 4, pltpu.roll(got, 4, 0), 0.0)]
        for j in range(2):
            near1_ref[i, j, 1:17] = near_ref[i, j, 1:17]
            moved = parts[j] + shift
            near1_ref[i, j, 0] = jnp.where(dz == 1, moved, 0.0)
            near1_ref[i, j, 17] = jnp.where(dz == 0, moved, 0.0)
    lane = lax.broadcasted_iota(i32, (24, 128), 1)
    high_op, low_op = op_ref[dz, 0], op_ref[dz, 1]
    down = down_ref[...]
    lane16 = lax.broadcasted_iota(i32, (16, 128), 1)
    keep = inside_mask((16, 128), 0, 8 * dy - 1, 64)
    for g in range(4):
        planes = range(5 * g, min(5 * g + 5, 19))
        stacked = []
        for p, a in enumerate(planes):
            face = pltpu.roll(got_ref[24 + 24 * p : 48 + 24 * p], (32 - 32 * g) % 128, 1)
            second = jnp.where((lane >= 32) & (lane < 64), face, rho_ref[a, :, 128:256])
            stacked.append(jnp.concatenate([rho_ref[a, :, 0:128], second], 1))
        high, low = split2(jnp.concatenate(stacked, 0))
        result = dot(high, high_op) + dot(low, high_op) + dot(high, low_op)
        for p, a in enumerate(planes):
            plane = result[24 * p : 24 * p + 24]
            full_ref[a] = plane
            h, m, l = split3(plane[:, 128:256])
            restricted = dot(down, jnp.concatenate([h, m, l], 0).astype(bf16)) * keep
            restr_ref[a] = restricted
            for out, way in ((a_ref, even), (b_ref, ~even)):
                window = jnp.where(way, plane[8:24], plane[0:16])
                out[152 + 16 * a : 168 + 16 * a] = window[:, 0:128]
                out[456 + 16 * a : 472 + 16 * a] = jnp.where(lane16 < 8, window[:, 128:256], restricted)
            m_ref[8 * a : 8 * a + 8] = jnp.where(far, restricted[8:16], restricted[0:8])
            n_ref[8 * a : 8 * a + 8] = jnp.where(far, restricted[0:8], restricted[8:16])
    counts = jnp.where(row8 == 0, own_msg_ref[0:8], jnp.where(row8 == 1, pltpu.roll(got_ref[0:8], 1, 0), 0.0))
    for out, j in ((a_ref, 1 - (dy & 1)), (b_ref, dy & 1)):
        out[0:8] = counts
        for level in range(18):
            out[8 + 8 * level : 16 + 8 * level] = jnp.where(
                row8 < 4, near1_ref[0, j, level], pltpu.roll(near1_ref[1, j, level], 4, 0)
            )


def along_y_kernel(near1_ref, full_ref, restr_ref, own_msg_ref, got_a_ref, got_b_ref, got_m_ref, got_n_ref,
                   fine_ref, coarse_ref, after_ref, near2_ref, fine2_ref, coarse2_ref,
                   a_ref, b_ref, m_ref, n_ref):
    dx, dy = lax.axis_index("gx"), lax.axis_index("gy")
    even, odd_x = (dy & 1) == 0, dx & 1
    far_x = (dx & 2) == 0
    row8 = lax.broadcasted_iota(i32, (8, 128), 0)
    keep = inside_mask((16, 128), 0, 8 * dy - 1, 64)
    lane16 = lax.broadcasted_iota(i32, (16, 128), 1)
    lane24 = lax.broadcasted_iota(i32, (24, 128), 1)
    fine_op, coarse_op = fine_ref[dy & 3], coarse_ref[dy & 3]

    def plane(a, _):
        at = pl.multiple_of(16 * a, 16)
        at8 = pl.multiple_of(8 * a, 8)
        a_low, a_high = got_a_ref[pl.ds(152 + at, 16)], got_a_ref[pl.ds(456 + at, 16)]
        b_low, b_high = got_b_ref[pl.ds(152 + at, 16)], got_b_ref[pl.ds(456 + at, 16)]
        stack = jnp.concatenate(
            [full_ref[a], jnp.concatenate([a_low, a_high], 1), jnp.concatenate([b_low, b_high], 1)], 0
        )
        high, low = split3(stack)[:2]
        fine2_ref[a] = dot(fine_op, jnp.concatenate([high, high, low], 0).astype(bf16))
        stack = jnp.concatenate(
            [restr_ref[a], a_high, b_high, got_m_ref[pl.ds(at8, 8)], got_n_ref[pl.ds(at8, 8)]], 0
        )
        high, low = split3(stack)[:2]
        coarse2_ref[a] = dot(coarse_op, jnp.concatenate([high, high, low], 0).astype(bf16)) * keep
        return 0

    lax.fori_loop(0, 19, plane, 0)
    restricted = []
    for e in range(11):
        value = None
        for a, weight in ((2 * e - 2, 0.5), (2 * e - 1, 1.0), (2 * e, 0.5)):
            if 0 <= a < 19:
                term = coarse2_ref[a] * weight
                value = term if value is None else value + term
        point = 8 * dx - 1 + e
        restricted.append(value * ((point >= 0) & (point < 64)).astype(f32))
    blank = jnp.zeros((8, 128), f32)
    for out, first in ((a_ref, 8 * (1 - odd_x)), (b_ref, 8 * odd_x)):
        for n in range(11):
            plane_value = fine2_ref[first + n]
            out[296 + 24 * n : 320 + 24 * n] = plane_value[:, 0:128]
            out[560 + 24 * n : 584 + 24 * n] = jnp.where(
                lane24 < 8, plane_value[:, 128:256], jnp.concatenate([restricted[n], blank], 0)
            )
    for n in range(3):
        m_ref[16 * n : 16 * n + 16] = jnp.where(far_x, restricted[8 + n], restricted[n])
        n_ref[16 * n : 16 * n + 16] = jnp.where(far_x, restricted[n], restricted[8 + n])
    shift_a = jnp.where(row8 == 1, jnp.where(even, 16.0, -16.0), 0.0)
    at_a = 3 * (1 - (dy & 1))
    for level in range(18):
        for y, source, shift in ((at_a, got_a_ref, shift_a), (3 - at_a, got_b_ref, -shift_a)):
            got = source[8 + 8 * level : 16 + 8 * level]
            near2_ref[0, y, level] = jnp.where(row8 < 4, got, 0.0) + shift
            near2_ref[1, y, level] = jnp.where(row8 < 4, pltpu.roll(got, 4, 0), 0.0) + shift
        for x in range(2):
            for y in range(2):
                near2_ref[x, y + 1, level] = near1_ref[x, y, level]
    below, above = jnp.where(even, got_b_ref[0:8], got_a_ref[0:8]), jnp.where(even, got_a_ref[0:8], got_b_ref[0:8])
    counts = jnp.where(row8 < 2, own_msg_ref[0:8], 0.0)
    counts = jnp.where((row8 >= 2) & (row8 < 4), pltpu.roll(below, 2, 0), counts)
    counts = jnp.where((row8 >= 4) & (row8 < 6), pltpu.roll(above, 4, 0), counts)
    for out, x in ((a_ref, 1 - odd_x), (b_ref, odd_x)):
        out[0:8] = counts
        for level in range(18):
            for pair in range(2):
                at = 8 + 8 * (2 * level + pair)
                out[at : at + 8] = jnp.where(
                    row8 < 4, near2_ref[x, 2 * pair, level], pltpu.roll(near2_ref[x, 2 * pair + 1, level], 4, 0)
                )


def along_x_kernel(fine2_ref, own_msg_ref, got_a_ref, got_b_ref, got_m_ref, got_n_ref,
                   up_y_ref, up_z_ref, after_ref, phi_ref, source, third, coarse):
    dx, dy, dz = lax.axis_index("gx"), lax.axis_index("gy"), lax.axis_index("ga")
    even, far = 1 - (dx & 1), 1 - ((dx >> 1) & 1)
    for p in range(8):
        source[p] = jnp.zeros((24, 256), f32)
        source[27 + p] = jnp.zeros((24, 256), f32)
        coarse[p] = jnp.zeros((16, 128), f32)
        coarse[19 + p] = jnp.zeros((16, 128), f32)
    for p in range(19):
        source[8 + p] = fine2_ref[p]
    for got, first in ((got_a_ref, 24 * even), (got_b_ref, 24 * (1 - even))):
        for n in range(11):
            source[first + n, :, 0:128] += got[296 + 24 * n : 320 + 24 * n]
            source[first + n, :, 128:256] += got[560 + 24 * n : 584 + 24 * n]
    for n in range(11):
        coarse[8 + n] = own_msg_ref[560 + 24 * n : 576 + 24 * n]
    for got, first in ((got_a_ref, 16 * even), (got_b_ref, 16 * (1 - even))):
        for n in range(11):
            coarse[first + n] += got[560 + 24 * n : 576 + 24 * n]
    for got, first in ((got_m_ref, 24 * far), (got_n_ref, 24 * (1 - far))):
        for n in range(3):
            coarse[first + n] += got[16 * n : 16 * n + 16]
    fine_weights = [float(w) for w in fine_kernel(np.arange(9.0))]
    coarse_weights = [float(w) for w in coarse_kernel(np.arange(9.0))]

    def fine_plane(a, _):
        value = source[a + 8] * (4.0 * fine_weights[0])
        for d in range(1, 9):
            value = value + (source[a + 8 - d] + source[a + 8 + d]) * (4.0 * fine_weights[d])
        third[a] = value
        return 0

    lax.fori_loop(0, 19, fine_plane, 0)

    lifted = []
    up_y, up_z = up_y_ref[...], up_z_ref[...]
    for e in range(11):
        value = coarse[e + 8] * (2.0 * coarse_weights[0])
        for d in range(1, 9):
            value = value + (coarse[e + 8 - d] + coarse[e + 8 + d]) * (2.0 * coarse_weights[d])
        point = 8 * dx - 1 + e
        value = value * ((point >= 0) & (point < 64)).astype(f32)
        h, m, l = split3(value)
        tall = dot(up_y, jnp.concatenate([h, m, l], 0).astype(bf16))
        h, m, l = split3(tall)
        stacked = jnp.concatenate([h, m, l], 0).astype(bf16)
        wide = dot(stacked, up_z)
        lifted.append(wide[0:24] + wide[24:48] + wide[48:72])
    mask = inside_mask((24, 256), 0, 16 * dy - 1, 128) * inside_mask((24, 256), 1, 128 * dz - 1, 256)
    lane = lax.broadcasted_iota(i32, (24, 256), 1)
    mask = jnp.where(lane < 131, mask, 0.0)
    for a in range(19):
        if a % 2:
            value = lifted[(a + 1) // 2]
        else:
            value = 0.5 * (lifted[a // 2] + lifted[a // 2 + 1])
        point = 16 * dx - 1 + a
        keep = mask * ((point >= 0) & (point < 128)).astype(f32)
        phi_ref[a] = jnp.where(keep > 0.0, third[a] + value, 0.0)


def gather_kernel(off_ref, charge_ref, counts_ref, phi_ref, out_ref):
    lane = lax.broadcasted_iota(i32, (1, 128), 1)
    lane176 = lax.broadcasted_iota(i32, (176, 128), 1)

    def column(ij, _):
        i, j = ij >> 1, ij & 1
        first = pl.multiple_of(8 * j, 8)
        low = jnp.concatenate([phi_ref[8 * i + a, pl.ds(first, 16), 0:128] for a in range(11)], 0)
        high = jnp.concatenate([phi_ref[8 * i + a, pl.ds(first, 16), 128:256] for a in range(11)], 0)
        for m in range(8):
            window = pltpu.roll(low, (128 - 16 * m) % 128, 1) if m else low
            if m == 7:
                window = jnp.where(lane176 < 16, window, pltpu.roll(high, 16, 1))
            window = jnp.where(lane176 < 32, window, 0.0)
            part_h = window.astype(bf16).astype(f32)
            part_m = window - part_h
            left = (part_h + pltpu.roll(part_m, 32, 1) + pltpu.roll(part_h, 64, 1)).astype(bf16)
            stacks, slopes, sides = [], [], []
            for half in range(2):
                k = 2 * m + half
                ox = off_ref[0, i, j, k : k + 1]
                oy = off_ref[1, i, j, k : k + 1]
                oz = off_ref[2, i, j, k : k + 1]
                count = counts_ref[i, j, k]
                weighted = jnp.where(lane < count, charge_ref[i, j, k : k + 1], 0.0)
                shifted = weights_at(oz, 32, 8 * half)
                for bag, value in ((stacks, spline(shifted)), (slopes, spline_slope(shifted))):
                    high_part, low_part = split2(value)
                    bag.append(jnp.concatenate([high_part, high_part, low_part, jnp.zeros((32, 128), bf16)], 0))
                sides.append((ox, oy, weighted))
            right = jnp.concatenate(stacks + slopes, 1)
            product = dot(left, right)
            for half in range(2):
                k = 2 * m + half
                ox, oy, weighted = sides[half]
                level = product[:, 128 * half : 128 * half + 128]
                rising = product[:, 256 + 128 * half : 384 + 128 * half]
                sx = weights_at(ox, 16, 0)
                sy = weights_at(oy, 16, 0)
                wx, gx = spline(sx), spline_slope(sx)
                wy, gy = spline(sy), spline_slope(sy)
                along = across = up = None
                for a in range(11):
                    piece = level[16 * a : 16 * a + 16]
                    rise = rising[16 * a : 16 * a + 16]
                    terms = (gx[a : a + 1] * piece, wx[a : a + 1] * piece, wx[a : a + 1] * rise)
                    if a == 0:
                        along, across, up = terms
                    else:
                        along, across, up = along + terms[0], across + terms[1], up + terms[2]
                force_x = jnp.sum(along * wy, axis=0, keepdims=True)
                force_y = jnp.sum(across * gy, axis=0, keepdims=True)
                force_z = jnp.sum(up * wy, axis=0, keepdims=True)
                out_ref[0, i, j, k : k + 1] = -weighted * force_x
                out_ref[1, i, j, k : k + 1] = -weighted * force_y
                out_ref[2, i, j, k : k + 1] = -weighted * force_z
        return 0

    lax.fori_loop(0, 4, column, 0)


def pair_scratch(form, cells, tiles):
    rows, slots, share = form
    sets = cells // share
    return (
        [
            pltpu.VMEM((tiles, 8, 128), f32),
            pltpu.VMEM((tiles, 48, 128), bf16),
            pltpu.VMEM((tiles, 16, 128), bf16),
            pltpu.VMEM((sets + 1, share * 128, 128), f32),
            pltpu.VMEM(((sets + 1) * (share * 128 // rows), 16, 128), f32),
        ]
        + [
            pltpu.VMEM((rows, TILES * 128), f32),
            pltpu.VMEM((rows, TILES * 128), bf16),
            pltpu.VMEM((rows, TILES * 128), bf16),
        ]
        * slots
        + [pltpu.SMEM((128,), i32), pltpu.SMEM((cells,), i32)]
        + [pltpu.SMEM((sets + 1,), i32)] * 3
    )


def middle_of(center):
    row = lax.broadcasted_iota(i32, (8, 128), 0)
    return jnp.where(row < 2, 16.0, jnp.where(row == 2, center, 0.0))


def pack_list(packed, start, base, tile, levels, center):
    lane = lax.broadcasted_iota(i32, (8, 128), 1)
    middle = middle_of(center)
    end, current = tile * 128, jnp.zeros((8, 128), f32)
    for level, beads in enumerate(levels):
        start[base + level] = end
        for value, count in beads:
            within, tile = end & 127, end >> 7
            turned = pltpu.roll(value - middle, within, 1)
            keep = lane < within
            current = jnp.where(keep, current, turned)
            packed[tile] = current
            end = end + count
            current = jnp.where((end >> 7) > tile, jnp.where(keep, turned, 0.0), current)
    start[base + 10] = end
    packed[end >> 7] = jnp.where(lane < (end & 127), current, 0.0)
    for e in range(1, TILES):
        packed[(end >> 7) + e] = jnp.zeros((8, 128), f32)
    return (end >> 7) + TILES


def pair_sums(scratch, form, cells, used, own_pos, own_count, own_start, own_center, emit):
    packed, features, sources, own_features, sums = scratch[:5]
    start, row_at, first_tile, groups_of, blocks_of = scratch[-5:]
    height, flight, share = form
    sets = cells // share
    slots = [scratch[5 + 3 * e : 8 + 3 * e] for e in range(flight)]
    blocks = share * 128 // height
    lane = lax.broadcasted_iota(i32, (16, 128), 1)
    row = lax.broadcasted_iota(i32, (8, 128), 0)
    for e in range(8):
        packed[used + e] = jnp.zeros((8, 128), f32)

    def near_step(step, _):
        for e in range(8):
            tile = 8 * step + e
            value = packed[tile]
            norm = value[0:1] * value[0:1] + value[1:2] * value[1:2] + value[2:3] * value[2:3]
            vector = jnp.where(row < 3, value, jnp.where(row == 3, norm, jnp.where(row == 4, 1.0, 0.0)))
            h, m, l = split3(vector)
            features[tile] = jnp.concatenate([h, h, m, m, h, l], 0).astype(bf16)
            charge = value[3:4]
            vector = jnp.where(row < 3, value * charge, jnp.where(row == 3, charge, 0.0))
            h, m, l = split3(vector)
            sources[tile] = jnp.concatenate(
                [jnp.where(row < 4, h, pltpu.roll(m, 4, 0)), jnp.where(row < 4, l, 0.0)], 0
            ).astype(bf16)
        return 0

    lax.fori_loop(0, (used + 7) // 8, near_step, 0)

    def own_one(n, which, at):
        value = own_pos(n) - middle_of(own_center(n))
        norm = value[0:1] * value[0:1] + value[1:2] * value[1:2] + value[2:3] * value[2:3]
        vector = jnp.where(
            row < 3,
            value * (2.0 / 64),
            jnp.where(row == 3, -1.0 / 64, jnp.where(row == 4, 1.0 - norm * (1.0 / 64), 0.0)),
        )
        h, m, l = split3(vector)
        stacked = jnp.concatenate([h, m, h, m, l, h, jnp.zeros((80, 128), f32)], 0)
        own_features[which, pl.ds(pl.multiple_of(at, 8), 128), :] = jnp.transpose(stacked)
        row_at[n] = at
        return at + ((own_count(n) + 7) >> 3) * 8

    def own_step(step, total):
        for e in range(8 // share):
            which = step * (8 // share) + e
            at = i32(0)
            for c in range(share):
                at = own_one(c * sets + which, which, at)
            for b in range(blocks):
                sums[which * blocks + b] = jnp.zeros((16, 128), f32)
            level = own_start(which)
            begin, stop = start[level], start[level + 3]
            tile = begin >> 7
            groups = jnp.maximum((((stop + 127) >> 7) - tile + TILES - 1) // TILES, 1)
            rows = (at + height - 1) // height
            first_tile[which], groups_of[which], blocks_of[which] = tile, groups, rows
            total = total + groups * rows
        return total

    total = lax.fori_loop(0, cells // 8, own_step, i32(0))
    own_features[sets] = jnp.zeros((share * 128, 128), f32)
    for e in range(blocks):
        sums[sets * blocks + e] = jnp.zeros((16, 128), f32)
    first_tile[sets], groups_of[sets], blocks_of[sets] = i32(0), i32(1), i32(1)
    for distance, high, low in slots:
        distance[...] = jnp.zeros((height, TILES * 128), f32)
        high[...] = jnp.zeros((height, TILES * 128), bf16)
        low[...] = jnp.zeros((height, TILES * 128), bf16)

    def item(_, state):
        cell, block, group = state[:3]
        older, oldest = state[3 : 3 + 2 * flight], state[3 + 2 * flight :]
        added, shares, fresh, tags = [], [], [], []
        for e in range(flight):
            distance, high, low = slots[e]
            tile = oldest[2 * e + 1]
            source = jnp.concatenate([sources[tile + s] for s in range(TILES)], 1)
            added.append(
                lax.dot_general(
                    jnp.concatenate([source, source], 1),
                    jnp.concatenate([high[...], low[...]], 1),
                    LAST,
                    preferred_element_type=f32,
                )
            )
            reach = distance[...]
            kept = jnp.maximum(reach, 0.0)
            strength = (kept * kept * kept) / (CAP - reach)
            shares.append(split2(strength))
            groups, rows = groups_of[cell], blocks_of[cell]
            tile = first_tile[cell] + group * TILES
            at = pl.multiple_of(block * height, height)
            left = own_features[cell, pl.ds(at, height), 0:48].astype(bf16)
            right = jnp.concatenate([features[tile + s] for s in range(TILES)], 1)
            fresh.append(dot(left, right))
            tags += [cell * blocks + block, tile]
            group = group + 1
            wrap = (group >= groups).astype(i32)
            group = group * (1 - wrap)
            block = block + wrap
            wrap = (block >= rows).astype(i32)
            block = block * (1 - wrap)
            cell = jnp.minimum(cell + wrap, sets)
        for e in range(flight):
            distance, high, low = slots[e]
            where = oldest[2 * e]
            sums[where, :, 0:height] = sums[where, :, 0:height] + added[e]
            high[...], low[...] = shares[e]
            distance[...] = fresh[e]
        return (cell, block, group) + tuple(tags) + tuple(older)

    spare = (i32(sets * blocks), i32(0))
    lax.fori_loop(0, (total + flight - 1) // flight + 2, item, (i32(0),) * 3 + spare * (2 * flight))

    def finish_one(n):
        if share == 1:
            parts = [sums[n * blocks + e, :, 0:height] for e in range(blocks)]
            whole = jnp.concatenate(parts, 1) if blocks > 1 else parts[0]
        else:
            at = row_at[n]
            block, within = (n % sets) * blocks + (at >> 7), at & 127
            back = (128 - within) & 127
            whole = jnp.where(
                lane < 128 - within, pltpu.roll(sums[block], back, 1), pltpu.roll(sums[block + 1], back, 1)
            )
        whole = whole[0:4] + whole[4:8] + whole[8:12]
        raw = own_pos(n)
        value = raw - middle_of(own_center(n))
        emit(n, (value[0:3] * whole[3:4] - whole[0:3]) * (raw[3:4] * (1.0 / 64)), raw)

    def finish(step, _):
        for e in range(4):
            finish_one(4 * step + e)
        return 0

    lax.fori_loop(0, cells // 4, finish, 0)


def inner_pairs_kernel(part, near_ref, counts_ref, partners_ref, after_ref, out_ref, table, *scratch):
    lane = lax.broadcasted_iota(i32, (1, 128), 1)
    for column in range(4):
        table[18 * column] = i32(0)
        table[18 * column + 17] = i32(0)

    def copy_count(k, _):
        for column in range(4):
            table[18 * column + 1 + k] = counts_ref[column >> 1, column & 1, k]
        return 0

    lax.fori_loop(0, 16, copy_count, 0)

    levels = [[(near_ref[18 * c + 8 * part + n], table[18 * c + 8 * part + n]) for c in range(4)] for n in range(10)]
    used = pack_list(scratch[0], scratch[-5], 0, i32(0), levels, 64.0 * part + 40.0)

    def cell_at(n):
        return (n >> 3) * 18 + (n & 7) + (8 * part + 1)

    def emit(n, value, raw):
        x, y, k = n >> 4, (n >> 3) & 1, 8 * part + (n & 7)
        count = table[cell_at(n)]
        partner = partners_ref[x, y, pl.ds(k, 1), :]
        other = jnp.take_along_axis(raw, jnp.broadcast_to(partner, (8, 128)), axis=1)
        both = (lane < count) & (partner < count)
        out_ref[x, y, n & 7, 0:3] = value + jnp.where(both, -0.1 * (raw[0:3] - other[0:3]), 0.0)

    pair_sums(
        scratch,
        INNER,
        32,
        used,
        lambda n: near_ref[cell_at(n)],
        lambda n: table[cell_at(n)],
        lambda n: n & 7,
        lambda n: 64.0 * part + 40.0,
        emit,
    )


def outer_pairs_kernel(near2_ref, own_msg_ref, got_a_ref, got_b_ref, first_ref, second_ref, out_ref,
                       near, counts, table, *scratch):
    dz, odd = lax.axis_index("ga"), lax.axis_index("gx") & 1
    row8 = lax.broadcasted_iota(i32, (8, 128), 0)
    for n, source in enumerate((got_a_ref, own_msg_ref, got_b_ref)):
        pltpu.sync_copy(source.at[0:8], counts.at[n])
    shift_a = jnp.where(row8 == 0, jnp.where(odd == 0, 16.0, -16.0), 0.0)
    at_a = 3 * (1 - odd)

    def level_step(level, _):
        for x in range(2):
            for y in range(4):
                near[(4 * x + 4 + y) * 18 + level] = near2_ref[x, y, level]
        for x, source, shift in ((at_a, got_a_ref, shift_a), (3 - at_a, got_b_ref, -shift_a)):
            for pair in range(2):
                at = pl.multiple_of(8 + 8 * (2 * level + pair), 8)
                got = source[pl.ds(at, 8)]
                near[(4 * x + 2 * pair) * 18 + level] = jnp.where(row8 < 4, got, 0.0) + shift
                near[(4 * x + 2 * pair + 1) * 18 + level] = jnp.where(row8 < 4, pltpu.roll(got, 4, 0), 0.0) + shift
        return 0

    lax.fori_loop(0, 18, level_step, 0)
    for x in range(4):
        which, along = ((2 * (1 - odd), 1), (1, 0), (1, 1), (2 * odd, 0))[x]
        for y in range(4):
            pair_row, across = ((2, 1), (0, 0), (0, 1), (4, 0))[y]
            base = 32 * along + 16 * across
            at = (x * 4 + y) * 18
            table[at] = jnp.where(dz == 1, counts[which, pair_row + 1, base + 15], 0.0).astype(i32)
            table[at + 17] = jnp.where(dz == 0, counts[which, pair_row + 1, base], 0.0).astype(i32)

            def copy_count(k, _, which=which, pair_row=pair_row, base=base, at=at):
                table[at + 1 + k] = counts[which, pair_row, base + k].astype(i32)
                return 0

            lax.fori_loop(0, 16, copy_count, 0)

    def split(number):
        return number >> 2, (number >> 1) & 1, number & 1

    def one_list(number, tile):
        i, j, part = split(number)
        outside = [(12 * i + j + c) * 18 + 8 * part for c in range(3)]
        outside += [(4 * x + 3 * j) * 18 + 8 * part for x in (1, 2)]
        within = [(4 * x + y) * 18 + 8 * part for x in (1, 2) for y in (1, 2)]
        levels = []
        for level in range(10):
            beads = [(near[base + level], table[base + level]) for base in outside]
            if level in (0, 9):
                use = part if level else 1 - part
                beads += [(near[base + level], table[base + level] * use) for base in within]
            levels.append(beads)
        return pack_list(scratch[0], scratch[-5], 16 * number, tile, levels, 64.0 * part.astype(f32) + 40.0)

    used = lax.fori_loop(0, 8, one_list, i32(0))

    def own_at(n):
        i, j, part = split(n >> 3)
        return (4 * (i + 1) + j + 1) * 18 + 8 * part + 1 + (n & 7)

    def emit(n, value, raw):
        i, j, part = split(n >> 3)
        value = value + jnp.where(part == 0, first_ref[i, j, n & 7, 0:3], second_ref[i, j, n & 7, 0:3])
        for d in range(3):
            out_ref[d, i, j, pl.ds(8 * part + (n & 7), 1), :] = value[d : d + 1]

    pair_sums(
        scratch,
        OUTER,
        64,
        used,
        lambda n: near[own_at(n)],
        lambda n: table[own_at(n)],
        lambda n: 16 * (n >> 3) + (n & 7),
        lambda n: 64.0 * ((n >> 3) & 1).astype(f32) + 40.0,
        emit,
    )


def call(kernel, shapes, inputs, specs=None, scratch=(), flops=10**6, out_specs=None):
    single = not isinstance(shapes, (list, tuple)) or isinstance(shapes[0], int)
    shapes = [shapes] if single else shapes
    result = pl.pallas_call(
        kernel,
        out_shape=[jax.ShapeDtypeStruct(s, f32) for s in shapes],
        in_specs=specs or [VMEM] * len(inputs),
        out_specs=[VMEM] * len(shapes),
        scratch_shapes=list(scratch),
        cost_estimate=pl.CostEstimate(flops=flops, transcendentals=0, bytes_accessed=10**6),
        compiler_params=pltpu.CompilerParams(vmem_limit_bytes=40 << 20),
    )(*inputs)
    return result[0] if single else result


PARTNERS = (
    ((0, 1), (2, 3), (4, 5), (6, 7)),
    ((1, 2), (3, 4), (5, 6)),
    ((0, 2), (1, 3), (4, 6), (5, 7)),
    ((2, 4), (3, 5)),
)


def exchange(messages, axis):
    return [
        lax.ppermute(value, axis, [way for p, q in pairs for way in ((p, q), (q, p))])
        for value, pairs in zip(messages, PARTNERS)
    ]


def per_device(offsets, charge, counts, partners):
    z_op = jnp.asarray(np.stack([np.stack(halves(z_operator(part))) for part in range(2)]))
    fine_op, coarse_op, y_down, y_up = [jnp.asarray(m) for m in y_operators()]
    z_up = jnp.asarray(z_prolong())
    near, rho, z_msg = call(
        spread_kernel,
        [(2, 2, 18, 8, 128), (19, 24, 256), (144, 128)],
        (offsets, charge, counts),
        [VMEM, VMEM, SMEM],
    )
    z_got = lax.ppermute(z_msg, "ga", [(0, 1), (1, 0)])
    near1, full, restr, *y_msgs = call(
        along_z_kernel,
        [(2, 2, 18, 8, 128), (19, 24, 256), (19, 16, 128), (760, 128), (760, 128), (152, 128), (152, 128)],
        (near, rho, z_msg, z_got, z_op, y_down),
    )
    y_got = exchange(y_msgs, "gy")
    inner = lambda part, near_in, after: call(
        lambda *refs: inner_pairs_kernel(part, *refs),
        (2, 2, 8, 8, 128),
        (near_in.reshape(72, 8, 128), counts, partners, after),
        [VMEM, SMEM, VMEM, ANY],
        [pltpu.SMEM((72,), i32)] + pair_scratch(INNER, 32, 40 + TILES + 16),
        flops=10**9,
    )
    first = inner(0, near, full)
    near2, fine2, _, *x_msgs = call(
        along_y_kernel,
        [(2, 4, 18, 8, 128), (19, 24, 256), (19, 16, 128), (824, 128), (824, 128), (48, 128), (48, 128)],
        (near1, full, restr, y_msgs[0], *y_got, fine_op, coarse_op, first),
        [VMEM] * 10 + [ANY],
    )
    x_got = exchange(x_msgs, "gx")
    second = inner(1, near, fine2)
    phi = call(
        along_x_kernel,
        (19, 24, 256),
        (fine2, x_msgs[0], *x_got, y_up, z_up, second),
        [VMEM] * 8 + [ANY],
        [pltpu.VMEM((35, 24, 256), f32), pltpu.VMEM((19, 24, 256), f32), pltpu.VMEM((27, 16, 128), f32)],
    )
    short_force = call(
        outer_pairs_kernel,
        (3, 2, 2, 16, 128),
        (near2, x_msgs[0], x_got[0], x_got[1], first, second),
        None,
        [
            pltpu.VMEM((288, 8, 128), f32),
            pltpu.SMEM((3, 8, 128), f32),
            pltpu.SMEM((288,), i32),
        ]
        + pair_scratch(OUTER, 64, 8 * (54 + TILES) + 24),
        flops=10**9,
    )
    long_force = call(
        gather_kernel, (3, 2, 2, 16, 128), (offsets, charge, counts, phi), [VMEM, VMEM, SMEM, VMEM]
    )
    return short_force, long_force


def solution(mesh):
    return jax.shard_map(
        per_device,
        mesh=mesh,
        in_specs=(
            P(None, "gx", "gy", "ga", None),
            P("gx", "gy", "ga", None),
            P("gx", "gy", "ga"),
            P("gx", "gy", "ga", None),
        ),
        out_specs=(P(None, "gx", "gy", "ga", None), P(None, "gx", "gy", "ga", None)),
        check_vma=False,
    )
```

```python
import jax
import jax.numpy as jnp
import numpy as np
from jax import lax
from jax.experimental import pallas as pl
from jax.experimental.pallas import tpu as pltpu
from jax.sharding import PartitionSpec as P

f32, bf16, i32 = jnp.float32, jnp.bfloat16, jnp.int32
LAST = (((1,), (1,)), ((), ()))
CAP = 65.0 / 64.0
TILES = 2
EARLY = 12
INNER, OUTER = (128, 8, 4), (64, 16, 1)
VMEM = pl.BlockSpec(memory_space=pltpu.VMEM)
SMEM = pl.BlockSpec(memory_space=pltpu.SMEM)
ANY = pl.BlockSpec(memory_space=pl.ANY)


def fine_kernel(gap):
    return np.where(np.abs(gap) <= 8, np.exp(-gap * gap / 12.5), 0.0)


def coarse_kernel(gap):
    return np.where(np.abs(gap) <= 8, np.exp(-gap * gap / 72.0), 0.0)


def hat(gap):
    return np.where(gap == 0, 1.0, np.where(np.abs(gap) == 1, 0.5, 0.0))


def halves(matrix):
    high = matrix.astype(np.float32).astype(jnp.bfloat16)
    low = (matrix - high.astype(np.float64)).astype(np.float32).astype(jnp.bfloat16)
    return high, low


def z_operator(part):
    source = np.full(256, 10**6, np.int64)
    source[:131] = 128 * part - 1 + np.arange(131)
    source[160:181] = np.arange(21) + (127 if part == 0 else 109)
    inside = (source >= 0) & (source < 256)
    result = np.zeros((256, 256))
    target = 128 * part - 1 + np.arange(131)
    fine = fine_kernel((target[None, :] - source[:, None]).astype(np.float64))
    result[:, :131] = fine * ((target >= 0) & (target < 256))[None, :]
    middle = np.arange(128)
    down = hat((source[:, None] - 2 * middle[None, :]).astype(np.float64))
    point = 64 * part - 1 + np.arange(67)
    spread = coarse_kernel((middle[:, None] - point[None, :]).astype(np.float64))
    spread = spread * ((point >= 0) & (point < 128))[None, :]
    result[:, 136:203] = down @ spread
    return result * inside[:, None]


def y_operators():
    fines, coarses = [], []
    for place in range(4):
        near, far = (1 - 2 * (place & 1)), (1 - (place & 2))
        parts = [np.where(np.arange(24) < 19, np.arange(24), 10**6)]
        for side in (near, -near):
            parts.append(np.where(np.arange(16) < 11, np.arange(16) + (16 if side > 0 else -8), 10**6))
        fine = fine_kernel(np.arange(24)[:, None] - np.concatenate(parts)[None, :].astype(np.float64))
        fine[19:] = 0
        parts = [np.where(np.arange(16) < 11, np.arange(16), 10**6)]
        for side in (near, -near):
            parts.append(np.where(np.arange(16) < 11, np.arange(16) + (8 if side > 0 else -8), 10**6))
        for side in (far, -far):
            parts.append(np.where(np.arange(8) < 3, np.arange(8) + (16 if side > 0 else -8), 10**6))
        coarse = coarse_kernel(np.arange(16)[:, None] - np.concatenate(parts)[None, :].astype(np.float64))
        coarse[11:] = 0
        fines.append(fine)
        coarses.append(coarse)
    down = hat(np.arange(24)[None, :] - (2.0 * np.arange(16)[:, None] - 1))
    down[11:] = 0
    up = hat(np.arange(24)[:, None] - (2.0 * np.arange(16)[None, :] - 1))
    up[19:] = 0
    up[:, 11:] = 0
    stack = lambda m: np.concatenate([halves(m)[0], halves(m)[1], halves(m)[0]], 1)
    thrice = lambda m: np.concatenate([halves(m)[0]] * 3, 1)
    return np.stack([stack(m) for m in fines]), np.stack([stack(m) for m in coarses]), thrice(down), thrice(up)


def z_prolong():
    result = np.zeros((128, 256))
    point = 2.0 * np.arange(67) - 1
    result[8:75, :131] = hat(np.arange(131)[None, :] - point[:, None])
    return halves(result)[0]


def split2(value):
    high = value.astype(bf16)
    return high, (value - high.astype(f32)).astype(bf16)


def split3(value):
    high = value.astype(bf16).astype(f32)
    rest = value - high
    middle = rest.astype(bf16).astype(f32)
    return high, middle, rest - middle


def dot(left, right):
    return jnp.dot(left, right, preferred_element_type=f32)


def spline(shifted):
    magnitude = jnp.abs(shifted)
    margin = jnp.maximum(1.5 - magnitude, 0.0)
    return jnp.where(magnitude < 0.5, 0.75 - shifted * shifted, 0.5 * margin * margin)


def spline_slope(shifted):
    magnitude = jnp.abs(shifted)
    margin = jnp.maximum(1.5 - magnitude, 0.0)
    return jnp.where(magnitude < 0.5, -2.0 * shifted, jnp.where(shifted > 0.0, -margin, margin))


def weights_at(offset, rows, first):
    points = lax.broadcasted_iota(i32, (rows, 128), 0).astype(f32)
    return 8.0 * offset + (1.0 + first) - points


def inside_mask(shape, dim, start, count):
    point = lax.broadcasted_iota(i32, shape, dim) + start
    return ((point >= 0) & (point < count)).astype(f32)


def spread_kernel(off_ref, charge_ref, counts_ref, near_ref, rho_ref, msg_ref):
    dx, dy, dz = lax.axis_index("gx"), lax.axis_index("gy"), lax.axis_index("ga")
    lane = lax.broadcasted_iota(i32, (1, 128), 1)
    row8 = lax.broadcasted_iota(i32, (8, 128), 0)
    rho_ref[...] = jnp.zeros((19, 24, 256), f32)
    zero8 = jnp.zeros((8, 128), f32)
    for i in range(2):
        for j in range(2):
            near_ref[i, j, 0] = zero8
            near_ref[i, j, 17] = zero8

    def column(ij, _):
        i, j = ij >> 1, ij & 1
        shift_x = 8.0 * (i + 1).astype(f32)
        shift_y = 8.0 * (j + 1).astype(f32)
        total = jnp.zeros((176, 128), f32)
        tail = None
        for m in range(8):
            highs, lows, z_highs, z_lows = [], [], [], []
            for half in range(2):
                k = 2 * m + half
                ox = off_ref[0, i, j, k : k + 1]
                oy = off_ref[1, i, j, k : k + 1]
                oz = off_ref[2, i, j, k : k + 1]
                count = counts_ref[i, j, k]
                weighted = jnp.where(lane < count, charge_ref[i, j, k : k + 1], 0.0)
                near_ref[i, j, k + 1] = jnp.concatenate(
                    [8.0 * ox + shift_x, 8.0 * oy + shift_y, 8.0 * oz + 8.0 * (k + 1), weighted, zero8[:4]], 0
                )
                wx = spline(weights_at(ox, 16, 0)) * weighted
                wy = spline(weights_at(oy, 16, 0))
                wz = spline(weights_at(oz, 32, 8 * half))
                plane = jnp.concatenate([wx[a : a + 1] * wy for a in range(11)], 0)
                high, low = split2(plane)
                highs.append(high)
                lows.append(low)
                z_high, z_low = split2(wz)
                z_highs.append(z_high)
                z_lows.append(z_low)
            left = jnp.concatenate(highs + lows + highs, 1)
            right = jnp.concatenate(z_highs + z_highs + z_lows, 1)
            if m < 7:
                pieces = [right]
                if m > 0:
                    pieces = [jnp.zeros((16 * m, 768), bf16)] + pieces
                if m < 6:
                    pieces = pieces + [jnp.zeros((96 - 16 * m, 768), bf16)]
                total = total + lax.dot_general(left, jnp.concatenate(pieces, 0), LAST, preferred_element_type=f32)
            else:
                wide = jnp.concatenate([jnp.zeros((112, 768), bf16), right, jnp.zeros((112, 768), bf16)], 0)
                both = lax.dot_general(left, wide, LAST, preferred_element_type=f32)
                total = total + both[:, :128]
                tail = both[:, 128:]
        first = pl.multiple_of(8 * j, 8)
        for a in range(11):
            rho_ref[8 * i + a, pl.ds(first, 16), 0:128] += total[16 * a : 16 * a + 16]
            rho_ref[8 * i + a, pl.ds(first, 16), 128:256] += tail[16 * a : 16 * a + 16]
        return 0

    lax.fori_loop(0, 4, column, 0)
    mask_y = inside_mask((24, 256), 0, 16 * dy - 1, 128)
    mask_z = inside_mask((24, 256), 1, 128 * dz - 1, 256)
    mask = mask_y * mask_z
    wide_lane = lax.broadcasted_iota(i32, (24, 128), 1)
    lane8 = lax.broadcasted_iota(i32, (8, 128), 1)
    block = jnp.zeros((8, 128), i32)
    for n in range(64):
        block = jnp.where(lane8 == n, counts_ref[n >> 5, (n >> 4) & 1, n & 15], block)
    msg_ref[0:8] = block.astype(f32)
    for i in range(2):
        picked = [jnp.where(dz == 0, near_ref[i, j, 16], near_ref[i, j, 1]) for j in range(2)]
        msg_ref[8 + 8 * i : 16 + 8 * i] = jnp.where(row8 < 4, picked[0], pltpu.roll(picked[1], 4, 0))
    faces = []
    for a in range(19):
        point = 16 * dx - 1 + a
        keep = ((point >= 0) & (point < 128)).astype(f32)
        plane = rho_ref[a] * (mask * keep)
        rho_ref[a] = plane
        low, high = plane[:, :128], plane[:, 128:]
        top = jnp.where(wide_lane < 18, pltpu.roll(low, 18, 1), pltpu.roll(high, 18, 1))
        face = jnp.where(dz == 0, top, low)
        faces.append(jnp.where(wide_lane < 21, face, 0.0))
    faces.append(jnp.zeros((24, 128), f32))
    for p in range(5):
        packed = faces[p]
        for g in range(1, 4):
            packed = packed + pltpu.roll(faces[5 * g + p], 32 * g, 1)
        msg_ref[24 + 24 * p : 48 + 24 * p] = packed


def along_z_kernel(near_ref, rho_ref, own_msg_ref, got_ref, op_ref, down_ref,
                   near1_ref, full_ref, restr_ref, a_ref, b_ref, m_ref, n_ref):
    dy, dz = lax.axis_index("gy"), lax.axis_index("ga")
    even, far = (dy & 1) == 0, (dy & 2) == 0
    row8 = lax.broadcasted_iota(i32, (8, 128), 0)
    shift = jnp.where(row8 == 2, jnp.where(dz == 0, 128.0, -128.0), 0.0)
    for i in range(2):
        got = got_ref[8 + 8 * i : 16 + 8 * i]
        parts = [jnp.where(row8 < 4, got, 0.0), jnp.where(row8 < 4, pltpu.roll(got, 4, 0), 0.0)]
        for j in range(2):
            near1_ref[i, j, 1:17] = near_ref[i, j, 1:17]
            moved = parts[j] + shift
            near1_ref[i, j, 0] = jnp.where(dz == 1, moved, 0.0)
            near1_ref[i, j, 17] = jnp.where(dz == 0, moved, 0.0)
    lane = lax.broadcasted_iota(i32, (24, 128), 1)
    high_op, low_op = op_ref[dz, 0], op_ref[dz, 1]
    down = down_ref[...]
    lane16 = lax.broadcasted_iota(i32, (16, 128), 1)
    keep = inside_mask((16, 128), 0, 8 * dy - 1, 64)
    for g in range(4):
        planes = range(5 * g, min(5 * g + 5, 19))
        stacked = []
        for p, a in enumerate(planes):
            face = pltpu.roll(got_ref[24 + 24 * p : 48 + 24 * p], (32 - 32 * g) % 128, 1)
            second = jnp.where((lane >= 32) & (lane < 64), face, rho_ref[a, :, 128:256])
            stacked.append(jnp.concatenate([rho_ref[a, :, 0:128], second], 1))
        high, low = split2(jnp.concatenate(stacked, 0))
        result = dot(high, high_op) + dot(low, high_op) + dot(high, low_op)
        for p, a in enumerate(planes):
            plane = result[24 * p : 24 * p + 24]
            full_ref[a] = plane
            h, m, l = split3(plane[:, 128:256])
            restricted = dot(down, jnp.concatenate([h, m, l], 0).astype(bf16)) * keep
            restr_ref[a] = restricted
            for out, way in ((a_ref, even), (b_ref, ~even)):
                window = jnp.where(way, plane[8:24], plane[0:16])
                out[152 + 16 * a : 168 + 16 * a] = window[:, 0:128]
                out[456 + 16 * a : 472 + 16 * a] = jnp.where(lane16 < 8, window[:, 128:256], restricted)
            m_ref[8 * a : 8 * a + 8] = jnp.where(far, restricted[8:16], restricted[0:8])
            n_ref[8 * a : 8 * a + 8] = jnp.where(far, restricted[0:8], restricted[8:16])
    counts = jnp.where(row8 == 0, own_msg_ref[0:8], jnp.where(row8 == 1, pltpu.roll(got_ref[0:8], 1, 0), 0.0))
    for out, j in ((a_ref, 1 - (dy & 1)), (b_ref, dy & 1)):
        out[0:8] = counts
        for level in range(18):
            out[8 + 8 * level : 16 + 8 * level] = jnp.where(
                row8 < 4, near1_ref[0, j, level], pltpu.roll(near1_ref[1, j, level], 4, 0)
            )


def along_y_kernel(near1_ref, full_ref, restr_ref, own_msg_ref, got_a_ref, got_b_ref, got_m_ref, got_n_ref,
                   fine_ref, coarse_ref, after_ref, near2_ref, fine2_ref, coarse2_ref,
                   a_ref, b_ref, m_ref, n_ref):
    dx, dy = lax.axis_index("gx"), lax.axis_index("gy")
    even, odd_x = (dy & 1) == 0, dx & 1
    far_x = (dx & 2) == 0
    row8 = lax.broadcasted_iota(i32, (8, 128), 0)
    keep = inside_mask((16, 128), 0, 8 * dy - 1, 64)
    lane16 = lax.broadcasted_iota(i32, (16, 128), 1)
    lane24 = lax.broadcasted_iota(i32, (24, 128), 1)
    fine_op, coarse_op = fine_ref[dy & 3], coarse_ref[dy & 3]

    def plane(a, _):
        at = pl.multiple_of(16 * a, 16)
        at8 = pl.multiple_of(8 * a, 8)
        a_low, a_high = got_a_ref[pl.ds(152 + at, 16)], got_a_ref[pl.ds(456 + at, 16)]
        b_low, b_high = got_b_ref[pl.ds(152 + at, 16)], got_b_ref[pl.ds(456 + at, 16)]
        stack = jnp.concatenate(
            [full_ref[a], jnp.concatenate([a_low, a_high], 1), jnp.concatenate([b_low, b_high], 1)], 0
        )
        high, low = split3(stack)[:2]
        fine2_ref[a] = dot(fine_op, jnp.concatenate([high, high, low], 0).astype(bf16))
        stack = jnp.concatenate(
            [restr_ref[a], a_high, b_high, got_m_ref[pl.ds(at8, 8)], got_n_ref[pl.ds(at8, 8)]], 0
        )
        high, low = split3(stack)[:2]
        coarse2_ref[a] = dot(coarse_op, jnp.concatenate([high, high, low], 0).astype(bf16)) * keep
        return 0

    lax.fori_loop(0, 19, plane, 0)
    restricted = []
    for e in range(11):
        value = None
        for a, weight in ((2 * e - 2, 0.5), (2 * e - 1, 1.0), (2 * e, 0.5)):
            if 0 <= a < 19:
                term = coarse2_ref[a] * weight
                value = term if value is None else value + term
        point = 8 * dx - 1 + e
        restricted.append(value * ((point >= 0) & (point < 64)).astype(f32))
    blank = jnp.zeros((8, 128), f32)
    for out, first in ((a_ref, 8 * (1 - odd_x)), (b_ref, 8 * odd_x)):
        for n in range(11):
            plane_value = fine2_ref[first + n]
            out[296 + 24 * n : 320 + 24 * n] = plane_value[:, 0:128]
            out[560 + 24 * n : 584 + 24 * n] = jnp.where(
                lane24 < 8, plane_value[:, 128:256], jnp.concatenate([restricted[n], blank], 0)
            )
    for n in range(3):
        m_ref[16 * n : 16 * n + 16] = jnp.where(far_x, restricted[8 + n], restricted[n])
        n_ref[16 * n : 16 * n + 16] = jnp.where(far_x, restricted[n], restricted[8 + n])
    shift_a = jnp.where(row8 == 1, jnp.where(even, 16.0, -16.0), 0.0)
    at_a = 3 * (1 - (dy & 1))
    for level in range(18):
        for y, source, shift in ((at_a, got_a_ref, shift_a), (3 - at_a, got_b_ref, -shift_a)):
            got = source[8 + 8 * level : 16 + 8 * level]
            near2_ref[0, y, level] = jnp.where(row8 < 4, got, 0.0) + shift
            near2_ref[1, y, level] = jnp.where(row8 < 4, pltpu.roll(got, 4, 0), 0.0) + shift
        for x in range(2):
            for y in range(2):
                near2_ref[x, y + 1, level] = near1_ref[x, y, level]
    below, above = jnp.where(even, got_b_ref[0:8], got_a_ref[0:8]), jnp.where(even, got_a_ref[0:8], got_b_ref[0:8])
    counts = jnp.where(row8 < 2, own_msg_ref[0:8], 0.0)
    counts = jnp.where((row8 >= 2) & (row8 < 4), pltpu.roll(below, 2, 0), counts)
    counts = jnp.where((row8 >= 4) & (row8 < 6), pltpu.roll(above, 4, 0), counts)
    for out, x in ((a_ref, 1 - odd_x), (b_ref, odd_x)):
        out[0:8] = counts
        for level in range(18):
            for pair in range(2):
                at = 8 + 8 * (2 * level + pair)
                out[at : at + 8] = jnp.where(
                    row8 < 4, near2_ref[x, 2 * pair, level], pltpu.roll(near2_ref[x, 2 * pair + 1, level], 4, 0)
                )


def along_x_kernel(fine2_ref, own_msg_ref, got_a_ref, got_b_ref, got_m_ref, got_n_ref,
                   up_y_ref, up_z_ref, after_ref, phi_ref, source, third, coarse):
    dx, dy, dz = lax.axis_index("gx"), lax.axis_index("gy"), lax.axis_index("ga")
    even, far = 1 - (dx & 1), 1 - ((dx >> 1) & 1)
    for p in range(8):
        source[p] = jnp.zeros((24, 256), f32)
        source[27 + p] = jnp.zeros((24, 256), f32)
        coarse[p] = jnp.zeros((16, 128), f32)
        coarse[19 + p] = jnp.zeros((16, 128), f32)
    for p in range(19):
        source[8 + p] = fine2_ref[p]
    for got, first in ((got_a_ref, 24 * even), (got_b_ref, 24 * (1 - even))):
        for n in range(11):
            source[first + n, :, 0:128] += got[296 + 24 * n : 320 + 24 * n]
            source[first + n, :, 128:256] += got[560 + 24 * n : 584 + 24 * n]
    for n in range(11):
        coarse[8 + n] = own_msg_ref[560 + 24 * n : 576 + 24 * n]
    for got, first in ((got_a_ref, 16 * even), (got_b_ref, 16 * (1 - even))):
        for n in range(11):
            coarse[first + n] += got[560 + 24 * n : 576 + 24 * n]
    for got, first in ((got_m_ref, 24 * far), (got_n_ref, 24 * (1 - far))):
        for n in range(3):
            coarse[first + n] += got[16 * n : 16 * n + 16]
    fine_weights = [float(w) for w in fine_kernel(np.arange(9.0))]
    coarse_weights = [float(w) for w in coarse_kernel(np.arange(9.0))]

    def fine_plane(a, _):
        value = source[a + 8] * (4.0 * fine_weights[0])
        for d in range(1, 9):
            value = value + (source[a + 8 - d] + source[a + 8 + d]) * (4.0 * fine_weights[d])
        third[a] = value
        return 0

    lax.fori_loop(0, 19, fine_plane, 0)

    lifted = []
    up_y, up_z = up_y_ref[...], up_z_ref[...]
    for e in range(11):
        value = coarse[e + 8] * (2.0 * coarse_weights[0])
        for d in range(1, 9):
            value = value + (coarse[e + 8 - d] + coarse[e + 8 + d]) * (2.0 * coarse_weights[d])
        point = 8 * dx - 1 + e
        value = value * ((point >= 0) & (point < 64)).astype(f32)
        h, m, l = split3(value)
        tall = dot(up_y, jnp.concatenate([h, m, l], 0).astype(bf16))
        h, m, l = split3(tall)
        stacked = jnp.concatenate([h, m, l], 0).astype(bf16)
        wide = dot(stacked, up_z)
        lifted.append(wide[0:24] + wide[24:48] + wide[48:72])
    mask = inside_mask((24, 256), 0, 16 * dy - 1, 128) * inside_mask((24, 256), 1, 128 * dz - 1, 256)
    lane = lax.broadcasted_iota(i32, (24, 256), 1)
    mask = jnp.where(lane < 131, mask, 0.0)
    for a in range(19):
        if a % 2:
            value = lifted[(a + 1) // 2]
        else:
            value = 0.5 * (lifted[a // 2] + lifted[a // 2 + 1])
        point = 16 * dx - 1 + a
        keep = mask * ((point >= 0) & (point < 128)).astype(f32)
        phi_ref[a] = jnp.where(keep > 0.0, third[a] + value, 0.0)


def gather_kernel(off_ref, charge_ref, counts_ref, phi_ref, out_ref):
    lane = lax.broadcasted_iota(i32, (1, 128), 1)
    lane176 = lax.broadcasted_iota(i32, (176, 128), 1)

    def column(ij, _):
        i, j = ij >> 1, ij & 1
        first = pl.multiple_of(8 * j, 8)
        low = jnp.concatenate([phi_ref[8 * i + a, pl.ds(first, 16), 0:128] for a in range(11)], 0)
        high = jnp.concatenate([phi_ref[8 * i + a, pl.ds(first, 16), 128:256] for a in range(11)], 0)
        for m in range(8):
            window = pltpu.roll(low, (128 - 16 * m) % 128, 1) if m else low
            if m == 7:
                window = jnp.where(lane176 < 16, window, pltpu.roll(high, 16, 1))
            window = jnp.where(lane176 < 32, window, 0.0)
            part_h = window.astype(bf16).astype(f32)
            part_m = window - part_h
            left = (part_h + pltpu.roll(part_m, 32, 1) + pltpu.roll(part_h, 64, 1)).astype(bf16)
            stacks, slopes, sides = [], [], []
            for half in range(2):
                k = 2 * m + half
                ox = off_ref[0, i, j, k : k + 1]
                oy = off_ref[1, i, j, k : k + 1]
                oz = off_ref[2, i, j, k : k + 1]
                count = counts_ref[i, j, k]
                weighted = jnp.where(lane < count, charge_ref[i, j, k : k + 1], 0.0)
                shifted = weights_at(oz, 32, 8 * half)
                for bag, value in ((stacks, spline(shifted)), (slopes, spline_slope(shifted))):
                    high_part, low_part = split2(value)
                    bag.append(jnp.concatenate([high_part, high_part, low_part, jnp.zeros((32, 128), bf16)], 0))
                sides.append((ox, oy, weighted))
            right = jnp.concatenate(stacks + slopes, 1)
            product = dot(left, right)
            for half in range(2):
                k = 2 * m + half
                ox, oy, weighted = sides[half]
                level = product[:, 128 * half : 128 * half + 128]
                rising = product[:, 256 + 128 * half : 384 + 128 * half]
                sx = weights_at(ox, 16, 0)
                sy = weights_at(oy, 16, 0)
                wx, gx = spline(sx), spline_slope(sx)
                wy, gy = spline(sy), spline_slope(sy)
                along = across = up = None
                for a in range(11):
                    piece = level[16 * a : 16 * a + 16]
                    rise = rising[16 * a : 16 * a + 16]
                    terms = (gx[a : a + 1] * piece, wx[a : a + 1] * piece, wx[a : a + 1] * rise)
                    if a == 0:
                        along, across, up = terms
                    else:
                        along, across, up = along + terms[0], across + terms[1], up + terms[2]
                force_x = jnp.sum(along * wy, axis=0, keepdims=True)
                force_y = jnp.sum(across * gy, axis=0, keepdims=True)
                force_z = jnp.sum(up * wy, axis=0, keepdims=True)
                out_ref[0, i, j, k : k + 1] = -weighted * force_x
                out_ref[1, i, j, k : k + 1] = -weighted * force_y
                out_ref[2, i, j, k : k + 1] = -weighted * force_z
        return 0

    lax.fori_loop(0, 4, column, 0)


def pair_scratch(form, cells, tiles):
    rows, slots, share = form
    sets = cells // share
    return (
        [
            pltpu.VMEM((tiles, 8, 128), f32),
            pltpu.VMEM((tiles, 48, 128), bf16),
            pltpu.VMEM((tiles, 16, 128), bf16),
            pltpu.VMEM((sets + 1, share * 128, 128), f32),
            pltpu.VMEM(((sets + 1) * (share * 128 // rows), 16, 128), f32),
        ]
        + [
            pltpu.VMEM((rows, TILES * 128), f32),
            pltpu.VMEM((rows, TILES * 128), bf16),
            pltpu.VMEM((rows, TILES * 128), bf16),
        ]
        * slots
        + [pltpu.SMEM((128,), i32), pltpu.SMEM((cells,), i32)]
        + [pltpu.SMEM((sets + 1,), i32)] * 3
    )


def middle_of(center):
    row = lax.broadcasted_iota(i32, (8, 128), 0)
    return jnp.where(row < 2, 16.0, jnp.where(row == 2, center, 0.0))


def pack_list(packed, start, base, tile, levels, center):
    lane = lax.broadcasted_iota(i32, (8, 128), 1)
    middle = middle_of(center)
    end, current = tile * 128, jnp.zeros((8, 128), f32)
    for level, beads in enumerate(levels):
        start[base + level] = end
        for value, count in beads:
            within, tile = end & 127, end >> 7
            turned = pltpu.roll(value - middle, within, 1)
            keep = lane < within
            current = jnp.where(keep, current, turned)
            packed[tile] = current
            end = end + count
            current = jnp.where((end >> 7) > tile, jnp.where(keep, turned, 0.0), current)
    start[base + len(levels)] = end
    packed[end >> 7] = jnp.where(lane < (end & 127), current, 0.0)
    for e in range(1, TILES):
        packed[(end >> 7) + e] = jnp.zeros((8, 128), f32)
    return (end >> 7) + TILES


def pair_sums(scratch, form, cells, used, own_pos, own_count, own_start, own_center, emit):
    packed, features, sources, own_features, sums = scratch[:5]
    start, row_at, first_tile, groups_of, blocks_of = scratch[-5:]
    height, flight, share = form
    sets = cells // share
    slots = [scratch[5 + 3 * e : 8 + 3 * e] for e in range(flight)]
    blocks = share * 128 // height
    lane = lax.broadcasted_iota(i32, (16, 128), 1)
    row = lax.broadcasted_iota(i32, (8, 128), 0)
    for e in range(8):
        packed[used + e] = jnp.zeros((8, 128), f32)

    def near_step(step, _):
        for e in range(8):
            tile = 8 * step + e
            value = packed[tile]
            norm = value[0:1] * value[0:1] + value[1:2] * value[1:2] + value[2:3] * value[2:3]
            vector = jnp.where(row < 3, value, jnp.where(row == 3, norm, jnp.where(row == 4, 1.0, 0.0)))
            h, m, l = split3(vector)
            features[tile] = jnp.concatenate([h, h, m, m, h, l], 0).astype(bf16)
            charge = value[3:4]
            vector = jnp.where(row < 3, value * charge, jnp.where(row == 3, charge, 0.0))
            h, m, l = split3(vector)
            sources[tile] = jnp.concatenate(
                [jnp.where(row < 4, h, pltpu.roll(m, 4, 0)), jnp.where(row < 4, l, 0.0)], 0
            ).astype(bf16)
        return 0

    lax.fori_loop(0, (used + 7) // 8, near_step, 0)

    def own_one(n, which, at):
        value = own_pos(n) - middle_of(own_center(n))
        norm = value[0:1] * value[0:1] + value[1:2] * value[1:2] + value[2:3] * value[2:3]
        vector = jnp.where(
            row < 3,
            value * (2.0 / 64),
            jnp.where(row == 3, -1.0 / 64, jnp.where(row == 4, 1.0 - norm * (1.0 / 64), 0.0)),
        )
        h, m, l = split3(vector)
        stacked = jnp.concatenate([h, m, h, m, l, h, jnp.zeros((80, 128), f32)], 0)
        own_features[which, pl.ds(pl.multiple_of(at, 8), 128), :] = jnp.transpose(stacked)
        row_at[n] = at
        return at + ((own_count(n) + 7) >> 3) * 8

    def own_step(step, total):
        for e in range(8 // share):
            which = step * (8 // share) + e
            at = i32(0)
            for c in range(share):
                at = own_one(c * sets + which, which, at)
            for b in range(blocks):
                sums[which * blocks + b] = jnp.zeros((16, 128), f32)
            level = own_start(which)
            begin, stop = start[level], start[level + 3]
            tile = begin >> 7
            groups = jnp.maximum((((stop + 127) >> 7) - tile + TILES - 1) // TILES, 1)
            rows = (at + height - 1) // height
            first_tile[which], groups_of[which], blocks_of[which] = tile, groups, rows
            total = total + groups * rows
        return total

    total = lax.fori_loop(0, cells // 8, own_step, i32(0))
    own_features[sets] = jnp.zeros((share * 128, 128), f32)
    for e in range(blocks):
        sums[sets * blocks + e] = jnp.zeros((16, 128), f32)
    first_tile[sets], groups_of[sets], blocks_of[sets] = i32(0), i32(1), i32(1)
    for distance, high, low in slots:
        distance[...] = jnp.zeros((height, TILES * 128), f32)
        high[...] = jnp.zeros((height, TILES * 128), bf16)
        low[...] = jnp.zeros((height, TILES * 128), bf16)

    def item(_, state):
        cell, block, group = state[:3]
        older, oldest = state[3 : 3 + 2 * flight], state[3 + 2 * flight :]
        added, shares, fresh, tags = [], [], [], []
        for e in range(flight):
            distance, high, low = slots[e]
            tile = oldest[2 * e + 1]
            source = jnp.concatenate([sources[tile + s] for s in range(TILES)], 1)
            added.append(
                lax.dot_general(
                    jnp.concatenate([source, source], 1),
                    jnp.concatenate([high[...], low[...]], 1),
                    LAST,
                    preferred_element_type=f32,
                )
            )
            reach = distance[...]
            kept = jnp.maximum(reach, 0.0)
            strength = (kept * kept * kept) / (CAP - reach)
            shares.append(split2(strength))
            groups, rows = groups_of[cell], blocks_of[cell]
            tile = first_tile[cell] + group * TILES
            at = pl.multiple_of(block * height, height)
            left = own_features[cell, pl.ds(at, height), 0:48].astype(bf16)
            right = jnp.concatenate([features[tile + s] for s in range(TILES)], 1)
            fresh.append(dot(left, right))
            tags += [cell * blocks + block, tile]
            group = group + 1
            wrap = (group >= groups).astype(i32)
            group = group * (1 - wrap)
            block = block + wrap
            wrap = (block >= rows).astype(i32)
            block = block * (1 - wrap)
            cell = jnp.minimum(cell + wrap, sets)
        for e in range(flight):
            distance, high, low = slots[e]
            where = oldest[2 * e]
            sums[where, :, 0:height] = sums[where, :, 0:height] + added[e]
            high[...], low[...] = shares[e]
            distance[...] = fresh[e]
        return (cell, block, group) + tuple(tags) + tuple(older)

    spare = (i32(sets * blocks), i32(0))
    lax.fori_loop(0, (total + flight - 1) // flight + 2, item, (i32(0),) * 3 + spare * (2 * flight))

    def finish_one(n):
        if share == 1:
            parts = [sums[n * blocks + e, :, 0:height] for e in range(blocks)]
            whole = jnp.concatenate(parts, 1) if blocks > 1 else parts[0]
        else:
            at = row_at[n]
            block, within = (n % sets) * blocks + (at >> 7), at & 127
            back = (128 - within) & 127
            whole = jnp.where(
                lane < 128 - within, pltpu.roll(sums[block], back, 1), pltpu.roll(sums[block + 1], back, 1)
            )
        whole = whole[0:4] + whole[4:8] + whole[8:12]
        raw = own_pos(n)
        value = raw - middle_of(own_center(n))
        emit(n, (value[0:3] * whole[3:4] - whole[0:3]) * (raw[3:4] * (1.0 / 64)), raw)

    def finish(step, _):
        for e in range(4):
            finish_one(4 * step + e)
        return 0

    lax.fori_loop(0, cells // 4, finish, 0)


def inner_pairs_kernel(first, depth, near_ref, counts_ref, partners_ref, after_ref, out_ref, table, *scratch):
    lane = lax.broadcasted_iota(i32, (1, 128), 1)
    for column in range(4):
        table[18 * column] = i32(0)
        table[18 * column + 17] = i32(0)

    def copy_count(k, _):
        for column in range(4):
            table[18 * column + 1 + k] = counts_ref[column >> 1, column & 1, k]
        return 0

    lax.fori_loop(0, 16, copy_count, 0)

    center = 8.0 * first + 4.0 * depth + 8.0
    levels = [
        [(near_ref[18 * c + first + n], table[18 * c + first + n]) for c in range(4)] for n in range(depth + 2)
    ]
    used = pack_list(scratch[0], scratch[-5], 0, i32(0), levels, center)

    def split(n):
        column = lax.div(n, i32(depth))
        return column, n - column * depth

    def cell_at(n):
        column, level = split(n)
        return column * 18 + level + (first + 1)

    def emit(n, value, raw):
        column, level = split(n)
        x, y, k = column >> 1, column & 1, first + level
        count = table[cell_at(n)]
        partner = partners_ref[x, y, pl.ds(k, 1), :]
        other = jnp.take_along_axis(raw, jnp.broadcast_to(partner, (8, 128)), axis=1)
        both = (lane < count) & (partner < count)
        out_ref[x, y, level, 0:3] = value + jnp.where(both, -0.1 * (raw[0:3] - other[0:3]), 0.0)

    pair_sums(
        scratch,
        INNER,
        4 * depth,
        used,
        lambda n: near_ref[cell_at(n)],
        lambda n: table[cell_at(n)],
        lambda n: n,
        lambda n: center,
        emit,
    )


def outer_pairs_kernel(near2_ref, own_msg_ref, got_a_ref, got_b_ref, first_ref, second_ref, out_ref,
                       near, counts, table, *scratch):
    dz, odd = lax.axis_index("ga"), lax.axis_index("gx") & 1
    row8 = lax.broadcasted_iota(i32, (8, 128), 0)
    for n, source in enumerate((got_a_ref, own_msg_ref, got_b_ref)):
        pltpu.sync_copy(source.at[0:8], counts.at[n])
    shift_a = jnp.where(row8 == 0, jnp.where(odd == 0, 16.0, -16.0), 0.0)
    at_a = 3 * (1 - odd)

    def level_step(level, _):
        for x in range(2):
            for y in range(4):
                near[(4 * x + 4 + y) * 18 + level] = near2_ref[x, y, level]
        for x, source, shift in ((at_a, got_a_ref, shift_a), (3 - at_a, got_b_ref, -shift_a)):
            for pair in range(2):
                at = pl.multiple_of(8 + 8 * (2 * level + pair), 8)
                got = source[pl.ds(at, 8)]
                near[(4 * x + 2 * pair) * 18 + level] = jnp.where(row8 < 4, got, 0.0) + shift
                near[(4 * x + 2 * pair + 1) * 18 + level] = jnp.where(row8 < 4, pltpu.roll(got, 4, 0), 0.0) + shift
        return 0

    lax.fori_loop(0, 18, level_step, 0)
    for x in range(4):
        which, along = ((2 * (1 - odd), 1), (1, 0), (1, 1), (2 * odd, 0))[x]
        for y in range(4):
            pair_row, across = ((2, 1), (0, 0), (0, 1), (4, 0))[y]
            base = 32 * along + 16 * across
            at = (x * 4 + y) * 18
            table[at] = jnp.where(dz == 1, counts[which, pair_row + 1, base + 15], 0.0).astype(i32)
            table[at + 17] = jnp.where(dz == 0, counts[which, pair_row + 1, base], 0.0).astype(i32)

            def copy_count(k, _, which=which, pair_row=pair_row, base=base, at=at):
                table[at + 1 + k] = counts[which, pair_row, base + k].astype(i32)
                return 0

            lax.fori_loop(0, 16, copy_count, 0)

    def split(number):
        return number >> 2, (number >> 1) & 1, number & 1

    def one_list(number, tile):
        i, j, part = split(number)
        outside = [(12 * i + j + c) * 18 + 8 * part for c in range(3)]
        outside += [(4 * x + 3 * j) * 18 + 8 * part for x in (1, 2)]
        within = [(4 * x + y) * 18 + 8 * part for x in (1, 2) for y in (1, 2)]
        levels = []
        for level in range(10):
            beads = [(near[base + level], table[base + level]) for base in outside]
            if level in (0, 9):
                use = part if level else 1 - part
                beads += [(near[base + level], table[base + level] * use) for base in within]
            levels.append(beads)
        return pack_list(scratch[0], scratch[-5], 16 * number, tile, levels, 64.0 * part.astype(f32) + 40.0)

    used = lax.fori_loop(0, 8, one_list, i32(0))

    def own_at(n):
        i, j, part = split(n >> 3)
        return (4 * (i + 1) + j + 1) * 18 + 8 * part + 1 + (n & 7)

    def emit(n, value, raw):
        i, j, part = split(n >> 3)
        k = 8 * part + (n & 7)
        early = first_ref[i, j, jnp.minimum(k, EARLY - 1), 0:3]
        value = value + jnp.where(k < EARLY, early, second_ref[i, j, jnp.maximum(k - EARLY, 0), 0:3])
        for d in range(3):
            out_ref[d, i, j, pl.ds(k, 1), :] = value[d : d + 1]

    pair_sums(
        scratch,
        OUTER,
        64,
        used,
        lambda n: near[own_at(n)],
        lambda n: table[own_at(n)],
        lambda n: 16 * (n >> 3) + (n & 7),
        lambda n: 64.0 * ((n >> 3) & 1).astype(f32) + 40.0,
        emit,
    )


def call(kernel, shapes, inputs, specs=None, scratch=(), flops=10**6, out_specs=None):
    single = not isinstance(shapes, (list, tuple)) or isinstance(shapes[0], int)
    shapes = [shapes] if single else shapes
    result = pl.pallas_call(
        kernel,
        out_shape=[jax.ShapeDtypeStruct(s, f32) for s in shapes],
        in_specs=specs or [VMEM] * len(inputs),
        out_specs=[VMEM] * len(shapes),
        scratch_shapes=list(scratch),
        cost_estimate=pl.CostEstimate(flops=flops, transcendentals=0, bytes_accessed=10**6),
        compiler_params=pltpu.CompilerParams(vmem_limit_bytes=40 << 20),
    )(*inputs)
    return result[0] if single else result


PARTNERS = (
    ((0, 1), (2, 3), (4, 5), (6, 7)),
    ((1, 2), (3, 4), (5, 6)),
    ((0, 2), (1, 3), (4, 6), (5, 7)),
    ((2, 4), (3, 5)),
)


def exchange(messages, axis):
    return [
        lax.ppermute(value, axis, [way for p, q in pairs for way in ((p, q), (q, p))])
        for value, pairs in zip(messages, PARTNERS)
    ]


def per_device(offsets, charge, counts, partners):
    z_op = jnp.asarray(np.stack([np.stack(halves(z_operator(part))) for part in range(2)]))
    fine_op, coarse_op, y_down, y_up = [jnp.asarray(m) for m in y_operators()]
    z_up = jnp.asarray(z_prolong())
    near, rho, z_msg = call(
        spread_kernel,
        [(2, 2, 18, 8, 128), (19, 24, 256), (144, 128)],
        (offsets, charge, counts),
        [VMEM, VMEM, SMEM],
    )
    z_got = lax.ppermute(z_msg, "ga", [(0, 1), (1, 0)])
    near1, full, restr, *y_msgs = call(
        along_z_kernel,
        [(2, 2, 18, 8, 128), (19, 24, 256), (19, 16, 128), (760, 128), (760, 128), (152, 128), (152, 128)],
        (near, rho, z_msg, z_got, z_op, y_down),
    )
    y_got = exchange(y_msgs, "gy")
    inner = lambda level, depth, near_in, after: call(
        lambda *refs: inner_pairs_kernel(level, depth, *refs),
        (2, 2, depth, 8, 128),
        (near_in.reshape(72, 8, 128), counts, partners, after),
        [VMEM, SMEM, VMEM, ANY],
        [pltpu.SMEM((72,), i32)] + pair_scratch(INNER, 4 * depth, 4 * depth + TILES + 24),
        flops=10**9,
    )
    first = inner(0, EARLY, near, full)
    near2, fine2, _, *x_msgs = call(
        along_y_kernel,
        [(2, 4, 18, 8, 128), (19, 24, 256), (19, 16, 128), (824, 128), (824, 128), (48, 128), (48, 128)],
        (near1, full, restr, y_msgs[0], *y_got, fine_op, coarse_op, first),
        [VMEM] * 10 + [ANY],
    )
    x_got = exchange(x_msgs, "gx")
    second = inner(EARLY, 16 - EARLY, near, fine2)
    phi = call(
        along_x_kernel,
        (19, 24, 256),
        (fine2, x_msgs[0], *x_got, y_up, z_up, second),
        [VMEM] * 8 + [ANY],
        [pltpu.VMEM((35, 24, 256), f32), pltpu.VMEM((19, 24, 256), f32), pltpu.VMEM((27, 16, 128), f32)],
    )
    short_force = call(
        outer_pairs_kernel,
        (3, 2, 2, 16, 128),
        (near2, x_msgs[0], x_got[0], x_got[1], first, second),
        None,
        [
            pltpu.VMEM((288, 8, 128), f32),
            pltpu.SMEM((3, 8, 128), f32),
            pltpu.SMEM((288,), i32),
        ]
        + pair_scratch(OUTER, 64, 8 * (54 + TILES) + 24),
        flops=10**9,
    )
    long_force = call(
        gather_kernel, (3, 2, 2, 16, 128), (offsets, charge, counts, phi), [VMEM, VMEM, SMEM, VMEM]
    )
    return short_force, long_force


def solution(mesh):
    return jax.shard_map(
        per_device,
        mesh=mesh,
        in_specs=(
            P(None, "gx", "gy", "ga", None),
            P("gx", "gy", "ga", None),
            P("gx", "gy", "ga"),
            P("gx", "gy", "ga", None),
        ),
        out_specs=(P(None, "gx", "gy", "ga", None), P(None, "gx", "gy", "ga", None)),
        check_vma=False,
    )
```
